32 devices in a mesh: rep: 2 (over x), shard: 16 (over z, y, core).
Axes of the slice: x: 2, y: 2, z: 4, core: 2. Of those that a mesh axis runs over, the one named last changes fastest.
Arguments:
- tokens: bfloat16 [8192, 2048], P(('rep', 'shard')), may hold values from -6 to 6
- seg_ids: int32 [8192], P(('rep', 'shard')), may hold values from 0 to 7, never falling along the last dimension, each value on 1 to 2000 neighbouring positions
- mix_gain: bfloat16 [2048], P('shard'), may hold values from 0.099609375 to 1.8984375
- mix_in: bfloat16 [2048, 5120], P('shard'), may hold values from -0.125 to 0.125
- conv_par: bfloat16 [5, 2560], P(None, 'shard'), may hold values from -3 to 3
- gate_w: bfloat16 [2560, 320], P('shard'), may hold values from -0.5 to 0.5
- gate_bias: bfloat16 [2, 2560], P(None, 'shard'), may hold values from -3 to 3
- decay: bfloat16 [2560], P('shard'), may hold values from 2.1875 to 6.875
- out_proj: bfloat16 [2560, 2048], P('shard'), may hold values from -0.5 to 0.5
- mlp_gain: bfloat16 [2048], P('shard'), may hold values from 0.099609375 to 1.8984375
- mlp_in: bfloat16 [2048, 12288], P('shard'), may hold values from -0.125 to 0.125
- mlp_out: bfloat16 [6144, 2048], P('shard'), may hold values from -0.15625 to 0.15625
- cotangent: bfloat16 [8192, 2048], P(('rep', 'shard')), may hold values from -6 to 6
Outputs:
- output: bfloat16 [8192, 2048], P(('rep', 'shard'))
- grad_tokens: float32 [8192, 2048], P(('rep', 'shard'))
- grad_mix_gain: float32 [2048], P('shard')
- grad_mix_in: float32 [2048, 5120], P('shard')
- grad_conv_par: float32 [5, 2560], P(None, 'shard')
- grad_gate_w: float32 [2560, 320], P('shard')
- grad_gate_bias: float32 [2, 2560], P(None, 'shard')
- grad_decay: float32 [2560], P('shard')
- grad_out_proj: float32 [2560, 2048], P('shard')
- grad_mlp_gain: float32 [2048], P('shard')
- grad_mlp_in: float32 [2048, 12288], P('shard')
- grad_mlp_out: float32 [6144, 2048], P('shard')
The draws below stay inside these ranges and needn't reach their ends.
Inputs may be any that keep to these rules, and one draw needn't show every extreme that they name: `seg_ids`: along the token order the ids never fall; each document has 1 to 2000 tokens and one has exactly 2000.
All inputs are finite; a program needn't handle non-finite values.
Results may differ from the reference program's by a relative error of at most 0.013.
Values may be sent and summed in bfloat16 or wider, within the bound.
A program may use at most 512 MiB of HBM per device.

```python
import math
import jax
import jax.numpy as jnp
import numpy as np
from jax import lax

D = 2048
R = 2560
NBLK = 16
FF = 6144
SEQ_LEN = 4096
DOC_MAX = 2000
BW = 160
TOKENS = 8192
DOCS = 8


def steps_of(stream_key, dims, pieces, least, high):
    loudness, own = 1.0, jax.random.fold_in(stream_key, 6)
    for position, parts in pieces:
        steps = jnp.exp(jax.random.uniform(jax.random.fold_in(own, position), (parts,), jnp.float32, least / len(pieces), high / len(pieces)))
        loudness = loudness * jnp.repeat(steps, dims[position] // parts).reshape([-1 if axis == position else 1 for axis in range(len(dims))])
    return loudness


def profile(number_of, total, bound, slope):
    portions = [(1 << 20) // math.isqrt(rank ** slope) + 1 for rank in range(2, number_of + 1)]
    spare, holding = total - bound - (number_of - 1), [1] * (number_of - 1)
    while spare > 0:
        free = [i for i in range(number_of - 1) if holding[i] < bound]
        pool, budget = sum([portions[i] for i in free]), spare
        for i in free:
            extra = min(bound - holding[i], max(1, budget * portions[i] // pool), spare)
            holding[i] = holding[i] + extra
            spare = spare - extra
    return np.array([bound] + holding)


def ragged_sizes(key, amount, total, bound, slope):
    if amount == 2:
        one = jax.random.randint(key, (), max(1, total - bound), min(bound, total - 1) + 1)
        return jnp.stack([one, total - one])
    tallies = jnp.asarray(profile(amount, total, bound, slope), jnp.int32)
    couples = (amount - 1) // 2
    source_of, taker = tallies[1:1 + 2 * couples:2], tallies[2:2 + 2 * couples:2]
    room = jnp.minimum(source_of - 1, bound - taker)
    moved = jax.random.randint(jax.random.fold_in(key, 1), (couples,), 0, 1 << 20) % (room + 1)
    tallies = tallies.at[1:1 + 2 * couples:2].set(source_of - moved).at[2:2 + 2 * couples:2].set(taker + moved)
    return tallies[jax.random.permutation(jax.random.fold_in(key, 2), amount)]


def normal_values(own_key, shape, scale, bound, pieces=(), dtype=jnp.bfloat16):
    drawn = jax.random.normal(own_key, shape, jnp.float32) * scale
    if len(pieces) > 0:
        drawn = steps_of(own_key, shape, pieces, -0.22, 0.18) * drawn
    return jnp.clip(drawn, min=-bound, max=bound).astype(dtype)


def setup_inputs(seed: int = 0) -> dict:
    keys = jax.random.split(jax.random.key(seed), 14)
    return {
        "tokens": normal_values(keys[0], (TOKENS, D), 1.0, 6.0, ((0, 32),)),
        "seg_ids": jnp.searchsorted(jnp.cumsum(ragged_sizes(keys[1], DOCS, TOKENS, DOC_MAX, 0)), jnp.arange(TOKENS), side="right").astype(jnp.int32),
        "mix_gain": jnp.clip(1.0 + 0.18 * jax.random.normal(keys[2], (D,), jnp.float32), 0.099609375, 1.8984375).astype(jnp.bfloat16),
        "mix_in": normal_values(keys[3], (D, 2 * R), D ** -0.5, 0.125, ((0, 16),)),
        "conv_par": normal_values(keys[4], (5, R), 0.5, 3.0, ((1, 16),)),
        "gate_w": normal_values(keys[5], (R, 2 * BW), BW ** -0.5, 0.5, ((0, 16),)),
        "gate_bias": normal_values(keys[6], (2, R), 1.0, 3.0, ((1, 16),)),
        "decay": jnp.clip(2.1875 + 4.6875 * jax.random.uniform(keys[7], (R,), jnp.float32) ** steps_of(keys[7], (R,), ((0, 16),), -0.2, 0.2), 2.1875, 6.875).astype(jnp.bfloat16),
        "out_proj": normal_values(keys[8], (R, D), (R // 16) ** -0.5, 0.5, ((0, 16),)),
        "mlp_gain": jnp.clip(1.0 + 0.18 * jax.random.normal(keys[9], (D,), jnp.float32), 0.099609375, 1.8984375).astype(jnp.bfloat16),
        "mlp_in": normal_values(keys[10], (D, 2 * FF), D ** -0.5, 0.125, ((0, 16),)),
        "mlp_out": normal_values(keys[11], (FF, D), (FF // 4) ** -0.5, 0.15625, ((0, 16),)),
        "cotangent": normal_values(keys[12], (TOKENS, D), 1.0, 6.0, ((0, 32),)),
    }


@jax.custom_vjp
def low(v):
    return lax.optimization_barrier(v.astype(jnp.bfloat16)).astype(jnp.float32)

@jax.custom_vjp
def low_back(v):
    return v

def low_keep(v):
    return (low(v), None)

def low_pass(kept, grad):
    return (grad,)

def back_keep(v):
    return (v, None)

def back_low(kept, grad):
    return (low(grad),)
low.defvjp(low_keep, low_pass)
low_back.defvjp(back_keep, back_low)
EPSILON = 1e-06
DECAY_RATE = 8.0

def product(left_in, right_in):
    return jnp.dot(left_in, right_in, precision=lax.Precision.HIGHEST, preferred_element_type=jnp.float32)

def norm_rows(values, factor):
    return values * lax.rsqrt(lax.optimization_barrier(jnp.mean(values * values, axis=-1, keepdims=True)) + EPSILON) * factor

def combine_pairs(earlier, later):
    return (earlier[0] * later[0], later[0] * earlier[1] + later[1])

def gate_terms(pre_sum, decay_in, conv_out, fresh_mask, block_size):
    length = pre_sum.shape[0]
    channels = decay_in.shape[0]
    recur_gate = jax.nn.sigmoid(pre_sum[:, :, :block_size].reshape(length, channels))
    input_gate = jax.nn.sigmoid(pre_sum[:, :, block_size:].reshape(length, channels))
    log_decay = -DECAY_RATE * jax.nn.softplus(-decay_in) * recur_gate
    kept_rows = (1.0 - fresh_mask.astype(jnp.float32))[:, None]
    coefficient = jnp.exp(log_decay) * kept_rows
    scaling = jnp.where(fresh_mask[:, None], 1.0, jnp.sqrt(-jnp.expm1(2.0 * log_decay)))
    return (coefficient, scaling * input_gate * conv_out)

def layer(inputs, doc_ids, weight_set):
    mix_gain, mix_in, conv_par, gate_w, gate_bias, decay, out_proj, mlp_gain, mlp_in, mlp_out = weight_set
    length = inputs.shape[0]
    channels = decay.shape[0]
    block_size = channels // NBLK
    places = jnp.arange(length)
    fresh_mask = (places == 0) | (doc_ids != jnp.concatenate([doc_ids[:1], doc_ids[:-1]]))
    keep_mask = 1.0 - fresh_mask.astype(jnp.float32)
    normed_one = low(norm_rows(inputs, mix_gain))
    projected = low_back(product(normed_one, mix_in))
    branch = projected[:, :channels]
    conv_in = low(projected[:, channels:])
    conv_sum = conv_par[4] + conv_par[0] * conv_in
    factor = jnp.ones((length,), jnp.float32)
    for offset in range(1, 4):
        factor = factor * jnp.pad(keep_mask, (offset - 1, 0))[:length]
        shifted = jnp.pad(conv_in, ((offset, 0), (0, 0)))[:length]
        conv_sum = conv_sum + conv_par[offset] * shifted * factor[:, None]
    conv_out = low(conv_sum)
    bias_blocks = jnp.concatenate([gate_bias[0].reshape(NBLK, block_size), gate_bias[1].reshape(NBLK, block_size)], axis=-1)
    pre_sum = jnp.einsum('tbj,bjk->tbk', conv_out.reshape(length, NBLK, block_size), gate_w.reshape(NBLK, block_size, 2 * block_size), precision=lax.Precision.HIGHEST)
    pre_sum = low_back(pre_sum + bias_blocks)
    coefficient, drive = gate_terms(pre_sum, decay, conv_out, fresh_mask, block_size)
    scanned = lax.associative_scan(combine_pairs, (coefficient, drive))
    state = scanned[1]
    mixed = low(state * jax.nn.gelu(branch))
    residual = inputs + low_back(product(mixed, out_proj))
    normed_two = low(norm_rows(residual, mlp_gain))
    hidden = low_back(product(normed_two, mlp_in))
    activated = low(jax.nn.gelu(hidden[:, :FF]) * hidden[:, FF:])
    return residual + low_back(product(activated, mlp_out))

def reference(tokens, seg_ids, mix_gain, mix_in, conv_par, gate_w, gate_bias, decay, out_proj, mlp_gain, mlp_in, mlp_out, cotangent):
    weight_set = tuple((weight_arg.astype(jnp.float32) for weight_arg in (mix_gain, mix_in, conv_par, gate_w, gate_bias, decay, out_proj, mlp_gain, mlp_in, mlp_out)))
    inputs_all = tokens.astype(jnp.float32).reshape(-1, SEQ_LEN, D)
    ids_all = seg_ids.reshape(-1, SEQ_LEN)
    upstream_all = cotangent.astype(jnp.float32).reshape(-1, SEQ_LEN, D)

    def one_sequence(summed, seq_items):
        inputs, doc_ids, upstream = seq_items
        layer_out, pullback = jax.vjp(lambda values, param_set: layer(values, doc_ids, param_set), inputs, weight_set)
        input_grad, param_grads = pullback(upstream)
        summed = tuple((running + increment for running, increment in zip(summed, param_grads)))
        return (summed, (layer_out.astype(jnp.bfloat16), input_grad))
    initial = tuple((jnp.zeros_like(weight_arg) for weight_arg in weight_set))
    summed, (outputs, input_grads) = lax.scan(one_sequence, initial, (inputs_all, ids_all, upstream_all))
    return (outputs.reshape(TOKENS, D), input_grads.reshape(TOKENS, D), summed[0], summed[1], summed[2], summed[3], summed[4], summed[5], summed[6], summed[7], summed[8], summed[9])
```

```python
import functools

import jax
import jax.numpy as jnp
from jax import lax
from jax.experimental import pallas as pl
from jax.experimental.pallas import tpu as pltpu
from jax.sharding import Mesh, PartitionSpec as P

NBLK = 16
SEQ_LEN = 4096

EPSILON = 1e-06
DECAY_RATE = 8.0
PLANE = ("x", "y", "c")
SHARD = ("l", "y", "c")
EVERY = ("x", "l", "y", "c")
BF = jnp.bfloat16
F32 = jnp.float32


def norm_rows(values, factor):
    return values * lax.rsqrt(jnp.mean(values * values, axis=-1, keepdims=True) + EPSILON) * factor


def contract_rows(left_in, right_in):
    return lax.dot_general(
        left_in, right_in, (((0,), (0,)), ((), ())), preferred_element_type=F32
    )


def times_transposed(left_in, matrix):
    return lax.dot_general(
        left_in, matrix, (((1,), (1,)), ((), ())), preferred_element_type=F32
    )


def scan_kernel(rows, backward, a_ref, b_ref, pa_ref, pb_ref, carry):
    @pl.when(pl.program_id(1) == 0)
    def _():
        carry[0] = jnp.ones_like(carry[0])
        carry[1] = jnp.zeros_like(carry[1])

    place = lax.broadcasted_iota(jnp.int32, (8, a_ref.shape[-1]), 0)
    tiles = rows // 8

    def step(i, state):
        before_a, before_b = state
        tile = tiles - 1 - i if backward else i
        at = pl.ds(pl.multiple_of(tile * 8, 8), 8)
        a, b = a_ref[0, at, :], b_ref[0, at, :]
        for gap in (1, 2, 4):
            turn = 8 - gap if backward else gap
            inside = place < 8 - gap if backward else place >= gap
            near_a = jnp.where(inside, pltpu.roll(a, turn, 0), 1.0)
            near_b = jnp.where(inside, pltpu.roll(b, turn, 0), 0.0)
            b = b + a * near_b
            a = a * near_a
        b = b + a * before_b
        a = a * before_a
        pa_ref[0, at, :] = a
        pb_ref[0, at, :] = b
        last = 0 if backward else 7
        return (
            jnp.broadcast_to(a[last : last + 1], a.shape),
            jnp.broadcast_to(b[last : last + 1], b.shape),
        )

    end = lax.fori_loop(0, tiles, step, (carry[0], carry[1]))
    carry[0] = end[0]
    carry[1] = end[1]


def scan_pairs(a, b, backward):
    runs, length, channels = a.shape
    rows = 256
    steps = length // rows
    place = (lambda i, j: (i, steps - 1 - j, 0)) if backward else (lambda i, j: (i, j, 0))
    spec = pl.BlockSpec((1, rows, channels), place)
    return pl.pallas_call(
        functools.partial(scan_kernel, rows, backward),
        out_shape=[jax.ShapeDtypeStruct(a.shape, F32)] * 2,
        grid=(runs, steps),
        in_specs=[spec, spec],
        out_specs=[spec, spec],
        scratch_shapes=[pltpu.VMEM((2, 8, channels), F32)],
        compiler_params=pltpu.CompilerParams(vmem_limit_bytes=16 << 20),
        cost_estimate=pl.CostEstimate(
            flops=20 * a.size, bytes_accessed=16 * a.size, transcendentals=0
        ),
        name="scan_back" if backward else "scan_fwd",
    )(a, b)


def gate_terms(pre_sum, decay_in, conv_out, fresh, keep, width):
    recur_gate = jax.nn.sigmoid(pre_sum[..., :width])
    input_gate = jax.nn.sigmoid(pre_sum[..., width:])
    log_decay = -DECAY_RATE * jax.nn.softplus(-decay_in) * recur_gate
    coefficient = jnp.exp(log_decay) * keep
    scaling = jnp.where(fresh, 1.0, jnp.sqrt(-jnp.expm1(2.0 * log_decay)))
    return (coefficient, scaling * input_gate * conv_out)


def gated_product(first_in, second_in):
    return jax.nn.gelu(first_in) * second_in


def plane_gather(block):
    return lax.all_gather(block, PLANE, axis=0, tiled=True)


def plane_scatter(partial):
    return lax.psum_scatter(partial.astype(BF), PLANE, scatter_dimension=0, tiled=True)


def columns_in(weight, pieces):
    rows = weight.shape[0]
    pieces = pieces.reshape(rows, -1, 4, pieces.shape[-1])
    sent = jnp.moveaxis(pieces, 2, 0)
    got = lax.all_to_all(sent, ("y", "c"), split_axis=0, concat_axis=0, tiled=True)
    return lax.all_gather(got.reshape(4 * rows, -1), "l", axis=0, tiled=True)


def on_device(
    tokens,
    seg_ids,
    mix_gain,
    mix_in,
    conv_par,
    gate_w,
    gate_bias,
    decay,
    out_proj,
    mlp_gain,
    mlp_in,
    mlp_out,
    cotangent,
):
    lines = lax.axis_size("l")
    owners = 4 * lines
    half, line = lax.axis_index("x"), lax.axis_index("l")
    quarter = 2 * lax.axis_index("y") + lax.axis_index("c")
    mine = 4 * half + quarter
    me = 4 * line + quarter
    length, width = tokens.shape
    channels = owners * decay.shape[0]
    block_size = channels // NBLK
    own = channels // 8
    blocks = NBLK // 8
    ff = owners * mlp_out.shape[0]
    run = 4 * length
    plane = 8 * length
    share = mlp_out.shape[0] // 2
    rows = mix_in.shape[0]

    gains = lax.all_gather(jnp.stack([mix_gain, mlp_gain]), SHARD, axis=1, tiled=True)
    packed = jnp.concatenate([conv_par.T, gate_bias.T, decay[:, None], gate_w], axis=1)
    packed = lax.all_gather(packed, SHARD, axis=0, tiled=True)
    packed = lax.dynamic_slice_in_dim(packed, mine * own, own, 0)
    ids_all = lax.all_gather(seg_ids, EVERY, axis=0, tiled=True).reshape(2, lines, run)

    gain_one = gains[0].astype(F32)
    gain_two = gains[1].astype(F32)
    taps = packed[:, :5].T.astype(F32)
    bias = packed[:, 5:7].T.astype(F32)
    decay_own = packed[:, 7].astype(F32)
    gates = packed[:, 8:].reshape(blocks, block_size, 2 * block_size)

    inputs = tokens.astype(F32)
    normed_one = norm_rows(inputs, gain_one).astype(BF)
    all_one = plane_gather(normed_one)

    by_half = mix_in.reshape(rows, 2, 2, 4, own)
    by_half = lax.dynamic_index_in_dim(by_half, half, 2, keepdims=False)
    in_matrix = columns_in(mix_in, by_half)
    out_matrix = lax.dynamic_slice_in_dim(
        lax.all_gather(out_proj, SHARD, axis=0, tiled=True), mine * own, own, 0
    )
    by_half = mlp_in.reshape(rows, 2 * lines, 4, 2, share)
    by_half = lax.dynamic_index_in_dim(by_half, half, 3, keepdims=False)
    up_matrix = columns_in(mlp_in, by_half)
    down_matrix = lax.all_gather(
        lax.dynamic_slice_in_dim(mlp_out, half * share, share, 0), "l", axis=0, tiled=True
    )
    all_cot = plane_gather(cotangent)

    projected = jnp.dot(all_one, in_matrix, preferred_element_type=F32)
    branch = projected[:, :own].reshape(2, run, own)
    conv_in = projected[:, own:].astype(BF).reshape(2, run, own)

    ids = lax.dynamic_index_in_dim(ids_all, line, 1, keepdims=False)
    ids_before = lax.dynamic_index_in_dim(
        ids_all, jnp.maximum(line - 1, 0), 1, keepdims=False
    )[:, -3:]
    ids_before = jnp.where(line > 0, ids_before, -1)
    route = [(i, i + 1) for i in range(lines - 1)]
    rows_before = lax.ppermute(conv_in[:, -3:], "l", route)
    extended = jnp.concatenate([ids_before, ids], axis=1)
    places = (half * 0 + line * run + lax.broadcasted_iota(jnp.int32, (2, run), 1)) % SEQ_LEN
    fresh = (extended[:, 3:] != extended[:, 2:-1]) | (places == 0)
    keep = 1.0 - fresh.astype(F32)
    before_start = jnp.concatenate(
        [(extended[:, 1:3] == extended[:, 0:2]).astype(F32), keep], axis=1
    )
    padded_in = jnp.concatenate([rows_before, conv_in], axis=1).astype(F32)
    factors = [None]
    factor = jnp.ones((2, run), F32)
    conv_sum = taps[4] + taps[0] * padded_in[:, 3:]
    for offset in range(1, 4):
        factor = factor * before_start[:, 3 - offset : 3 - offset + run]
        factors.append(factor[:, :, None])
        conv_sum = (
            conv_sum
            + taps[offset] * padded_in[:, 3 - offset : 3 - offset + run] * factors[offset]
        )
    conv_out = conv_sum.astype(BF)
    conv_blocks = conv_out.reshape(plane, blocks, block_size)
    pre_sum = jnp.einsum("tbj,bjk->btk", conv_blocks, gates, preferred_element_type=F32)
    recur_pre = jnp.moveaxis(pre_sum[:, :, :block_size], 0, 1).reshape(2, run, own) + bias[0]
    input_pre = jnp.moveaxis(pre_sum[:, :, block_size:], 0, 1).reshape(2, run, own) + bias[1]
    pre_sum = jnp.concatenate([recur_pre, input_pre], axis=-1)
    (coefficient, drive), gate_pull = jax.vjp(
        lambda pre_in, decay_in, conv_value: gate_terms(
            pre_in, decay_in, conv_value, fresh[:, :, None], keep[:, :, None], own
        ),
        pre_sum,
        decay_own,
        conv_out.astype(F32),
    )
    prefix_coef, local_state = scan_pairs(coefficient, drive, False)
    ends = lax.all_gather(
        jnp.stack([prefix_coef[:, -1], local_state[:, -1]]), "l", axis=0, tiled=False
    )
    state_in = jnp.zeros((2, own), F32)
    for other in range(lines - 1):
        longer = ends[other, 0] * state_in + ends[other, 1]
        state_in = jnp.where(other < line, longer, state_in)
    state = local_state + prefix_coef * state_in[:, None]
    mixed = (state * jax.nn.gelu(branch)).astype(BF).reshape(plane, own)
    residual = inputs + plane_scatter(
        jnp.dot(mixed, out_matrix, preferred_element_type=F32)
    ).astype(F32)

    normed_two = norm_rows(residual, gain_two).astype(BF)
    all_two = plane_gather(normed_two)
    hidden = jnp.dot(all_two, up_matrix, preferred_element_type=F32)
    part = ff // 8
    activated = gated_product(hidden[:, :part], hidden[:, part:]).astype(BF)
    output = (
        residual
        + plane_scatter(jnp.dot(activated, down_matrix, preferred_element_type=F32)).astype(F32)
    ).astype(BF)

    act_grad = times_transposed(all_cot, down_matrix)
    _, act_pull = jax.vjp(gated_product, hidden[:, :part], hidden[:, part:])
    hidden_grad = jnp.concatenate(act_pull(act_grad), axis=1).astype(BF)
    normed_two_grad = plane_scatter(times_transposed(hidden_grad, up_matrix)).astype(F32)
    down_grad = contract_rows(activated, all_cot).astype(BF)
    down_grad = lax.psum_scatter(down_grad, "l", scatter_dimension=0, tiled=True)
    down_grad = lax.all_gather(down_grad, "x", axis=0, tiled=True).astype(F32)
    up_grad = contract_rows(all_two, hidden_grad).astype(BF)

    def columns_out(grad):
        grad = lax.psum_scatter(grad, "l", scatter_dimension=0, tiled=True)
        grad = lax.all_to_all(
            grad.reshape(4, rows, -1), ("y", "c"), split_axis=0, concat_axis=0, tiled=True
        )
        return lax.all_gather(grad, "x", axis=0, tiled=False)

    up_grad = columns_out(up_grad).reshape(2, 4, rows, 2 * lines, share)
    up_grad = up_grad.transpose(2, 3, 1, 0, 4).reshape(rows, 2 * ff).astype(F32)

    _, norm_two_pull = jax.vjp(norm_rows, residual, gain_two)
    residual_norm_grad, gain_two_grad = norm_two_pull(normed_two_grad)
    residual_grad = cotangent.astype(F32) + residual_norm_grad
    all_res = plane_gather(residual_grad.astype(BF))
    mixed_grad = times_transposed(all_res, out_matrix).reshape(2, run, own)
    out_grad = contract_rows(mixed, all_res)
    _, mix_pull = jax.vjp(
        lambda state_value, branch_value: state_value * jax.nn.gelu(branch_value), state, branch
    )
    state_grad, branch_grad = mix_pull(mixed_grad)
    next_coef = jnp.concatenate([coefficient[:, 1:], jnp.ones((2, 1, own), F32)], axis=1)
    suffix_coef, local_grad = scan_pairs(next_coef, state_grad, True)
    first = coefficient[:, 0]
    ends = lax.all_gather(
        jnp.stack([first * suffix_coef[:, 0], first * local_grad[:, 0]]), "l", axis=0, tiled=False
    )
    from_right = jnp.zeros((2, own), F32)
    for other in reversed(range(1, lines)):
        longer = ends[other, 0] * from_right + ends[other, 1]
        from_right = jnp.where(other > line, longer, from_right)
    total = local_grad + suffix_coef * from_right[:, None]
    prev_state = jnp.concatenate([state_in[:, None], state[:, :-1]], axis=1)
    pre_grad, decay_grad, conv_rec_grad = gate_pull((total * prev_state, total))
    pre_low = pre_grad.astype(BF)
    bias_grad = jnp.sum(pre_low.astype(F32), axis=(0, 1)).reshape(2, own)
    pre_low = pre_low.reshape(plane, 2, blocks, block_size)
    pre_low = pre_low.transpose(2, 0, 1, 3).reshape(blocks, plane, 2 * block_size)
    gate_grad = jnp.einsum(
        "tbj,btk->bjk", conv_blocks, pre_low, preferred_element_type=F32
    ).reshape(own, 2 * block_size)
    conv_grad = conv_rec_grad + jnp.einsum(
        "btk,bjk->tbj", pre_low, gates, preferred_element_type=F32
    ).reshape(2, run, own)
    edge_sum = jnp.zeros((2, run + 3, own), F32)
    tap_list = []
    for offset in range(4):
        masked = conv_grad if offset == 0 else conv_grad * factors[offset]
        edge_sum = edge_sum + jnp.pad(
            taps[offset] * masked, ((0, 0), (3 - offset, offset), (0, 0))
        )
        tap_list.append(
            jnp.sum(masked * padded_in[:, 3 - offset : 3 - offset + run], axis=(0, 1))
        )
    tap_list.append(jnp.sum(conv_grad, axis=(0, 1)))
    tap_grads = jnp.stack(tap_list)
    back_edge = lax.ppermute(edge_sum[:, :3], "l", [(i + 1, i) for i in range(lines - 1)])
    conv_in_grad = edge_sum[:, 3:] + jnp.pad(back_edge, ((0, 0), (run - 3, 0), (0, 0)))
    proj_grad = jnp.concatenate([branch_grad, conv_in_grad], axis=-1).astype(BF)
    proj_grad = proj_grad.reshape(plane, 2 * own)
    normed_one_grad = plane_scatter(times_transposed(proj_grad, in_matrix)).astype(F32)
    in_grad = columns_out(contract_rows(all_one, proj_grad).astype(BF))
    in_grad = in_grad.reshape(2, 4, rows, 2, own).transpose(2, 3, 0, 1, 4)
    in_grad = in_grad.reshape(rows, 2 * channels).astype(F32)
    _, norm_one_pull = jax.vjp(norm_rows, inputs, gain_one)
    input_norm_grad, gain_one_grad = norm_one_pull(normed_one_grad)
    input_grad = residual_grad + input_norm_grad

    def to_owners(values):
        padded = jnp.zeros((channels,) + values.shape[1:], values.dtype)
        padded = lax.dynamic_update_slice_in_dim(padded, values, mine * own, 0)
        return lax.psum(lax.psum_scatter(padded, SHARD, scatter_dimension=0, tiled=True), "x")

    out_grad = to_owners(out_grad.astype(BF)).astype(F32)
    small = jnp.concatenate(
        [tap_grads.T, bias_grad.T, decay_grad[:, None], gate_grad], axis=1
    )
    small = to_owners(small)
    gain_grads = lax.psum(
        lax.psum_scatter(
            jnp.stack([gain_one_grad, gain_two_grad], axis=1), SHARD, scatter_dimension=0, tiled=True
        ),
        "x",
    )
    return (
        output,
        input_grad,
        gain_grads[:, 0],
        in_grad,
        small[:, :5].T,
        small[:, 8:],
        small[:, 5:7].T,
        small[:, 7],
        out_grad,
        gain_grads[:, 1],
        up_grad,
        down_grad,
    )


def solution(mesh):
    count = mesh.shape["shard"]
    fine = Mesh(mesh.devices.reshape(2, count // 4, 2, 2), EVERY)
    rows, cols = P(EVERY, None), P(SHARD, None)
    placed = (
        rows,
        P(EVERY),
        P(SHARD),
        cols,
        P(None, SHARD),
        cols,
        P(None, SHARD),
        P(SHARD),
        cols,
        P(SHARD),
        cols,
        cols,
        rows,
    )
    return jax.shard_map(
        on_device,
        mesh=fine,
        in_specs=placed,
        out_specs=(
            rows,
            rows,
            P(SHARD),
            cols,
            P(None, SHARD),
            cols,
            P(None, SHARD),
            P(SHARD),
            cols,
            P(SHARD),
            cols,
            cols,
        ),
        check_vma=False,
    )
```

```python
import functools

import jax
import jax.numpy as jnp
from jax import lax
from jax.experimental import pallas as pl
from jax.experimental.pallas import tpu as pltpu
from jax.sharding import Mesh, PartitionSpec as P

NBLK = 16
SEQ_LEN = 4096

EPSILON = 1e-06
DECAY_RATE = 8.0
PLANE = ("x", "y", "c")
SHARD = ("l", "y", "c")
EVERY = ("x", "l", "y", "c")
BF = jnp.bfloat16
F32 = jnp.float32


def norm_rows(values, factor):
    return values * lax.rsqrt(jnp.mean(values * values, axis=-1, keepdims=True) + EPSILON) * factor


def contract_rows(left_in, right_in):
    return lax.dot_general(
        left_in, right_in, (((0,), (0,)), ((), ())), preferred_element_type=F32
    )


def times_transposed(left_in, matrix):
    return lax.dot_general(
        left_in, matrix, (((1,), (1,)), ((), ())), preferred_element_type=F32
    )


def scan_kernel(rows, backward, a_ref, b_ref, pa_ref, pb_ref, carry):
    @pl.when(pl.program_id(1) == 0)
    def _():
        carry[0] = jnp.ones_like(carry[0])
        carry[1] = jnp.zeros_like(carry[1])

    place = lax.broadcasted_iota(jnp.int32, (8, a_ref.shape[-1]), 0)
    tiles = rows // 8

    def step(i, state):
        before_a, before_b = state
        tile = tiles - 1 - i if backward else i
        at = pl.ds(pl.multiple_of(tile * 8, 8), 8)
        a, b = a_ref[0, at, :], b_ref[0, at, :]
        for gap in (1, 2, 4):
            turn = 8 - gap if backward else gap
            inside = place < 8 - gap if backward else place >= gap
            near_a = jnp.where(inside, pltpu.roll(a, turn, 0), 1.0)
            near_b = jnp.where(inside, pltpu.roll(b, turn, 0), 0.0)
            b = b + a * near_b
            a = a * near_a
        b = b + a * before_b
        a = a * before_a
        pa_ref[0, at, :] = a
        pb_ref[0, at, :] = b
        last = 0 if backward else 7
        return (
            jnp.broadcast_to(a[last : last + 1], a.shape),
            jnp.broadcast_to(b[last : last + 1], b.shape),
        )

    end = lax.fori_loop(0, tiles, step, (carry[0], carry[1]))
    carry[0] = end[0]
    carry[1] = end[1]


def scan_pairs(a, b, backward):
    runs, length, channels = a.shape
    rows = 256
    steps = length // rows
    place = (lambda i, j: (i, steps - 1 - j, 0)) if backward else (lambda i, j: (i, j, 0))
    spec = pl.BlockSpec((1, rows, channels), place)
    return pl.pallas_call(
        functools.partial(scan_kernel, rows, backward),
        out_shape=[jax.ShapeDtypeStruct(a.shape, F32)] * 2,
        grid=(runs, steps),
        in_specs=[spec, spec],
        out_specs=[spec, spec],
        scratch_shapes=[pltpu.VMEM((2, 8, channels), F32)],
        compiler_params=pltpu.CompilerParams(vmem_limit_bytes=16 << 20),
        cost_estimate=pl.CostEstimate(
            flops=20 * a.size, bytes_accessed=16 * a.size, transcendentals=0
        ),
        name="scan_back" if backward else "scan_fwd",
    )(a, b)


def gate_terms(pre_sum, decay_in, conv_out, fresh, keep, width):
    recur_gate = jax.nn.sigmoid(pre_sum[..., :width])
    input_gate = jax.nn.sigmoid(pre_sum[..., width:])
    log_decay = -DECAY_RATE * jax.nn.softplus(-decay_in) * recur_gate
    coefficient = jnp.exp(log_decay) * keep
    scaling = jnp.where(fresh, 1.0, jnp.sqrt(-jnp.expm1(2.0 * log_decay)))
    return (coefficient, scaling * input_gate * conv_out)


def gated_product(first_in, second_in):
    return jax.nn.gelu(first_in) * second_in


def plane_gather(block):
    return lax.all_gather(block, PLANE, axis=0, tiled=True)


def plane_scatter(partial):
    return lax.psum_scatter(partial.astype(BF), PLANE, scatter_dimension=0, tiled=True)


MESH = pl.DeviceIdType.MESH


class Wires:
    def __init__(self, send_sems, recv_sems):
        self.send_sems, self.recv_sems, self.used = send_sems, recv_sems, 0

    def far(self, src, dst, device):
        at = self.used
        self.used += 1
        return pltpu.make_async_remote_copy(
            src_ref=src,
            dst_ref=dst,
            send_sem=self.send_sems.at[at],
            recv_sem=self.recv_sems.at[at],
            device_id=device,
            device_id_type=MESH,
        )

    def near(self, src, dst):
        at = self.used
        self.used += 1
        return pltpu.make_async_copy(src, dst, self.send_sems.at[at])


def greet(devices):
    barrier = pltpu.get_barrier_semaphore()
    for device in devices:
        pl.semaphore_signal(barrier, inc=1, device_id=device, device_id_type=MESH)
    pl.semaphore_wait(barrier, len(devices))


def sides():
    x, l, y, c = tuple(lax.axis_index(name) for name in EVERY)
    x_a, y_a = x + (1 - c) * (1 - 2 * x), y + c * (1 - 2 * y)
    x_b, y_b = x + c * (1 - 2 * x), y + (1 - c) * (1 - 2 * y)
    return (x, l, y, c), (x, l, y, 1 - c), (x_a, l, y_a, c), (x_b, l, y_b, c)


def slot_of(device):
    return device[0] * 4 + device[2] * 2 + device[3]


def over_rows(length, rows, step):
    @pl.loop(0, length // rows)
    def _(i):
        step(pl.ds(pl.multiple_of(i * rows, rows), rows))


class PlaneSum:
    def __init__(self, wires, partial, own, got, hop_a, hop_b, cuts):
        self.own, self.got, self.hop_a, self.hop_b = own, got, hop_a, hop_b
        self.cuts, self.part = cuts, own.shape[1] // cuts
        me, core, side_a, side_b = sides()
        diag = (1 - me[0], me[1], 1 - me[2], me[3])
        self.chips = [me, side_a, side_b, diag]
        self.theirs = {0: 0, 1: 2, 2: 1, 3: 3}
        self.order = [3, 1, 2, 0]
        self.swaps, self.loads = {}, {}
        self.far_a, self.near_a, self.far_b = {}, {}, {}
        for piece in range(cuts):
            rows = pl.ds(piece * self.part, self.part)
            for rel in self.order:
                chip = self.chips[rel]
                away = slot_of((chip[0], chip[1], chip[2], 1 - me[3]))
                self.swaps[rel, piece] = wires.far(
                    partial.at[away, rows], got.at[self.theirs[rel], rows], core
                )
                self.loads[rel, piece] = wires.near(
                    partial.at[slot_of(chip), rows], own.at[rel, rows]
                )
            self.far_a[piece] = wires.far(own.at[3, rows], hop_a.at[0, rows], side_a)
            self.near_a[piece] = wires.far(own.at[1, rows], hop_a.at[1, rows], side_a)
            self.far_b[piece] = wires.far(own.at[2, rows], hop_b.at[rows], side_b)

    def start(self):
        for rel in self.order:
            for piece in range(self.cuts):
                self.swaps[rel, piece].start()
                self.loads[rel, piece].start()

    def landed(self, rel, piece):
        self.loads[rel, piece].wait()
        self.swaps[self.theirs[rel], piece].wait_recv()

    def join(self, rel, piece, hopped):
        @pl.loop(0, self.part // 16)
        def _(i):
            rows = pl.ds(pl.multiple_of(piece * self.part + i * 16, 16), 16)
            total = self.own[rel, rows].astype(F32) + self.got[rel, rows].astype(F32)
            if hopped:
                total = total + self.hop_a[0, rows].astype(F32)
            self.own[rel, rows] = total.astype(BF)

    def first_side(self):
        for rel, copies in ((3, self.far_a), (1, self.near_a)):
            for piece in range(self.cuts):
                self.landed(rel, piece)
                self.join(rel, piece, False)
                copies[piece].start()

    def second_side(self):
        for piece in range(self.cuts):
            self.landed(2, piece)
            self.far_a[piece].wait_recv()
            self.join(2, piece, True)
            self.far_b[piece].start()

    def finish(self, piece, use):
        self.landed(0, piece)
        self.near_a[piece].wait_recv()
        self.far_b[piece].wait_recv()

        @pl.loop(0, self.part // 16)
        def _(i):
            rows = pl.ds(pl.multiple_of(piece * self.part + i * 16, 16), 16)
            total = self.own[0, rows].astype(F32) + self.got[0, rows].astype(F32)
            total = total + self.hop_a[1, rows].astype(F32) + self.hop_b[rows].astype(F32)
            use(rows, total)

    def drain(self):
        for piece in range(self.cuts):
            for rel in self.order:
                self.swaps[rel, piece].wait_send()
            for copy in (self.far_a[piece], self.near_a[piece], self.far_b[piece]):
                copy.wait_send()


class LineSum:
    def __init__(self, wires, lines, own, from_left, from_right, root):
        x, l, y, c = (lax.axis_index(name) for name in EVERY)
        self.own, self.from_left, self.from_right = own, from_left, from_right
        self.l, self.root, self.lines = l, root, lines
        self.to_right = wires.far(own, from_left, (x, l + 1, y, c))
        self.to_left = wires.far(own, from_right, (x, l - 1, y, c))

    def add(self, other):
        @pl.loop(0, self.own.shape[0] // 16)
        def _(i):
            at = pl.ds(pl.multiple_of(i * 16, 16), 16)
            self.own[at] = (self.own[at].astype(F32) + other[at].astype(F32)).astype(BF)

    def rightward(self):
        @pl.when(self.l < self.root)
        def _():
            @pl.when(self.l > 0)
            def _():
                self.to_right.wait_recv()
                self.add(self.from_left)

            self.to_right.start()

    def leftward(self):
        @pl.when(self.l > self.root)
        def _():
            @pl.when(self.l < self.lines - 1)
            def _():
                self.to_left.wait_recv()
                self.add(self.from_right)

            self.to_left.start()

    def end(self):
        @pl.when(self.l == self.root)
        def _():
            @pl.when(self.l > 0)
            def _():
                self.to_right.wait_recv()
                self.add(self.from_left)

            @pl.when(self.l < self.lines - 1)
            def _():
                self.to_left.wait_recv()
                self.add(self.from_right)

    def drain(self):
        @pl.when(self.l < self.root)
        def _():
            self.to_right.wait_send()

        @pl.when(self.l > self.root)
        def _():
            self.to_left.wait_send()


def back_rows(base_ref, up_ref, gain_ref, out_ref, gain_out, mine):
    def use(rows, total):
        base = base_ref[rows].astype(F32)
        scale = lax.rsqrt(jnp.mean(base * base, axis=-1, keepdims=True) + EPSILON)
        lean = total * gain_ref[...]
        along = jnp.mean(lean * base, axis=-1, keepdims=True)
        grad = up_ref[rows].astype(F32) + scale * lean
        grad = grad - base * (scale * scale * scale * along)
        out_ref[rows] = grad
        if mine is not None:
            mine[rows] = grad.astype(BF)
        share = total * base * scale
        gain_out[...] += share[:8] + share[8:]

    return use


def forward_rows(base_ref, gain_ref, out_ref, mine):
    def use(rows, total):
        base = base_ref[rows].astype(F32) + total
        out_ref[rows] = base
        scale = lax.rsqrt(jnp.mean(base * base, axis=-1, keepdims=True) + EPSILON)
        mine[rows] = (base * scale * gain_ref[...]).astype(BF)

    return use


class PlaneGather:
    def __init__(self, wires, mine, everything, cuts):
        me, core, side_a, side_b = sides()
        diag = (1 - me[0], me[1], 1 - me[2], me[3])
        here, from_a, from_b, from_diag = [slot_of(at) for at in (me, side_a, side_b, diag)]
        self.cuts, self.copies = cuts, {}
        part = mine.shape[0] // cuts
        for piece in range(cuts):
            rows = pl.ds(piece * part, part)
            for name, src, slot, target in (
                ("a", mine.at[rows], here, side_a),
                ("b", mine.at[rows], here, side_b),
                ("c", mine.at[rows], here, core),
                ("ab", everything.at[from_a, rows], from_a, side_b),
                ("ac", everything.at[from_a, rows], from_a, core),
                ("bc", everything.at[from_b, rows], from_b, core),
                ("dc", everything.at[from_diag, rows], from_diag, core),
            ):
                self.copies[name, piece] = wires.far(src, everything.at[slot, rows], target)
            self.copies["own", piece] = wires.near(mine.at[rows], everything.at[here, rows])

    def start(self, piece):
        for name in ("a", "b", "c", "own"):
            self.copies[name, piece].start()

    def forward(self, came, goes):
        for piece in range(self.cuts):
            self.copies[came, piece].wait_recv()
            for name in goes:
                self.copies[name, piece].start()

    def finish(self):
        for piece in range(self.cuts):
            for name in ("c", "ac", "bc", "dc"):
                self.copies[name, piece].wait_recv()
            self.copies["own", piece].wait()
            for name in ("a", "b", "c", "ab", "ac", "bc", "dc"):
                self.copies[name, piece].wait_send()


def plane_kernel(mode, cuts, *refs):
    refs = list(refs)
    partial, base_ref = refs.pop(0), refs.pop(0)
    up_ref = refs.pop(0) if mode == "back" else None
    gain_ref, out_ref = refs.pop(0), refs.pop(0)
    gain_out = refs.pop(0) if mode == "back" else None
    all_ref, own, got, hop_a, hop_b, mine, send_sems, recv_sems = refs
    _, core, side_a, side_b = sides()
    wires = Wires(send_sems, recv_sems)
    greet([core, side_a, side_b])
    total = PlaneSum(wires, partial, own, got, hop_a, hop_b, cuts)
    spread = PlaneGather(wires, mine, all_ref, cuts)
    total.start()
    total.first_side()
    total.second_side()
    if mode == "back":
        gain_out[...] = jnp.zeros_like(gain_out)
        use = back_rows(base_ref, up_ref, gain_ref, out_ref, gain_out, mine)
    else:
        use = forward_rows(base_ref, gain_ref, out_ref, mine)
    for piece in range(cuts):
        total.finish(piece, use)
        spread.start(piece)
    spread.forward("a", ("ab", "ac"))
    spread.forward("b", ("bc",))
    spread.forward("ab", ("dc",))
    spread.finish()
    total.drain()


def sum_scratch(length, width):
    return [
        pltpu.VMEM((4, length, width), BF),
        pltpu.VMEM((4, length, width), BF),
        pltpu.VMEM((2, length, width), BF),
        pltpu.VMEM((length, width), BF),
    ]


def plane_sum(partial, base, up, gain, number):
    mode = "forward" if up is None else "back"
    length, width = base.shape
    cuts = 2
    vmem, left = pl.BlockSpec(memory_space=pltpu.VMEM), pl.BlockSpec(memory_space=pl.ANY)
    args, specs = [partial.reshape(8, length, width), base], [left, vmem]
    outs, out_specs = [jax.ShapeDtypeStruct((length, width), F32)], [vmem]
    if mode == "back":
        args.append(up)
        specs.append(vmem)
        outs.append(jax.ShapeDtypeStruct((8, width), F32))
        out_specs.append(vmem)
    args.append(gain.reshape(1, width))
    specs.append(vmem)
    outs.append(jax.ShapeDtypeStruct((8, length, width), BF))
    out_specs.append(left)
    sems = cuts * (8 + 3 + 8)
    got = list(
        pl.pallas_call(
            functools.partial(plane_kernel, mode, cuts),
            out_shape=outs,
            in_specs=specs,
            out_specs=out_specs,
            scratch_shapes=sum_scratch(length, width)
            + [
                pltpu.VMEM((length, width), BF),
                pltpu.SemaphoreType.DMA((sems,)),
                pltpu.SemaphoreType.DMA((sems,)),
            ],
            compiler_params=pltpu.CompilerParams(
                collective_id=number, has_side_effects=True, vmem_limit_bytes=40 << 20
            ),
            cost_estimate=pl.CostEstimate(
                flops=20 * base.size, bytes_accessed=400 * base.size, transcendentals=0
            ),
            name=f"plane_{mode}_{number}",
        )(*args)
    )
    got[-1] = got[-1].reshape(8 * length, width)
    return got


def tail_kernel(lines, cuts, *refs):
    (partial, base_ref, up_ref, gain_ref, other_gain, in_ref, chan_ref, upz, downz) = refs[:9]
    (out_ref, in_all, chan_out, up_all, down_all, gains) = refs[9:15]
    (own, got, hop_a, hop_b, gain_out, in_own, in_left, in_right) = refs[15:23]
    (chan_own, chan_left, chan_right, chan_got, tiny, tiny_line, send_sems, recv_sems) = refs[23:]
    me, core, side_a, side_b = sides()
    x, l, y, c = me
    k = 2 * y + c
    mates = [core, (x, l, 1 - y, c), (x, l, 1 - y, 1 - c)]
    twin = (1 - x, l, y, c)
    twins = [(1 - x, l, at[2], at[3]) for at in mates]
    wires = Wires(send_sems, recv_sems)
    others = [(x, lax.rem(l + d, lines), y, c) for d in range(1, lines)]
    greet(mates + [twin] + twins + others)

    total = PlaneSum(wires, partial, own, got, hop_a, hop_b, cuts)
    per = chan_ref.shape[0]
    owner = (4 * x + k) * per
    load_in = wires.near(in_ref, in_own)
    load_chan = wires.near(chan_ref, chan_own)
    in_sums = [
        LineSum(wires, lines, in_own.at[q], in_left.at[q], in_right.at[q], q)
        for q in range(lines)
    ]
    chan_roots = [(owner + i) // 4 for i in range(per)]
    chan_sums = [
        LineSum(wires, lines, chan_own.at[i], chan_left.at[i], chan_right.at[i], chan_roots[i])
        for i in range(per)
    ]

    def deliver(block, target):
        copies = [wires.near(block(k), target.at[x, k])]
        for at in [twin] + mates + twins:
            copies.append(wires.far(block(2 * at[2] + at[3]), target.at[x, k], at))
        return copies

    total.start()
    load_in.start()
    load_chan.start()
    up_copies = deliver(lambda to: upz.at[to], up_all)
    down_copies = [wires.near(downz, down_all.at[x]), wires.far(downz, down_all.at[x], twin)]
    load_in.wait()
    q = lines - 1
    in_sums[q].rightward()
    in_sums[lines - 1 - q].leftward()
    total.first_side()
    for copy in down_copies + up_copies:
        copy.start()
    total.second_side()
    for q in reversed(range(1, lines - 1)):
        in_sums[q].rightward()
        in_sums[lines - 1 - q].leftward()
    gain_out[...] = jnp.zeros_like(gain_out)
    use = back_rows(base_ref, up_ref, gain_ref, out_ref, gain_out, None)
    for piece in range(cuts):
        total.finish(piece, use)
    load_chan.wait()
    for one in chan_sums:
        one.rightward()
        one.leftward()
    for q in range(lines):
        in_sums[q].end()
    rows = in_all.shape[2]
    in_copies = deliver(
        lambda to: in_own.at[l, pl.ds(pl.multiple_of(to * rows, rows), rows)], in_all
    )
    for copy in in_copies:
        copy.start()
    lane = lax.broadcasted_iota(jnp.int32, tiny.shape[1:], 0)
    first = jnp.sum(gain_out[...], axis=0, keepdims=True)
    second = jnp.sum(other_gain[...], axis=0, keepdims=True)
    tiny[0] = jnp.where(lane == 0, first, jnp.where(lane == 1, second, 0.0))
    for step, at in enumerate((core, twin, (x, l, 1 - y, c))):
        copy = wires.far(tiny.at[2 * step], tiny.at[2 * step + 1], at)
        copy.start()
        copy.wait()
        tiny[2 * step + 2] = tiny[2 * step] + tiny[2 * step + 1]
    line_copies = []
    for d, device in enumerate(others):
        line_copies.append(wires.far(tiny.at[6], tiny_line.at[l], device))
        line_copies[-1].start()
    tiny_line[l] = tiny[6]
    for one in chan_sums:
        one.end()
    goal = 4 * l + k
    holds = goal // (4 * per) == x
    chan_far, chan_near = [], []
    for i in range(per):
        s = owner + i
        mate = (x, l, lax.rem(s, 4) // 2, lax.rem(s, 2))
        far = wires.far(chan_own.at[i], chan_got, mate)
        near = wires.near(chan_own.at[i], chan_got)
        at_root = chan_roots[i] == l
        away = jnp.logical_and(at_root, lax.rem(s, 4) != k)
        stay = jnp.logical_and(at_root, lax.rem(s, 4) == k)
        chan_far.append((far, away))
        chan_near.append((near, stay))

        @pl.when(away)
        def _():
            far.start()

        @pl.when(stay)
        def _():
            near.start()
            near.wait()

    holder = lax.rem(goal // per, 4)
    for i in range(per):
        mine_here = jnp.logical_and(holds, lax.rem(goal, per) == i)

        @pl.when(jnp.logical_and(mine_here, holder != k))
        def _():
            chan_far[i][0].wait_recv()

    to_twin = wires.far(chan_got, chan_out, twin)
    keep = wires.near(chan_got, chan_out)

    @pl.when(holds)
    def _():
        to_twin.start()
        keep.start()
        keep.wait()

    @pl.when(jnp.logical_not(holds))
    def _():
        to_twin.wait_recv()

    for copy in line_copies:
        copy.wait()
    gains[...] = tiny_line[0]
    for q in range(1, lines):
        gains[...] += tiny_line[q]
    for copies in (in_copies, up_copies, down_copies):
        for copy in copies:
            copy.wait()

    @pl.when(holds)
    def _():
        to_twin.wait_send()

    for far, away in chan_far:

        @pl.when(away)
        def _():
            far.wait_send()

    for one in in_sums + chan_sums:
        one.drain()
    total.drain()


def tail(partial, base, up, gain, other_gain, in_grad, chan, upz, downz, lines):
    length, width = base.shape
    cuts = 2
    vmem, left = pl.BlockSpec(memory_space=pltpu.VMEM), pl.BlockSpec(memory_space=pl.ANY)
    rows = in_grad.shape[0] // (4 * lines)
    pieces = in_grad.reshape(lines, 4 * rows, in_grad.shape[1])
    per = chan.shape[0]
    sems = cuts * 11 + 2 + 2 * (lines + per) + 16 + 2 + 8 + 3 + lines + 2 * per + 4
    return pl.pallas_call(
        functools.partial(tail_kernel, lines, cuts),
        out_shape=[
            jax.ShapeDtypeStruct((length, width), F32),
            jax.ShapeDtypeStruct((2, 4, rows, in_grad.shape[1]), BF),
            jax.ShapeDtypeStruct(chan.shape[1:], BF),
            jax.ShapeDtypeStruct((2,) + upz.shape, BF),
            jax.ShapeDtypeStruct((2,) + downz.shape, BF),
            jax.ShapeDtypeStruct((8, width), F32),
        ],
        in_specs=[left, vmem, vmem, vmem, vmem, left, left, left, left],
        out_specs=[vmem, left, left, left, left, vmem],
        scratch_shapes=sum_scratch(length, width)
        + [pltpu.VMEM((8, width), F32)]
        + [pltpu.VMEM(pieces.shape, BF)] * 3
        + [pltpu.VMEM(chan.shape, BF)] * 3
        + [
            pltpu.VMEM(chan.shape[1:], BF),
            pltpu.VMEM((7, 8, width), F32),
            pltpu.VMEM((lines, 8, width), F32),
            pltpu.SemaphoreType.DMA((sems,)),
            pltpu.SemaphoreType.DMA((sems,)),
        ],
        compiler_params=pltpu.CompilerParams(
            collective_id=3, has_side_effects=True, vmem_limit_bytes=56 << 20
        ),
        cost_estimate=pl.CostEstimate(
            flops=20 * base.size, bytes_accessed=400 * base.size, transcendentals=0
        ),
        name="tail",
    )(partial.reshape(8, length, width), base, up, gain.reshape(1, width), other_gain, pieces, chan, upz, downz)


def columns_in(weight, pieces):
    rows = weight.shape[0]
    pieces = pieces.reshape(rows, -1, 4, pieces.shape[-1])
    sent = jnp.moveaxis(pieces, 2, 0)
    got = lax.all_to_all(sent, ("y", "c"), split_axis=0, concat_axis=0, tiled=True)
    return lax.all_gather(got.reshape(4 * rows, -1), "l", axis=0, tiled=True)


def on_device(
    tokens,
    seg_ids,
    mix_gain,
    mix_in,
    conv_par,
    gate_w,
    gate_bias,
    decay,
    out_proj,
    mlp_gain,
    mlp_in,
    mlp_out,
    cotangent,
):
    lines = lax.axis_size("l")
    owners = 4 * lines
    half, line = lax.axis_index("x"), lax.axis_index("l")
    quarter = 2 * lax.axis_index("y") + lax.axis_index("c")
    mine = 4 * half + quarter
    me = 4 * line + quarter
    length, width = tokens.shape
    channels = owners * decay.shape[0]
    block_size = channels // NBLK
    own = channels // 8
    blocks = NBLK // 8
    ff = owners * mlp_out.shape[0]
    run = 4 * length
    plane = 8 * length
    share = mlp_out.shape[0] // 2
    rows = mix_in.shape[0]

    gains = lax.all_gather(jnp.stack([mix_gain, mlp_gain]), SHARD, axis=1, tiled=True)
    packed = jnp.concatenate([conv_par.T, gate_bias.T, decay[:, None], gate_w], axis=1)
    packed = lax.all_gather(packed, SHARD, axis=0, tiled=True)
    packed = lax.dynamic_slice_in_dim(packed, mine * own, own, 0)
    ids_all = lax.all_gather(seg_ids, EVERY, axis=0, tiled=True).reshape(2, lines, run)

    gain_one = gains[0].astype(F32)
    gain_two = gains[1].astype(F32)
    taps = packed[:, :5].T.astype(F32)
    bias = packed[:, 5:7].T.astype(F32)
    decay_own = packed[:, 7].astype(F32)
    gates = packed[:, 8:].reshape(blocks, block_size, 2 * block_size)

    inputs = tokens.astype(F32)
    normed_one = norm_rows(inputs, gain_one).astype(BF)
    all_one = plane_gather(normed_one)

    by_half = mix_in.reshape(rows, 2, 2, 4, own)
    by_half = lax.dynamic_index_in_dim(by_half, half, 2, keepdims=False)
    in_matrix = columns_in(mix_in, by_half)
    out_matrix = lax.dynamic_slice_in_dim(
        lax.all_gather(out_proj, SHARD, axis=0, tiled=True), mine * own, own, 0
    )
    by_half = mlp_in.reshape(rows, 2 * lines, 4, 2, share)
    by_half = lax.dynamic_index_in_dim(by_half, half, 3, keepdims=False)
    up_matrix = columns_in(mlp_in, by_half)
    down_matrix = lax.all_gather(
        lax.dynamic_slice_in_dim(mlp_out, half * share, share, 0), "l", axis=0, tiled=True
    )
    all_cot = plane_gather(cotangent)

    projected = jnp.dot(all_one, in_matrix, preferred_element_type=F32)
    branch = projected[:, :own].reshape(2, run, own)
    conv_in = projected[:, own:].astype(BF).reshape(2, run, own)

    ids = lax.dynamic_index_in_dim(ids_all, line, 1, keepdims=False)
    ids_before = lax.dynamic_index_in_dim(
        ids_all, jnp.maximum(line - 1, 0), 1, keepdims=False
    )[:, -3:]
    ids_before = jnp.where(line > 0, ids_before, -1)
    route = [(i, i + 1) for i in range(lines - 1)]
    rows_before = lax.ppermute(conv_in[:, -3:], "l", route)
    extended = jnp.concatenate([ids_before, ids], axis=1)
    places = (half * 0 + line * run + lax.broadcasted_iota(jnp.int32, (2, run), 1)) % SEQ_LEN
    fresh = (extended[:, 3:] != extended[:, 2:-1]) | (places == 0)
    keep = 1.0 - fresh.astype(F32)
    before_start = jnp.concatenate(
        [(extended[:, 1:3] == extended[:, 0:2]).astype(F32), keep], axis=1
    )
    padded_in = jnp.concatenate([rows_before, conv_in], axis=1).astype(F32)
    factors = [None]
    factor = jnp.ones((2, run), F32)
    conv_sum = taps[4] + taps[0] * padded_in[:, 3:]
    for offset in range(1, 4):
        factor = factor * before_start[:, 3 - offset : 3 - offset + run]
        factors.append(factor[:, :, None])
        conv_sum = (
            conv_sum
            + taps[offset] * padded_in[:, 3 - offset : 3 - offset + run] * factors[offset]
        )
    conv_out = conv_sum.astype(BF)
    conv_blocks = conv_out.reshape(plane, blocks, block_size)
    pre_sum = jnp.einsum("tbj,bjk->btk", conv_blocks, gates, preferred_element_type=F32)
    recur_pre = jnp.moveaxis(pre_sum[:, :, :block_size], 0, 1).reshape(2, run, own) + bias[0]
    input_pre = jnp.moveaxis(pre_sum[:, :, block_size:], 0, 1).reshape(2, run, own) + bias[1]
    pre_sum = jnp.concatenate([recur_pre, input_pre], axis=-1)
    (coefficient, drive), gate_pull = jax.vjp(
        lambda pre_in, decay_in, conv_value: gate_terms(
            pre_in, decay_in, conv_value, fresh[:, :, None], keep[:, :, None], own
        ),
        pre_sum,
        decay_own,
        conv_out.astype(F32),
    )
    prefix_coef, local_state = scan_pairs(coefficient, drive, False)
    ends = lax.all_gather(
        jnp.stack([prefix_coef[:, -1], local_state[:, -1]]), "l", axis=0, tiled=False
    )
    state_in = jnp.zeros((2, own), F32)
    for other in range(lines - 1):
        longer = ends[other, 0] * state_in + ends[other, 1]
        state_in = jnp.where(other < line, longer, state_in)
    state = local_state + prefix_coef * state_in[:, None]
    mixed = (state * jax.nn.gelu(branch)).astype(BF).reshape(plane, own)
    partial = jnp.dot(mixed, out_matrix, preferred_element_type=F32).astype(BF)
    residual, all_two = plane_sum(partial, tokens, None, gain_two, 1)
    hidden = jnp.dot(all_two, up_matrix, preferred_element_type=F32)
    part = ff // 8
    activated = gated_product(hidden[:, :part], hidden[:, part:]).astype(BF)
    out_partial = jnp.dot(activated, down_matrix, preferred_element_type=F32).astype(BF)
    out_partial, all_cot = lax.optimization_barrier((out_partial, all_cot))
    output = (residual + plane_scatter(out_partial).astype(F32)).astype(BF)

    act_grad = times_transposed(all_cot, down_matrix)
    _, act_pull = jax.vjp(gated_product, hidden[:, :part], hidden[:, part:])
    hidden_grad = jnp.concatenate(act_pull(act_grad), axis=1).astype(BF)
    partial = times_transposed(hidden_grad, up_matrix).astype(BF)
    down_grad = contract_rows(activated, all_cot).astype(BF)
    up_grad = contract_rows(all_two, hidden_grad).astype(BF)
    partial, down_grad, up_grad = lax.optimization_barrier((partial, down_grad, up_grad))
    down_line = lax.psum_scatter(down_grad, "l", scatter_dimension=0, tiled=True)
    up_line = lax.psum_scatter(up_grad, "l", scatter_dimension=0, tiled=True)
    residual_grad, gain_two_grad, all_res = plane_sum(partial, residual, cotangent, gain_two, 2)
    mixed_grad = times_transposed(all_res, out_matrix).reshape(2, run, own)
    out_grad = contract_rows(mixed, all_res)
    _, mix_pull = jax.vjp(
        lambda state_value, branch_value: state_value * jax.nn.gelu(branch_value), state, branch
    )
    state_grad, branch_grad = mix_pull(mixed_grad)
    next_coef = jnp.concatenate([coefficient[:, 1:], jnp.ones((2, 1, own), F32)], axis=1)
    suffix_coef, local_grad = scan_pairs(next_coef, state_grad, True)
    first = coefficient[:, 0]
    ends = lax.all_gather(
        jnp.stack([first * suffix_coef[:, 0], first * local_grad[:, 0]]), "l", axis=0, tiled=False
    )
    from_right = jnp.zeros((2, own), F32)
    for other in reversed(range(1, lines)):
        longer = ends[other, 0] * from_right + ends[other, 1]
        from_right = jnp.where(other > line, longer, from_right)
    total = local_grad + suffix_coef * from_right[:, None]
    prev_state = jnp.concatenate([state_in[:, None], state[:, :-1]], axis=1)
    pre_grad, decay_grad, conv_rec_grad = gate_pull((total * prev_state, total))
    pre_low = pre_grad.astype(BF)
    bias_grad = jnp.sum(pre_low.astype(F32), axis=(0, 1)).reshape(2, own)
    pre_low = pre_low.reshape(plane, 2, blocks, block_size)
    pre_low = pre_low.transpose(2, 0, 1, 3).reshape(blocks, plane, 2 * block_size)
    gate_grad = jnp.einsum(
        "tbj,btk->bjk", conv_blocks, pre_low, preferred_element_type=F32
    ).reshape(own, 2 * block_size)
    conv_grad = conv_rec_grad + jnp.einsum(
        "btk,bjk->tbj", pre_low, gates, preferred_element_type=F32
    ).reshape(2, run, own)
    edge_sum = jnp.zeros((2, run + 3, own), F32)
    tap_list = []
    for offset in range(4):
        masked = conv_grad if offset == 0 else conv_grad * factors[offset]
        edge_sum = edge_sum + jnp.pad(
            taps[offset] * masked, ((0, 0), (3 - offset, offset), (0, 0))
        )
        tap_list.append(
            jnp.sum(masked * padded_in[:, 3 - offset : 3 - offset + run], axis=(0, 1))
        )
    tap_list.append(jnp.sum(conv_grad, axis=(0, 1)))
    tap_grads = jnp.stack(tap_list)
    back_edge = lax.ppermute(edge_sum[:, :3], "l", [(i + 1, i) for i in range(lines - 1)])
    conv_in_grad = edge_sum[:, 3:] + jnp.pad(back_edge, ((0, 0), (run - 3, 0), (0, 0)))
    proj_grad = jnp.concatenate([branch_grad, conv_in_grad], axis=-1).astype(BF)
    proj_grad = proj_grad.reshape(plane, 2 * own)
    partial = times_transposed(proj_grad, in_matrix).astype(BF)
    in_grad = contract_rows(all_one, proj_grad).astype(BF)
    owned = channels // owners
    chan = jnp.concatenate(
        [out_grad, tap_grads.T, bias_grad.T, decay_grad[:, None], gate_grad], axis=1
    ).astype(BF)
    used = chan.shape[1]
    chan = jnp.pad(
        chan.reshape(own // owned, owned, used), ((0, 0), (0, -owned % 16), (0, -used % 128))
    )
    input_grad, in_all, chan, up_all, down_all, gain_grads = tail(
        partial,
        tokens,
        residual_grad,
        gain_one,
        gain_two_grad,
        in_grad,
        chan,
        up_line.reshape(4, rows, -1),
        down_line,
        lines,
    )
    in_grad = in_all.reshape(2, 4, rows, 2, own).transpose(2, 3, 0, 1, 4)
    in_grad = in_grad.reshape(rows, 2 * channels).astype(F32)
    up_grad = up_all.reshape(2, 4, rows, 2 * lines, share).transpose(2, 3, 1, 0, 4)
    up_grad = up_grad.reshape(rows, 2 * ff).astype(F32)
    down_grad = down_all.reshape(2 * share, width).astype(F32)
    out_grad = chan[:owned, :width].astype(F32)
    small = chan[:owned, width:used].astype(F32)
    gain_grads = lax.dynamic_slice_in_dim(gain_grads[:2], me * rows, rows, 1)
    return (
        output,
        input_grad,
        gain_grads[0],
        in_grad,
        small[:, :5].T,
        small[:, 8:],
        small[:, 5:7].T,
        small[:, 7],
        out_grad,
        gain_grads[1],
        up_grad,
        down_grad,
    )


def solution(mesh):
    count = mesh.shape["shard"]
    fine = Mesh(mesh.devices.reshape(2, count // 4, 2, 2), EVERY)
    rows, cols = P(EVERY, None), P(SHARD, None)
    placed = (
        rows,
        P(EVERY),
        P(SHARD),
        cols,
        P(None, SHARD),
        cols,
        P(None, SHARD),
        P(SHARD),
        cols,
        P(SHARD),
        cols,
        cols,
        rows,
    )
    return jax.shard_map(
        on_device,
        mesh=fine,
        in_specs=placed,
        out_specs=(
            rows,
            rows,
            P(SHARD),
            cols,
            P(None, SHARD),
            cols,
            P(None, SHARD),
            P(SHARD),
            cols,
            P(SHARD),
            cols,
            cols,
        ),
        check_vma=False,
    )
```

```python
import functools

import jax
import jax.numpy as jnp
from jax import lax
from jax.experimental import pallas as pl
from jax.experimental.pallas import tpu as pltpu
from jax.sharding import Mesh, PartitionSpec as P

NBLK = 16
SEQ_LEN = 4096

EPSILON = 1e-06
DECAY_RATE = 8.0
PLANE = ("x", "y", "c")
SHARD = ("l", "y", "c")
EVERY = ("x", "l", "y", "c")
BF = jnp.bfloat16
F32 = jnp.float32


def norm_rows(values, factor):
    return values * lax.rsqrt(jnp.mean(values * values, axis=-1, keepdims=True) + EPSILON) * factor


def contract_rows(left_in, right_in):
    return lax.dot_general(
        left_in, right_in, (((0,), (0,)), ((), ())), preferred_element_type=F32
    )


def times_transposed(left_in, matrix):
    return lax.dot_general(
        left_in, matrix, (((1,), (1,)), ((), ())), preferred_element_type=F32
    )


def gated_product(first_in, second_in):
    return jax.nn.gelu(first_in) * second_in


def plane_gather(block):
    return lax.all_gather(block, PLANE, axis=0, tiled=True)


def plane_scatter(partial):
    return lax.psum_scatter(partial.astype(BF), PLANE, scatter_dimension=0, tiled=True)


MESH = pl.DeviceIdType.MESH


class Wires:
    def __init__(self, send_sems, recv_sems):
        self.send_sems, self.recv_sems, self.used = send_sems, recv_sems, 0

    def far(self, src, dst, device):
        at = self.used
        self.used += 1
        return pltpu.make_async_remote_copy(
            src_ref=src,
            dst_ref=dst,
            send_sem=self.send_sems.at[at],
            recv_sem=self.recv_sems.at[at],
            device_id=device,
            device_id_type=MESH,
        )

    def near(self, src, dst):
        at = self.used
        self.used += 1
        return pltpu.make_async_copy(src, dst, self.send_sems.at[at])


def greet(devices):
    barrier = pltpu.get_barrier_semaphore()
    for device in devices:
        pl.semaphore_signal(barrier, inc=1, device_id=device, device_id_type=MESH)
    pl.semaphore_wait(barrier, len(devices))


def sides():
    x, l, y, c = tuple(lax.axis_index(name) for name in EVERY)
    x_a, y_a = x + (1 - c) * (1 - 2 * x), y + c * (1 - 2 * y)
    x_b, y_b = x + c * (1 - 2 * x), y + (1 - c) * (1 - 2 * y)
    return (x, l, y, c), (x, l, y, 1 - c), (x_a, l, y_a, c), (x_b, l, y_b, c)


def slot_of(device):
    return device[0] * 4 + device[2] * 2 + device[3]


def over_rows(length, rows, step):
    @pl.loop(0, length // rows)
    def _(i):
        step(pl.ds(pl.multiple_of(i * rows, rows), rows))


class PlaneSum:
    def __init__(self, wires, partial, own, got, hop_a, hop_b, cuts):
        self.own, self.got, self.hop_a, self.hop_b = own, got, hop_a, hop_b
        self.cuts, self.part = cuts, own.shape[1] // cuts
        me, core, side_a, side_b = sides()
        diag = (1 - me[0], me[1], 1 - me[2], me[3])
        self.chips = [me, side_a, side_b, diag]
        self.theirs = {0: 0, 1: 2, 2: 1, 3: 3}
        self.order = [3, 1, 2, 0]
        self.swaps, self.loads = {}, {}
        self.far_a, self.near_a, self.far_b = {}, {}, {}
        for piece in range(cuts):
            rows = pl.ds(piece * self.part, self.part)
            for rel in self.order:
                chip = self.chips[rel]
                away = slot_of((chip[0], chip[1], chip[2], 1 - me[3]))
                self.swaps[rel, piece] = wires.far(
                    partial.at[away, rows], got.at[self.theirs[rel], rows], core
                )
                self.loads[rel, piece] = wires.near(
                    partial.at[slot_of(chip), rows], own.at[rel, rows]
                )
            self.far_a[piece] = wires.far(own.at[3, rows], hop_a.at[0, rows], side_a)
            self.near_a[piece] = wires.far(own.at[1, rows], hop_a.at[1, rows], side_a)
            self.far_b[piece] = wires.far(own.at[2, rows], hop_b.at[rows], side_b)

    def start(self):
        for rel in self.order:
            for piece in range(self.cuts):
                self.swaps[rel, piece].start()
                self.loads[rel, piece].start()

    def landed(self, rel, piece):
        self.loads[rel, piece].wait()
        self.swaps[self.theirs[rel], piece].wait_recv()

    def join(self, rel, piece, hopped):
        @pl.loop(0, self.part // 16)
        def _(i):
            rows = pl.ds(pl.multiple_of(piece * self.part + i * 16, 16), 16)
            total = self.own[rel, rows].astype(F32) + self.got[rel, rows].astype(F32)
            if hopped:
                total = total + self.hop_a[0, rows].astype(F32)
            self.own[rel, rows] = total.astype(BF)

    def first_side(self):
        for rel, copies in ((3, self.far_a), (1, self.near_a)):
            for piece in range(self.cuts):
                self.landed(rel, piece)
                self.join(rel, piece, False)
                copies[piece].start()

    def second_side(self):
        for piece in range(self.cuts):
            self.landed(2, piece)
            self.far_a[piece].wait_recv()
            self.join(2, piece, True)
            self.far_b[piece].start()

    def finish(self, piece, use):
        self.landed(0, piece)
        self.near_a[piece].wait_recv()
        self.far_b[piece].wait_recv()

        @pl.loop(0, self.part // 16)
        def _(i):
            rows = pl.ds(pl.multiple_of(piece * self.part + i * 16, 16), 16)
            total = self.own[0, rows].astype(F32) + self.got[0, rows].astype(F32)
            total = total + self.hop_a[1, rows].astype(F32) + self.hop_b[rows].astype(F32)
            use(rows, total)

    def drain(self):
        for piece in range(self.cuts):
            for rel in self.order:
                self.swaps[rel, piece].wait_send()
            for copy in (self.far_a[piece], self.near_a[piece], self.far_b[piece]):
                copy.wait_send()


class LineSum:
    def __init__(self, wires, lines, own, from_left, from_right, root):
        x, l, y, c = (lax.axis_index(name) for name in EVERY)
        self.own, self.from_left, self.from_right = own, from_left, from_right
        self.l, self.root, self.lines = l, root, lines
        self.to_right = wires.far(own, from_left, (x, l + 1, y, c))
        self.to_left = wires.far(own, from_right, (x, l - 1, y, c))

    def add(self, other):
        @pl.loop(0, self.own.shape[0] // 16)
        def _(i):
            at = pl.ds(pl.multiple_of(i * 16, 16), 16)
            self.own[at] = (self.own[at].astype(F32) + other[at].astype(F32)).astype(BF)

    def begin(self):
        @pl.when(jnp.logical_and(self.l == 0, self.l < self.root))
        def _():
            self.to_right.start()

        @pl.when(jnp.logical_and(self.l == self.lines - 1, self.l > self.root))
        def _():
            self.to_left.start()

    def through(self):
        @pl.when(jnp.logical_and(self.l > 0, self.l < self.root))
        def _():
            self.to_right.wait_recv()
            self.add(self.from_left)
            self.to_right.start()

        @pl.when(jnp.logical_and(self.l < self.lines - 1, self.l > self.root))
        def _():
            self.to_left.wait_recv()
            self.add(self.from_right)
            self.to_left.start()

    def end(self):
        @pl.when(self.l == self.root)
        def _():
            @pl.when(self.l > 0)
            def _():
                self.to_right.wait_recv()
                self.add(self.from_left)

            @pl.when(self.l < self.lines - 1)
            def _():
                self.to_left.wait_recv()
                self.add(self.from_right)

    def drain(self):
        @pl.when(self.l < self.root)
        def _():
            self.to_right.wait_send()

        @pl.when(self.l > self.root)
        def _():
            self.to_left.wait_send()


def back_rows(base_ref, up_ref, gain_ref, out_ref, gain_out, mine):
    def use(rows, total):
        base = base_ref[rows].astype(F32)
        scale = lax.rsqrt(jnp.mean(base * base, axis=-1, keepdims=True) + EPSILON)
        lean = total * gain_ref[...]
        along = jnp.mean(lean * base, axis=-1, keepdims=True)
        grad = up_ref[rows].astype(F32) + scale * lean
        grad = grad - base * (scale * scale * scale * along)
        out_ref[rows] = grad
        if mine is not None:
            mine[rows] = grad.astype(BF)
        share = total * base * scale
        gain_out[...] += share[:8] + share[8:]

    return use


def forward_rows(base_ref, gain_ref, out_ref, mine):
    def use(rows, total):
        base = base_ref[rows].astype(F32) + total
        out_ref[rows] = base
        scale = lax.rsqrt(jnp.mean(base * base, axis=-1, keepdims=True) + EPSILON)
        mine[rows] = (base * scale * gain_ref[...]).astype(BF)

    return use


class PlaneGather:
    def __init__(self, wires, mine, everything, cuts):
        me, core, side_a, side_b = sides()
        diag = (1 - me[0], me[1], 1 - me[2], me[3])
        here, from_a, from_b, from_diag = [slot_of(at) for at in (me, side_a, side_b, diag)]
        self.cuts, self.copies = cuts, {}
        part = mine.shape[0] // cuts
        for piece in range(cuts):
            rows = pl.ds(piece * part, part)
            for name, src, slot, target in (
                ("a", mine.at[rows], here, side_a),
                ("b", mine.at[rows], here, side_b),
                ("c", mine.at[rows], here, core),
                ("ab", everything.at[from_a, rows], from_a, side_b),
                ("ac", everything.at[from_a, rows], from_a, core),
                ("bc", everything.at[from_b, rows], from_b, core),
                ("dc", everything.at[from_diag, rows], from_diag, core),
            ):
                self.copies[name, piece] = wires.far(src, everything.at[slot, rows], target)
            self.copies["own", piece] = wires.near(mine.at[rows], everything.at[here, rows])

    def start(self, piece):
        for name in ("a", "b", "c", "own"):
            self.copies[name, piece].start()

    def forward(self, came, goes):
        for piece in range(self.cuts):
            self.copies[came, piece].wait_recv()
            for name in goes:
                self.copies[name, piece].start()

    def finish(self):
        for piece in range(self.cuts):
            for name in ("c", "ac", "bc", "dc"):
                self.copies[name, piece].wait_recv()
            self.copies["own", piece].wait()
            for name in ("a", "b", "c", "ab", "ac", "bc", "dc"):
                self.copies[name, piece].wait_send()


def plane_kernel(mode, cuts, *refs):
    refs = list(refs)
    partial, base_ref = refs.pop(0), refs.pop(0)
    up_ref = refs.pop(0) if mode == "back" else None
    gain_ref, out_ref = refs.pop(0), refs.pop(0)
    gain_out = refs.pop(0) if mode == "back" else None
    all_ref, own, got, hop_a, hop_b, mine, send_sems, recv_sems = refs
    _, core, side_a, side_b = sides()
    wires = Wires(send_sems, recv_sems)
    greet([core, side_a, side_b])
    total = PlaneSum(wires, partial, own, got, hop_a, hop_b, cuts)
    spread = PlaneGather(wires, mine, all_ref, cuts)
    total.start()
    total.first_side()
    total.second_side()
    if mode == "back":
        gain_out[...] = jnp.zeros_like(gain_out)
        use = back_rows(base_ref, up_ref, gain_ref, out_ref, gain_out, mine)
    else:
        use = forward_rows(base_ref, gain_ref, out_ref, mine)
    for piece in range(cuts):
        total.finish(piece, use)
        spread.start(piece)
    spread.forward("a", ("ab", "ac"))
    spread.forward("b", ("bc",))
    spread.forward("ab", ("dc",))
    spread.finish()
    total.drain()


def sum_scratch(length, width):
    return [
        pltpu.VMEM((4, length, width), BF),
        pltpu.VMEM((4, length, width), BF),
        pltpu.VMEM((2, length, width), BF),
        pltpu.VMEM((length, width), BF),
    ]


def plane_sum(partial, base, up, gain, number):
    mode = "forward" if up is None else "back"
    length, width = base.shape
    cuts = 2
    vmem, left = pl.BlockSpec(memory_space=pltpu.VMEM), pl.BlockSpec(memory_space=pl.ANY)
    args, specs = [partial.reshape(8, length, width), base], [left, vmem]
    outs, out_specs = [jax.ShapeDtypeStruct((length, width), F32)], [vmem]
    if mode == "back":
        args.append(up)
        specs.append(vmem)
        outs.append(jax.ShapeDtypeStruct((8, width), F32))
        out_specs.append(vmem)
    args.append(gain.reshape(1, width))
    specs.append(vmem)
    outs.append(jax.ShapeDtypeStruct((8, length, width), BF))
    out_specs.append(left)
    sems = cuts * (8 + 3 + 8)
    got = list(
        pl.pallas_call(
            functools.partial(plane_kernel, mode, cuts),
            out_shape=outs,
            in_specs=specs,
            out_specs=out_specs,
            scratch_shapes=sum_scratch(length, width)
            + [
                pltpu.VMEM((length, width), BF),
                pltpu.SemaphoreType.DMA((sems,)),
                pltpu.SemaphoreType.DMA((sems,)),
            ],
            compiler_params=pltpu.CompilerParams(
                collective_id=number, has_side_effects=True, vmem_limit_bytes=40 << 20
            ),
            cost_estimate=pl.CostEstimate(
                flops=20 * base.size, bytes_accessed=400 * base.size, transcendentals=0
            ),
            name=f"plane_{mode}_{number}",
        )(*args)
    )
    got[-1] = got[-1].reshape(8 * length, width)
    return got


def tail_kernel(lines, cuts, *refs):
    (partial, base_ref, up_ref, gain_ref, other_gain, in_ref, chan_ref, upz, downz) = refs[:9]
    (out_ref, in_all, chan_out, up_all, down_all, gains) = refs[9:15]
    (own, got, hop_a, hop_b, gain_out, in_own, in_left, in_right) = refs[15:23]
    (chan_own, chan_left, chan_right, chan_got, tiny, tiny_line, send_sems, recv_sems) = refs[23:]
    me, core, side_a, side_b = sides()
    x, l, y, c = me
    k = 2 * y + c
    mates = [core, (x, l, 1 - y, c), (x, l, 1 - y, 1 - c)]
    twin = (1 - x, l, y, c)
    twins = [(1 - x, l, at[2], at[3]) for at in mates]
    wires = Wires(send_sems, recv_sems)
    others = [(x, lax.rem(l + d, lines), y, c) for d in range(1, lines)]
    greet(mates + [twin] + twins + others)

    total = PlaneSum(wires, partial, own, got, hop_a, hop_b, cuts)
    per = chan_ref.shape[0]
    owner = (4 * x + k) * per
    load_in = wires.near(in_ref, in_own)
    load_chan = wires.near(chan_ref, chan_own)
    in_sums = [
        LineSum(wires, lines, in_own.at[q], in_left.at[q], in_right.at[q], q)
        for q in range(lines)
    ]
    chan_roots = [(owner + i) // 4 for i in range(per)]
    chan_sums = [
        LineSum(wires, lines, chan_own.at[i], chan_left.at[i], chan_right.at[i], chan_roots[i])
        for i in range(per)
    ]

    def deliver(block, target):
        copies = [wires.near(block(k), target.at[x, k])]
        for at in [twin] + mates + twins:
            copies.append(wires.far(block(2 * at[2] + at[3]), target.at[x, k], at))
        return copies

    total.start()
    load_in.start()
    load_chan.start()
    up_copies = deliver(lambda to: upz.at[to], up_all)
    down_copies = [wires.near(downz, down_all.at[x]), wires.far(downz, down_all.at[x], twin)]
    load_in.wait()
    load_chan.wait()

    def pass_right(q):
        one = in_sums[q]

        @pl.when(jnp.logical_and(l > 0, l < q))
        def _():
            one.to_right.wait_recv()
            one.add(one.from_left)
            one.to_right.start()

    def pass_left(q):
        one = in_sums[q]

        @pl.when(jnp.logical_and(l < lines - 1, l > q))
        def _():
            one.to_left.wait_recv()
            one.add(one.from_right)
            one.to_left.start()

    def send_ends(q):
        @pl.when(jnp.logical_and(l == 0, q > 0))
        def _():
            in_sums[q].to_right.start()

        @pl.when(jnp.logical_and(l == lines - 1, q > 0))
        def _():
            in_sums[lines - 1 - q].to_left.start()

    send_ends(lines - 1)
    total.first_side()
    if lines > 2:
        send_ends(lines - 2)
    pass_right(lines - 1)
    pass_left(0)
    total.second_side()
    for q in reversed(range(1, lines - 2)):
        send_ends(q)
    for copy in down_copies + up_copies:
        copy.start()
    for q in reversed(range(1, lines - 1)):
        pass_right(q)
        pass_left(lines - 1 - q)
    for one in chan_sums:
        one.begin()
    gain_out[...] = jnp.zeros_like(gain_out)
    use = back_rows(base_ref, up_ref, gain_ref, out_ref, gain_out, None)
    for piece in range(cuts):
        total.finish(piece, use)
    for one in chan_sums:
        one.through()
    for q in range(lines):
        in_sums[q].end()
    rows = in_all.shape[2]
    in_copies = deliver(
        lambda to: in_own.at[l, pl.ds(pl.multiple_of(to * rows, rows), rows)], in_all
    )
    for copy in in_copies:
        copy.start()
    lane = lax.broadcasted_iota(jnp.int32, tiny.shape[1:], 0)
    first = jnp.sum(gain_out[...], axis=0, keepdims=True)
    second = jnp.sum(other_gain[...], axis=0, keepdims=True)
    tiny[0] = jnp.where(lane == 0, first, jnp.where(lane == 1, second, 0.0))
    for step, at in enumerate((core, twin, (x, l, 1 - y, c))):
        copy = wires.far(tiny.at[2 * step], tiny.at[2 * step + 1], at)
        copy.start()
        copy.wait()
        tiny[2 * step + 2] = tiny[2 * step] + tiny[2 * step + 1]
    line_copies = []
    for d, device in enumerate(others):
        line_copies.append(wires.far(tiny.at[6], tiny_line.at[l], device))
        line_copies[-1].start()
    tiny_line[l] = tiny[6]
    for one in chan_sums:
        one.end()
    goal = 4 * l + k
    holds = goal // (4 * per) == x
    chan_far, chan_near = [], []
    for i in range(per):
        s = owner + i
        mate = (x, l, lax.rem(s, 4) // 2, lax.rem(s, 2))
        far = wires.far(chan_own.at[i], chan_got, mate)
        near = wires.near(chan_own.at[i], chan_got)
        at_root = chan_roots[i] == l
        away = jnp.logical_and(at_root, lax.rem(s, 4) != k)
        stay = jnp.logical_and(at_root, lax.rem(s, 4) == k)
        chan_far.append((far, away))
        chan_near.append((near, stay))

        @pl.when(away)
        def _():
            far.start()

        @pl.when(stay)
        def _():
            near.start()
            near.wait()

    holder = lax.rem(goal // per, 4)
    for i in range(per):
        mine_here = jnp.logical_and(holds, lax.rem(goal, per) == i)

        @pl.when(jnp.logical_and(mine_here, holder != k))
        def _():
            chan_far[i][0].wait_recv()

    to_twin = wires.far(chan_got, chan_out, twin)
    keep = wires.near(chan_got, chan_out)

    @pl.when(holds)
    def _():
        to_twin.start()
        keep.start()
        keep.wait()

    @pl.when(jnp.logical_not(holds))
    def _():
        to_twin.wait_recv()

    for copy in line_copies:
        copy.wait()
    gains[...] = tiny_line[0]
    for q in range(1, lines):
        gains[...] += tiny_line[q]
    for copies in (in_copies, up_copies, down_copies):
        for copy in copies:
            copy.wait()

    @pl.when(holds)
    def _():
        to_twin.wait_send()

    for far, away in chan_far:

        @pl.when(away)
        def _():
            far.wait_send()

    for one in in_sums + chan_sums:
        one.drain()
    total.drain()


def tail(partial, base, up, gain, other_gain, in_grad, chan, upz, downz, lines):
    length, width = base.shape
    cuts = 2
    vmem, left = pl.BlockSpec(memory_space=pltpu.VMEM), pl.BlockSpec(memory_space=pl.ANY)
    rows = in_grad.shape[0] // (4 * lines)
    pieces = in_grad.reshape(lines, 4 * rows, in_grad.shape[1])
    per = chan.shape[0]
    sems = cuts * 11 + 2 + 2 * (lines + per) + 16 + 2 + 8 + 3 + lines + 2 * per + 4
    return pl.pallas_call(
        functools.partial(tail_kernel, lines, cuts),
        out_shape=[
            jax.ShapeDtypeStruct((length, width), F32),
            jax.ShapeDtypeStruct((2, 4, rows, in_grad.shape[1]), BF),
            jax.ShapeDtypeStruct(chan.shape[1:], BF),
            jax.ShapeDtypeStruct((2,) + upz.shape, BF),
            jax.ShapeDtypeStruct((2,) + downz.shape, BF),
            jax.ShapeDtypeStruct((8, width), F32),
        ],
        in_specs=[left, vmem, vmem, vmem, vmem, left, left, left, left],
        out_specs=[vmem, left, left, left, left, vmem],
        scratch_shapes=sum_scratch(length, width)
        + [pltpu.VMEM((8, width), F32)]
        + [pltpu.VMEM(pieces.shape, BF)] * 3
        + [pltpu.VMEM(chan.shape, BF)] * 3
        + [
            pltpu.VMEM(chan.shape[1:], BF),
            pltpu.VMEM((7, 8, width), F32),
            pltpu.VMEM((lines, 8, width), F32),
            pltpu.SemaphoreType.DMA((sems,)),
            pltpu.SemaphoreType.DMA((sems,)),
        ],
        compiler_params=pltpu.CompilerParams(
            collective_id=3, has_side_effects=True, vmem_limit_bytes=56 << 20
        ),
        cost_estimate=pl.CostEstimate(
            flops=20 * base.size, bytes_accessed=400 * base.size, transcendentals=0
        ),
        name="tail",
    )(partial.reshape(8, length, width), base, up, gain.reshape(1, width), other_gain, pieces, chan, upz, downz)


class LineGather:
    def __init__(self, wires, lines, blocks):
        x, l, y, c = (lax.axis_index(name) for name in EVERY)
        self.l, self.lines = l, lines
        self.right, self.left = [], []
        for d in range(lines - 1):
            block = blocks.at[jnp.maximum(l - d, 0)]
            self.right.append(wires.far(block, block, (x, l + 1, y, c)))
            block = blocks.at[jnp.minimum(l + d, lines - 1)]
            self.left.append(wires.far(block, block, (x, l - 1, y, c)))

    def step(self, d):
        l, last = self.l, self.lines - 1

        @pl.when(l >= d)
        def _():
            if d > 0:
                self.right[d - 1].wait_recv()
            if d < last:

                @pl.when(l < last)
                def _():
                    self.right[d].start()

        @pl.when(l + d <= last)
        def _():
            if d > 0:
                self.left[d - 1].wait_recv()
            if d < last:

                @pl.when(l > 0)
                def _():
                    self.left[d].start()

    def drain(self):
        l, last = self.l, self.lines - 1
        for d in range(last):

            @pl.when(jnp.logical_and(l >= d, l < last))
            def _():
                self.right[d].wait_send()

            @pl.when(jnp.logical_and(l + d <= last, l > 0))
            def _():
                self.left[d].wait_send()


class FromRoot:
    def __init__(self, wires, lines, source, target, i, per):
        x, l, y, c = (lax.axis_index(name) for name in EVERY)
        k = 2 * y + c
        s = 4 * l + k
        self.l, self.lines = l, lines
        wanted = (4 * x + k) * per + i
        self.root = wanted // 4
        mine = jnp.logical_and(s // (4 * per) == x, lax.rem(s, per) == i)
        goal = lax.rem(s // per, 4)
        self.leaves = jnp.logical_and(mine, goal != k)
        self.stays = jnp.logical_and(mine, goal == k)
        self.comes = jnp.logical_and(self.root == l, lax.rem(wanted, 4) != k)
        self.far = wires.far(source, target.at[i], (x, l, goal // 2, lax.rem(goal, 2)))
        self.near = wires.near(source, target.at[i])
        self.right = wires.far(target.at[i], target.at[i], (x, l + 1, y, c))
        self.left = wires.far(target.at[i], target.at[i], (x, l - 1, y, c))

    def start(self):
        @pl.when(self.leaves)
        def _():
            self.far.start()

        @pl.when(self.stays)
        def _():
            self.near.start()

    def onward(self):
        l, root, last = self.l, self.root, self.lines - 1

        @pl.when(jnp.logical_and(l >= root, l < last))
        def _():
            self.right.start()

        @pl.when(jnp.logical_and(l <= root, l > 0))
        def _():
            self.left.start()

    def from_owner(self):
        @pl.when(self.stays)
        def _():
            self.near.wait()

        @pl.when(self.comes)
        def _():
            self.far.wait_recv()

        @pl.when(self.l == self.root)
        def _():
            self.onward()

    def from_line(self):
        @pl.when(self.l > self.root)
        def _():
            self.right.wait_recv()
            self.onward()

        @pl.when(self.l < self.root)
        def _():
            self.left.wait_recv()
            self.onward()

    def drain(self):
        l, root, last = self.l, self.root, self.lines - 1

        @pl.when(self.leaves)
        def _():
            self.far.wait_send()

        @pl.when(jnp.logical_and(l >= root, l < last))
        def _():
            self.right.wait_send()

        @pl.when(jnp.logical_and(l <= root, l > 0))
        def _():
            self.left.wait_send()


def start_kernel(lines, cuts, *refs):
    (tok, mix, up, small, out, tiny) = refs[:6]
    (tok_all, halo, mix_all, up_all, small_all, out_all, tiny_all) = refs[6:13]
    send_sems, recv_sems = refs[13:]
    me, core, side_a, side_b = sides()
    x, l, y, c = me
    k = 2 * y + c
    other_y, cross, twin = (x, l, 1 - y, c), (x, l, 1 - y, 1 - c), (1 - x, l, y, c)
    mates = [core, other_y, cross]
    others = [(x, lax.rem(l + d, lines), y, c) for d in range(1, lines)]
    per = small_all.shape[0]
    wires = Wires(send_sems, recv_sems)
    greet(mates + [twin] + others)

    def exchange(source, target):
        copies = [wires.near(source.at[k], target.at[k])]
        for at in mates:
            copies.append(wires.far(source.at[2 * at[2] + at[3]], target.at[k], at))
        return copies

    mix_swap = exchange(mix, mix_all.at[l])
    up_swap = exchange(up, up_all)
    spread = PlaneGather(wires, tok, tok_all, cuts)
    walk = LineGather(wires, lines, mix_all)
    roots = []
    for i in range(per):
        roots.append(FromRoot(wires, lines, small, small_all, i, per))
        roots.append(FromRoot(wires, lines, out, out_all, i, per))
    tiny_own = wires.near(tiny, tiny_all.at[x, c, y, l])
    tiny_line = [wires.far(tiny, tiny_all.at[x, c, y, l], at) for at in others]
    tiny_steps = [
        wires.far(tiny_all.at[x, c, y], tiny_all.at[x, c, y], other_y),
        wires.far(tiny_all.at[x, c], tiny_all.at[x, c], core),
        wires.far(tiny_all.at[x], tiny_all.at[x], twin),
    ]
    length = tok.shape[0]
    edge = pl.ds(length - 8, 8)
    halo_far = [
        wires.far(tok_all.at[4 * run + 3, edge], halo.at[run], (x, l + 1, y, c))
        for run in range(2)
    ]
    halo_near = [wires.near(tok.at[edge], halo.at[run]) for run in range(2)]

    for copy in mix_swap + [tiny_own] + tiny_line:
        copy.start()
    for piece in range(cuts):
        spread.start(piece)
    for one in roots:
        one.start()
    for copy in up_swap:
        copy.start()
    for copy in mix_swap:
        copy.wait()
    walk.step(0)
    for one in roots[:2]:
        one.from_owner()
    for copy in [tiny_own] + tiny_line:
        copy.wait()
    for copy in tiny_steps[:2]:
        copy.start()
        copy.wait()
    walk.step(1)
    for one in roots[2:]:
        one.from_owner()
    tiny_steps[2].start()
    tiny_steps[2].wait()
    for d in range(2, lines - 1):
        walk.step(d)
    spread.forward("a", ("ab", "ac"))
    for one in roots[:2]:
        one.from_line()
    if lines > 2:
        walk.step(lines - 1)
    spread.forward("b", ("bc",))
    for one in roots[2:]:
        one.from_line()
    spread.forward("ab", ("dc",))
    spread.finish()

    @pl.when(l < lines - 1)
    def _():
        for copy in halo_far:
            copy.start()

    @pl.when(l == 0)
    def _():
        for copy in halo_near:
            copy.start()
            copy.wait()

    for copy in up_swap:
        copy.wait()

    @pl.when(l > 0)
    def _():
        for copy in halo_far:
            copy.wait_recv()

    @pl.when(l < lines - 1)
    def _():
        for copy in halo_far:
            copy.wait_send()

    walk.drain()
    for one in roots:
        one.drain()


def spread_inputs(tok, mix, up, small, out, tiny, lines, per):
    length, width = tok.shape
    cuts = 2
    vmem, left = pl.BlockSpec(memory_space=pltpu.VMEM), pl.BlockSpec(memory_space=pl.ANY)
    sems = 8 + cuts * 8 + 2 * lines + 2 * per * 4 + lines + 1 + 3 + 4
    return pl.pallas_call(
        functools.partial(start_kernel, lines, cuts),
        out_shape=[
            jax.ShapeDtypeStruct((8, length, width), BF),
            jax.ShapeDtypeStruct((2, 8, width), BF),
            jax.ShapeDtypeStruct((lines,) + mix.shape, BF),
            jax.ShapeDtypeStruct(up.shape, BF),
            jax.ShapeDtypeStruct((per,) + small.shape, BF),
            jax.ShapeDtypeStruct((per,) + out.shape, BF),
            jax.ShapeDtypeStruct((2, 2, 2, lines) + tiny.shape, F32),
        ],
        in_specs=[left] * 5 + [vmem],
        out_specs=[left] * 6 + [vmem],
        scratch_shapes=[
            pltpu.SemaphoreType.DMA((sems,)),
            pltpu.SemaphoreType.DMA((sems,)),
        ],
        compiler_params=pltpu.CompilerParams(
            collective_id=4, has_side_effects=True, vmem_limit_bytes=16 << 20
        ),
        cost_estimate=pl.CostEstimate(
            flops=20 * tok.size, bytes_accessed=400 * tok.size, transcendentals=0
        ),
        name="spread",
    )(tok, mix, up, small, out, tiny)


def gelu_parts(value):
    slope = 0.7978845608028654
    bend = jnp.tanh(slope * (value + 0.044715 * value * value * value))
    gelu = 0.5 * value * (1.0 + bend)
    inner = slope * (1.0 + 0.134145 * value * value)
    return gelu, 0.5 * (1.0 + bend) + 0.5 * value * (1.0 - bend * bend) * inner


def recur_parts(conv_out, chan, gate_ref, keep):
    pre = jnp.dot(conv_out, gate_ref[...], preferred_element_type=F32) + chan[5:6]
    recur = jax.nn.sigmoid(pre)
    log_decay = chan[7:8] * recur
    decayed = jnp.exp(log_decay)
    twice = -2.0 * log_decay
    return recur, decayed, decayed * keep, twice


def below_one(decayed, twice):
    series = 1.0 / 5040.0
    for term in (-1.0 / 720.0, 1.0 / 120.0, -1.0 / 24.0, 1.0 / 6.0, -0.5, 1.0):
        series = series * twice + term
    return jnp.where(twice < 0.5, twice * series, 1.0 - decayed * decayed)


def scan_tiles(rows, backward, first, second, out_first, out_second, carry):
    channels = first.shape[-1]
    where = lax.broadcasted_iota(jnp.int32, (8, channels), 0)
    tiles = rows // 8

    def step(i, state):
        before_a, before_b = state
        tile = tiles - 1 - i if backward else i
        at = pl.ds(pl.multiple_of(tile * 8, 8), 8)
        a, b = first[at], second[at]
        for gap in (1, 2, 4):
            turn = 8 - gap if backward else gap
            inside = where < 8 - gap if backward else where >= gap
            near_a = jnp.where(inside, pltpu.roll(a, turn, 0), 1.0)
            near_b = jnp.where(inside, pltpu.roll(b, turn, 0), 0.0)
            b = b + a * near_b
            a = a * near_a
        b = b + a * before_b
        a = a * before_a
        out_first[at] = a
        out_second[at] = b
        last = 0 if backward else 7
        return (
            jnp.broadcast_to(a[last : last + 1], a.shape),
            jnp.broadcast_to(b[last : last + 1], b.shape),
        )

    end = lax.fori_loop(0, tiles, step, (carry[0], carry[1]), unroll=4)
    carry[0] = end[0]
    carry[1] = end[1]


def mix_forward_kernel(*refs):
    (tok, halo, weight, gain, chan_ref, gate_r, gate_i, fac) = refs[:8]
    (normed, branch, conv_in, conv_out, pa, pb, ends) = refs[8:15]
    (rows_in, coef, drive, carry) = refs[15:]
    length, own = branch.shape
    chunk = pl.program_id(1)
    chan = chan_ref[...]

    def norm_of(values):
        values = values.astype(F32)
        scale = lax.rsqrt(jnp.mean(values * values, axis=-1, keepdims=True) + EPSILON)
        return (values * scale * gain[...]).astype(BF)

    @pl.when(chunk == 0)
    def _():
        carry[0] = jnp.ones_like(carry[0])
        carry[1] = jnp.zeros_like(carry[1])
        edge = jnp.dot(norm_of(halo[0]), weight[...], preferred_element_type=F32)
        rows_in[8:16] = pltpu.roll(edge, own, 1)[:, :own].astype(BF).astype(F32)
        rows_in[0:8] = jnp.zeros((8, own), F32)
        conv_in[0, 0:16] = rows_in[0:16].astype(BF)

    @pl.when(chunk > 0)
    def _():
        rows_in[0:16] = rows_in[length : length + 16]

    @pl.loop(0, length // 16)
    def _(i):
        at = pl.ds(pl.multiple_of(i * 16, 16), 16)
        normed[0, at] = norm_of(tok[0, at])

    projected = jnp.dot(normed[0], weight[...], preferred_element_type=F32)
    branch[...] = projected[:, :own]
    rounded = pltpu.roll(projected, own, 1)[:, :own].astype(BF)
    conv_in[0, pl.ds(pl.multiple_of(16 + chunk * length, 16), length)] = rounded
    rows_in[16 : 16 + length] = rounded.astype(F32)
    window = rows_in[8 : 16 + length]
    total = chan[4:5] + chan[0:1] * window[8:]
    for gap in range(1, 4):
        total = total + chan[gap : gap + 1] * pltpu.roll(window, gap, 0)[8:] * fac[:, gap - 1 : gap]
    low = total.astype(BF)
    conv_out[...] = low
    keep = fac[:, 0:1]
    _, decayed, coefficient, twice = recur_parts(low, chan, gate_r, keep)
    coef[...] = coefficient
    input_gate = jax.nn.sigmoid(
        jnp.dot(low, gate_i[...], preferred_element_type=F32) + chan[6:7]
    )
    scaling = jnp.where(keep == 0.0, 1.0, jnp.sqrt(below_one(decayed, twice)))
    drive[...] = scaling * input_gate * low.astype(F32)
    scan_tiles(length, False, coef, drive, pa, pb, carry)
    ends[0, 0:8] = carry[0]
    ends[0, 8:16] = carry[1]


def mix_state_kernel(*refs):
    (res, weight, branch, pa, pb, state_in, conv_out, chan_ref, gate_r, fac) = refs[:10]
    (branch_grad, ta, tb, ends) = refs[10:14]
    (coef, grad, carry, first_coef) = refs[14:]
    length, own = branch.shape
    chan = chan_ref[...]
    turn = pl.program_id(1)

    @pl.when(turn == 0)
    def _():
        carry[0] = jnp.ones_like(carry[0])
        carry[1] = jnp.zeros_like(carry[1])
        first_coef[...] = jnp.ones_like(first_coef)

    mixed_grad = lax.dot_general(
        res[...], weight[...], (((1,), (1,)), ((), ())), preferred_element_type=F32
    )
    state = pb[...] + pa[...] * state_in[0, 0:1]
    gelu, slope = gelu_parts(branch[...])
    branch_grad[...] = (mixed_grad * state * slope).astype(BF)
    grad[...] = mixed_grad * gelu
    _, _, coefficient, _ = recur_parts(conv_out[...], chan, gate_r, fac[:, 0:1])
    row = lax.broadcasted_iota(jnp.int32, (length, own), 0)
    shifted = pltpu.roll(coefficient, length - 1, 0)
    coef[...] = jnp.where(row == length - 1, first_coef[0:1], shifted)
    first = jnp.broadcast_to(coefficient[0:1], first_coef.shape)
    first_coef[...] = first
    scan_tiles(length, True, coef, grad, ta, tb, carry)
    ends[0, 0:8] = first * carry[0]
    ends[0, 8:16] = first * carry[1]


def mix_gates_kernel(*refs):
    (ta, tb, from_right, pa, pb, pa_before, pb_before, state_in) = refs[:8]
    (conv_in, conv_out, branch_grad, chan_ref, gate_r, gate_i, fac) = refs[8:15]
    (proj_grad, last_rows, edges, sums, gate_grad) = refs[15:20]
    (after,) = refs[20:]
    length, own = ta.shape
    turn, turns = pl.program_id(1), pl.num_programs(1)
    chunk = turns - 1 - turn
    chan = chan_ref[...]

    @pl.when(jnp.logical_and(turn == 0, pl.program_id(0) == 0))
    def _():
        sums[...] = jnp.zeros_like(sums)
        gate_grad[...] = jnp.zeros_like(gate_grad)

    @pl.when(turn == 0)
    def _():
        after[...] = jnp.zeros_like(after)

    start = state_in[0, 0:1]
    total = tb[...] + ta[...] * from_right[0, 0:1]
    state = pb[...] + pa[...] * start
    row = lax.broadcasted_iota(jnp.int32, (length, own), 0)
    before = pb_before[7:8] + pa_before[7:8] * start
    before = jnp.where(chunk == 0, start, before)
    prev_state = jnp.where(row == 0, before, pltpu.roll(state, 1, 0))
    keep = fac[:, 0:1]
    low = conv_out[...]
    conv = low.astype(F32)
    recur, decayed, coefficient, twice = recur_parts(low, chan, gate_r, keep)
    input_gate = jax.nn.sigmoid(
        jnp.dot(low, gate_i[...], preferred_element_type=F32) + chan[6:7]
    )
    rest = below_one(decayed, twice)
    fresh = keep == 0.0
    scaling = jnp.where(fresh, 1.0, jnp.sqrt(rest))
    gated = total * input_gate
    by_scaling = jnp.where(fresh, 0.0, gated * conv * decayed * decayed * lax.rsqrt(rest))
    decay_grad = total * prev_state * coefficient - by_scaling
    recur_grad = (chan[7:8] * decay_grad * recur * (1.0 - recur)).astype(BF)
    input_grad = (total * scaling * conv * input_gate * (1.0 - input_gate)).astype(BF)

    def fold(values):
        return jnp.sum(values.reshape(length // 8, 8, own), axis=0)

    sums[5] += fold(recur_grad.astype(F32))
    sums[6] += fold(input_grad.astype(F32))
    sums[7] += fold(decay_grad * recur)
    contract = (((0,), (0,)), ((), ()))
    gate_grad[0] += lax.dot_general(low, recur_grad, contract, preferred_element_type=F32)
    gate_grad[1] += lax.dot_general(low, input_grad, contract, preferred_element_type=F32)
    across = (((1,), (1,)), ((), ()))
    conv_grad = gated * scaling
    conv_grad = conv_grad + lax.dot_general(
        recur_grad, gate_r[...], across, preferred_element_type=F32
    )
    conv_grad = conv_grad + lax.dot_general(
        input_grad, gate_i[...], across, preferred_element_type=F32
    )
    window = conv_in[0, pl.ds(pl.multiple_of(chunk * length, 16), length + 16)].astype(F32)[8:]
    sums[4] += fold(conv_grad)
    sums[0] += fold(conv_grad * window[8:])
    conv_in_grad = chan[0:1] * conv_grad
    edge_row = lax.broadcasted_iota(jnp.int32, (8, own), 0)
    edge = jnp.zeros((8, own), F32)
    for gap in range(1, 4):
        masked = conv_grad * fac[:, gap - 1 : gap]
        sums[gap] += fold(masked * pltpu.roll(window, gap, 0)[8:])
        moved = pltpu.roll(jnp.concatenate([masked, after[gap - 1]], axis=0), length + 8 - gap, 0)
        conv_in_grad = conv_in_grad + chan[gap : gap + 1] * moved[:length]
        head = masked[0:8]
        after[gap - 1] = head
        given = pltpu.roll(head, 3 - gap, 0)
        given = jnp.where((edge_row >= 3 - gap) & (edge_row < 3), given, 0.0)
        edge = edge + chan[gap : gap + 1] * given
    edges[0] = edge

    @pl.when(turn == 0)
    def _():
        last_rows[0] = conv_in_grad[length - 8 :]

    proj_grad[:, :own] = branch_grad[...]
    proj_grad[:, own:] = conv_in_grad.astype(BF)


def line_kernel(lines, backward, ends, start, got, send_sems, recv_sems):
    x, l, y, c = (lax.axis_index(name) for name in EVERY)
    wires = Wires(send_sems, recv_sems)
    others = [(x, lax.rem(l + d, lines), y, c) for d in range(1, lines)]
    greet(others)
    copies = [wires.far(ends, got.at[l], at) for at in others]
    for copy in copies:
        copy.start()
    for copy in copies:
        copy.wait()
    for run in range(2):
        value = jnp.zeros(start.shape[1:], F32)
        order = reversed(range(1, lines)) if backward else range(lines - 1)
        for other in order:
            longer = got[other, run, 0:8] * value + got[other, run, 8:16]
            reached = other > l if backward else other < l
            value = jnp.where(reached, longer, value)
        start[run] = value


def line_start(ends, lines, backward, number):
    vmem = pl.BlockSpec(memory_space=pltpu.VMEM)
    own = ends.shape[-1]
    return pl.pallas_call(
        functools.partial(line_kernel, lines, backward),
        out_shape=jax.ShapeDtypeStruct((2, 8, own), F32),
        in_specs=[vmem],
        out_specs=vmem,
        scratch_shapes=[
            pltpu.VMEM((lines,) + ends.shape, F32),
            pltpu.SemaphoreType.DMA((lines,)),
            pltpu.SemaphoreType.DMA((lines,)),
        ],
        compiler_params=pltpu.CompilerParams(
            collective_id=number, has_side_effects=True, vmem_limit_bytes=8 << 20
        ),
        name=f"line_{number}",
    )(ends)


def mix_specs(run, length, own, backward):
    steps = run // length

    def turn(j):
        return steps - 1 - j if backward else j

    def rows(width):
        return pl.BlockSpec((length, width), lambda i, j: (i * steps + turn(j), 0))

    def slots(width):
        return pl.BlockSpec((1, length, width), lambda i, j: (i * steps + turn(j), 0, 0))

    def whole(*shape):
        return pl.BlockSpec(shape, lambda i, j: (0,) * len(shape), pipeline_mode=pl.Buffered(1))

    def held(*shape):
        return pl.BlockSpec((1,) + shape, lambda i, j: (i,) + (0,) * len(shape))

    return steps, rows, slots, whole, held


def mix_forward(tok_all, halo, weight, gain, chan, gate_r, gate_i, fac):
    slots_in, length, width = tok_all.shape
    own, run = chan.shape[1], 4 * length
    steps, rows, slots, whole, held = mix_specs(run, length, own, False)
    flat = jax.ShapeDtypeStruct((2 * run, own), F32)
    return pl.pallas_call(
        mix_forward_kernel,
        grid=(2, steps),
        in_specs=[
            slots(width),
            held(8, width),
            whole(width, 2 * own),
            whole(1, width),
            whole(8, own),
            whole(own, own),
            whole(own, own),
            rows(fac.shape[1]),
        ],
        out_specs=[
            slots(width),
            rows(own),
            held(16 + run, own),
            rows(own),
            rows(own),
            rows(own),
            held(16, own),
        ],
        out_shape=[
            jax.ShapeDtypeStruct(tok_all.shape, BF),
            flat,
            jax.ShapeDtypeStruct((2, 16 + run, own), BF),
            jax.ShapeDtypeStruct((2 * run, own), BF),
            flat,
            flat,
            jax.ShapeDtypeStruct((2, 16, own), F32),
        ],
        scratch_shapes=[
            pltpu.VMEM((16 + length, own), F32),
            pltpu.VMEM((length, own), F32),
            pltpu.VMEM((length, own), F32),
            pltpu.VMEM((2, 8, own), F32),
        ],
        compiler_params=pltpu.CompilerParams(vmem_limit_bytes=40 << 20),
        cost_estimate=pl.CostEstimate(
            flops=4 * run * width * 2 * own, bytes_accessed=60 << 20, transcendentals=0
        ),
        name="mix_forward",
    )(tok_all, halo, weight, gain.reshape(1, width), chan, gate_r, gate_i, fac)


def mix_state(res, weight, branch, pa, pb, state_in, conv_out, chan, gate_r, fac, length):
    own, width = weight.shape
    run = res.shape[0] // 2
    steps, rows, slots, whole, held = mix_specs(run, length, own, True)
    flat = jax.ShapeDtypeStruct((2 * run, own), F32)
    return pl.pallas_call(
        mix_state_kernel,
        grid=(2, steps),
        in_specs=[
            rows(width),
            whole(own, width),
            rows(own),
            rows(own),
            rows(own),
            held(8, own),
            rows(own),
            whole(8, own),
            whole(own, own),
            rows(fac.shape[1]),
        ],
        out_specs=[rows(own), rows(own), rows(own), held(16, own)],
        out_shape=[
            jax.ShapeDtypeStruct((2 * run, own), BF),
            flat,
            flat,
            jax.ShapeDtypeStruct((2, 16, own), F32),
        ],
        scratch_shapes=[
            pltpu.VMEM((length, own), F32),
            pltpu.VMEM((length, own), F32),
            pltpu.VMEM((2, 8, own), F32),
            pltpu.VMEM((8, own), F32),
        ],
        compiler_params=pltpu.CompilerParams(vmem_limit_bytes=40 << 20),
        cost_estimate=pl.CostEstimate(
            flops=4 * run * width * own, bytes_accessed=40 << 20, transcendentals=0
        ),
        name="mix_state",
    )(res, weight, branch, pa, pb, state_in, conv_out, chan, gate_r, fac)


def mix_gates(
    ta, tb, from_right, pa, pb, state_in, conv_in, conv_out, branch_grad, chan, gate_r, gate_i, fac, length
):
    own = chan.shape[1]
    run = ta.shape[0] // 2
    steps, rows, slots, whole, held = mix_specs(run, length, own, True)
    eights = length // 8
    earlier = pl.BlockSpec(
        (8, own), lambda i, j: (jnp.maximum((i * steps + steps - 1 - j) * eights - 1, 0), 0)
    )
    return pl.pallas_call(
        mix_gates_kernel,
        grid=(2, steps),
        in_specs=[
            rows(own),
            rows(own),
            held(8, own),
            rows(own),
            rows(own),
            earlier,
            earlier,
            held(8, own),
            held(16 + run, own),
            rows(own),
            rows(own),
            whole(8, own),
            whole(own, own),
            whole(own, own),
            rows(fac.shape[1]),
        ],
        out_specs=[
            rows(2 * own),
            held(8, own),
            held(8, own),
            pl.BlockSpec((8, 8, own), lambda i, j: (0, 0, 0)),
            pl.BlockSpec((2, own, own), lambda i, j: (0, 0, 0)),
        ],
        out_shape=[
            jax.ShapeDtypeStruct((2 * run, 2 * own), BF),
            jax.ShapeDtypeStruct((2, 8, own), F32),
            jax.ShapeDtypeStruct((2, 8, own), F32),
            jax.ShapeDtypeStruct((8, 8, own), F32),
            jax.ShapeDtypeStruct((2, own, own), F32),
        ],
        scratch_shapes=[pltpu.VMEM((3, 8, own), F32)],
        compiler_params=pltpu.CompilerParams(vmem_limit_bytes=40 << 20),
        cost_estimate=pl.CostEstimate(
            flops=16 * run * own * own, bytes_accessed=40 << 20, transcendentals=0
        ),
        name="mix_gates",
    )(ta, tb, from_right, pa, pb, pa, pb, state_in, conv_in, conv_out, branch_grad, chan, gate_r, gate_i, fac)


def settle_kernel(lines, up_all, in_all, down_all, chan, up_out, in_out, down_out, out_out):
    share = up_all.shape[-1] // (2 * lines)
    own = in_all.shape[-1] // 2
    ups = [[up_all[x, k].astype(F32) for k in range(4)] for x in range(2)]
    for part in range(2 * lines):
        at = slice(part * share, (part + 1) * share)
        row = [ups[x][k][:, at] for k in range(4) for x in range(2)]
        up_out[:, part * 8 * share : (part + 1) * 8 * share] = jnp.concatenate(row, axis=1)
    for part in range(2):
        at = slice(part * own, (part + 1) * own)
        row = [in_all[x, k].astype(F32)[:, at] for x in range(2) for k in range(4)]
        in_out[:, part * 8 * own : (part + 1) * 8 * own] = jnp.concatenate(row, axis=1)
    down_out[...] = down_all[...].astype(F32)
    out_out[...] = chan[:, : out_out.shape[1]].astype(F32)


def settle(up_all, in_all, down_all, chan, owned, width, lines):
    rows, share2 = up_all.shape[2], down_all.shape[0]
    steps = 4 if not (rows % 64 or share2 % 64 or owned % 32) else 1
    r, d, o = rows // steps, share2 // steps, owned // steps
    wide, narrow = up_all.shape[-1], in_all.shape[-1]
    shapes = [(rows, 8 * wide), (rows, 8 * narrow), (share2, width), (owned, width)]
    return pl.pallas_call(
        functools.partial(settle_kernel, lines),
        grid=(steps,),
        in_specs=[
            pl.BlockSpec((2, 4, r, wide), lambda i: (0, 0, i, 0)),
            pl.BlockSpec((2, 4, r, narrow), lambda i: (0, 0, i, 0)),
            pl.BlockSpec((d, width), lambda i: (i, 0)),
            pl.BlockSpec((o, chan.shape[1]), lambda i: (i, 0)),
        ],
        out_specs=[
            pl.BlockSpec((n // steps, w), lambda i: (i, 0)) for n, w in shapes
        ],
        out_shape=[jax.ShapeDtypeStruct(one, F32) for one in shapes],
        compiler_params=pltpu.CompilerParams(vmem_limit_bytes=40 << 20),
        cost_estimate=pl.CostEstimate(
            flops=0, bytes_accessed=6 * sum(a * b for a, b in shapes), transcendentals=0
        ),
        name="settle",
    )(up_all, in_all, down_all, chan[:owned])


def on_device(
    tokens,
    seg_ids,
    mix_gain,
    mix_in,
    conv_par,
    gate_w,
    gate_bias,
    decay,
    out_proj,
    mlp_gain,
    mlp_in,
    mlp_out,
    cotangent,
):
    lines = lax.axis_size("l")
    owners = 4 * lines
    half, line = lax.axis_index("x"), lax.axis_index("l")
    quarter = 2 * lax.axis_index("y") + lax.axis_index("c")
    mine = 4 * half + quarter
    me = 4 * line + quarter
    length, width = tokens.shape
    channels = owners * decay.shape[0]
    block_size = channels // NBLK
    own = channels // 8
    blocks = NBLK // 8
    ff = owners * mlp_out.shape[0]
    run = 4 * length
    plane = 8 * length
    share = mlp_out.shape[0] // 2
    rows = mix_in.shape[0]

    per = owners // 8
    by_half = mix_in.reshape(rows, 2, 2, 4, own)
    by_half = lax.dynamic_index_in_dim(by_half, half, 2, keepdims=False)
    mix_sent = jnp.moveaxis(by_half, 2, 0).reshape(4, rows, 2 * own)
    by_half = mlp_in.reshape(rows, 2 * lines, 4, 2, share)
    by_half = lax.dynamic_index_in_dim(by_half, half, 3, keepdims=False)
    up_sent = jnp.moveaxis(by_half, 2, 0).reshape(4, rows, 2 * lines * share)
    small = jnp.concatenate([conv_par.T, gate_bias.T, decay[:, None], gate_w], axis=1)
    used = small.shape[1]
    small = jnp.pad(small, ((0, 0), (0, -used % 128)))
    tiny = jnp.concatenate([mix_gain.astype(F32), mlp_gain.astype(F32), seg_ids.astype(F32)])
    tiny = jnp.pad(tiny, (0, -tiny.shape[0] % 1024)).reshape(-1, 128)
    tok_all, halo, in_matrix, up_rows, packed, out_matrix, tiny = spread_inputs(
        tokens, mix_sent, up_sent, small, out_proj, tiny, lines, per
    )
    all_cot = plane_gather(cotangent)
    tok_all, all_cot = lax.optimization_barrier((tok_all, all_cot))
    in_matrix = in_matrix.reshape(-1, 2 * own)
    out_matrix = out_matrix.reshape(own, width)
    packed = packed.reshape(own, -1)
    tiny = tiny.transpose(0, 3, 2, 1, 4, 5).reshape(2, owners, -1)
    gain_one = tiny[0, :, :rows].reshape(-1)
    gain_two = tiny[0, :, rows : 2 * rows].reshape(-1)
    ids_all = tiny[:, :, 2 * rows : 2 * rows + length].reshape(2, lines, run).astype(jnp.int32)
    decay_own = packed[:, 7].astype(F32)
    chan = packed[:, :8].T.astype(F32)
    chan = chan.at[7].set(-DECAY_RATE * jax.nn.softplus(-decay_own))
    gates = packed[:, 8:used].reshape(blocks, block_size, 2, block_size)
    gate_r, gate_i = (
        lax.dynamic_update_slice(
            jnp.pad(gates[0, :, side], ((0, own - block_size), (0, own - block_size))),
            gates[1, :, side],
            (block_size, block_size),
        )
        for side in range(2)
    )

    ids = lax.dynamic_index_in_dim(ids_all, line, 1, keepdims=False)
    ids_before = lax.dynamic_index_in_dim(
        ids_all, jnp.maximum(line - 1, 0), 1, keepdims=False
    )[:, -3:]
    extended = jnp.concatenate([ids_before, ids], axis=1)
    places = (line * run + lax.broadcasted_iota(jnp.int32, (2, run), 1)) % SEQ_LEN
    fresh = (extended[:, 3:] != extended[:, 2:-1]) | (places == 0)
    keep = 1.0 - fresh.astype(F32)
    same = jnp.concatenate(
        [(extended[:, 1:3] == extended[:, 0:2]).astype(F32), keep], axis=1
    )
    fac = [keep]
    for offset in range(2, 4):
        fac.append(fac[-1] * same[:, 3 - offset : 3 - offset + run])
    fac = jnp.stack(fac + [keep], axis=-1).reshape(plane, 4)
    all_one, branch, conv_in, conv_out, pa, pb, ends = mix_forward(
        tok_all, halo, in_matrix, gain_one, chan, gate_r, gate_i, fac
    )
    all_one = all_one.reshape(plane, width)
    state_in = line_start(ends, lines, False, 5)
    up_rows = up_rows.reshape(4 * rows, 2, -1)
    first_up = lax.all_gather(up_rows[:, 0], "l", axis=0, tiled=True)
    later, down_rows, state_in = lax.optimization_barrier((up_rows[:, 1], mlp_out, state_in))
    second_up = lax.all_gather(later, "l", axis=0, tiled=True)
    down_matrix = lax.all_gather(
        lax.dynamic_slice_in_dim(down_rows, half * share, share, 0), "l", axis=0, tiled=True
    )
    state = pb.reshape(2, run, own) + pa.reshape(2, run, own) * state_in[:, :1]
    mixed = (state * jax.nn.gelu(branch.reshape(2, run, own))).astype(BF).reshape(plane, own)
    partial = jnp.dot(mixed, out_matrix, preferred_element_type=F32).astype(BF)
    residual, all_two = plane_sum(partial, tokens, None, gain_two, 1)
    gate_part = jnp.dot(all_two, first_up, preferred_element_type=F32)
    up_part = jnp.dot(all_two, second_up, preferred_element_type=F32)
    activated = gated_product(gate_part, up_part).astype(BF)
    out_partial = jnp.dot(activated, down_matrix, preferred_element_type=F32).astype(BF)
    out_partial, all_cot = lax.optimization_barrier((out_partial, all_cot))
    out_sum = plane_scatter(out_partial)

    act_grad = times_transposed(all_cot, down_matrix)
    _, act_pull = jax.vjp(gated_product, gate_part, up_part)
    gate_back, up_back = (one.astype(BF) for one in act_pull(act_grad))
    partial = times_transposed(gate_back, first_up) + times_transposed(up_back, second_up)
    partial = partial.astype(BF)
    down_grad = contract_rows(activated, all_cot).astype(BF)
    hidden_grad = jnp.concatenate([gate_back, up_back], axis=1)
    up_grad = contract_rows(all_two, hidden_grad).astype(BF)
    partial, down_grad, up_grad, out_sum = lax.optimization_barrier(
        (partial, down_grad, up_grad, out_sum)
    )
    output = (residual + out_sum.astype(F32)).astype(BF)
    down_line = lax.psum_scatter(down_grad, "l", scatter_dimension=0, tiled=True)
    up_line = lax.psum_scatter(up_grad, "l", scatter_dimension=0, tiled=True)
    residual_grad, gain_two_grad, all_res = plane_sum(partial, residual, cotangent, gain_two, 2)
    out_grad = contract_rows(mixed, all_res)
    branch_grad, ta, tb, ends = mix_state(
        all_res, out_matrix, branch, pa, pb, state_in, conv_out, chan, gate_r, fac, length
    )
    from_right = line_start(ends, lines, True, 6)
    proj_grad, last_rows, edges, sums, gate_grad = mix_gates(
        ta, tb, from_right, pa, pb, state_in, conv_in, conv_out, branch_grad, chan, gate_r, gate_i, fac, length
    )
    edges = lax.ppermute(edges, "l", [(i + 1, i) for i in range(lines - 1)])
    last_rows = last_rows + jnp.pad(edges[:, :3], ((0, 0), (5, 0), (0, 0)))
    for one in range(2):
        proj_grad = lax.dynamic_update_slice(
            proj_grad, last_rows[one].astype(BF), ((one + 1) * run - 8, own)
        )
    sums = jnp.sum(sums, axis=1)
    sums = sums.at[7].multiply(DECAY_RATE * jax.nn.sigmoid(-decay_own))
    gate_grad = jnp.stack(
        [
            gate_grad[:, b * block_size : (b + 1) * block_size, b * block_size : (b + 1) * block_size]
            for b in range(blocks)
        ]
    )
    gate_grad = gate_grad.transpose(0, 2, 1, 3).reshape(own, 2 * block_size)
    partial = times_transposed(proj_grad, in_matrix).astype(BF)
    in_grad = contract_rows(all_one, proj_grad).astype(BF)
    owned = channels // owners
    chan = jnp.concatenate(
        [out_grad, sums.T, gate_grad], axis=1
    ).astype(BF)
    used = chan.shape[1]
    chan = jnp.pad(
        chan.reshape(own // owned, owned, used), ((0, 0), (0, -owned % 16), (0, -used % 128))
    )
    input_grad, in_all, chan, up_all, down_all, gain_grads = tail(
        partial,
        tokens,
        residual_grad,
        gain_one,
        gain_two_grad,
        in_grad,
        chan,
        up_line.reshape(4, rows, -1),
        down_line,
        lines,
    )
    up_grad, in_grad, down_grad, out_grad = settle(
        up_all, in_all, down_all.reshape(2 * share, width), chan, owned, width, lines
    )
    small = chan[:owned, width:used].astype(F32)
    gain_grads = lax.dynamic_slice_in_dim(gain_grads[:2], me * rows, rows, 1)
    return (
        output,
        input_grad,
        gain_grads[0],
        in_grad,
        small[:, :5].T,
        small[:, 8:],
        small[:, 5:7].T,
        small[:, 7],
        out_grad,
        gain_grads[1],
        up_grad,
        down_grad,
    )


def solution(mesh):
    count = mesh.shape["shard"]
    fine = Mesh(mesh.devices.reshape(2, count // 4, 2, 2), EVERY)
    rows, cols = P(EVERY, None), P(SHARD, None)
    placed = (
        rows,
        P(EVERY),
        P(SHARD),
        cols,
        P(None, SHARD),
        cols,
        P(None, SHARD),
        P(SHARD),
        cols,
        P(SHARD),
        cols,
        cols,
        rows,
    )
    return jax.shard_map(
        on_device,
        mesh=fine,
        in_specs=placed,
        out_specs=(
            rows,
            rows,
            P(SHARD),
            cols,
            P(None, SHARD),
            cols,
            P(None, SHARD),
            P(SHARD),
            cols,
            P(SHARD),
            cols,
            cols,
        ),
        check_vma=False,
    )
```

```python
import functools

import jax
import jax.numpy as jnp
from jax import lax
from jax.experimental import pallas as pl
from jax.experimental.pallas import tpu as pltpu
from jax.sharding import Mesh, PartitionSpec as P

NBLK = 16
SEQ_LEN = 4096

EPSILON = 1e-06
DECAY_RATE = 8.0
PLANE = ("x", "y", "c")
SHARD = ("l", "y", "c")
EVERY = ("x", "l", "y", "c")
BF = jnp.bfloat16
F32 = jnp.float32


def norm_rows(values, factor):
    return values * lax.rsqrt(jnp.mean(values * values, axis=-1, keepdims=True) + EPSILON) * factor


def contract_rows(left_in, right_in):
    return lax.dot_general(
        left_in, right_in, (((0,), (0,)), ((), ())), preferred_element_type=F32
    )


def times_transposed(left_in, matrix):
    return lax.dot_general(
        left_in, matrix, (((1,), (1,)), ((), ())), preferred_element_type=F32
    )


def gated_product(first_in, second_in):
    return jax.nn.gelu(first_in) * second_in


def plane_gather(block):
    return lax.all_gather(block, PLANE, axis=0, tiled=True)


def plane_scatter(partial):
    return lax.psum_scatter(partial.astype(BF), PLANE, scatter_dimension=0, tiled=True)


MESH = pl.DeviceIdType.MESH


class Wires:
    def __init__(self, send_sems, recv_sems):
        self.send_sems, self.recv_sems, self.used = send_sems, recv_sems, 0

    def far(self, src, dst, device):
        at = self.used
        self.used += 1
        return pltpu.make_async_remote_copy(
            src_ref=src,
            dst_ref=dst,
            send_sem=self.send_sems.at[at],
            recv_sem=self.recv_sems.at[at],
            device_id=device,
            device_id_type=MESH,
        )

    def near(self, src, dst):
        at = self.used
        self.used += 1
        return pltpu.make_async_copy(src, dst, self.send_sems.at[at])


def greet(devices):
    barrier = pltpu.get_barrier_semaphore()
    for device in devices:
        pl.semaphore_signal(barrier, inc=1, device_id=device, device_id_type=MESH)
    pl.semaphore_wait(barrier, len(devices))


def sides():
    x, l, y, c = tuple(lax.axis_index(name) for name in EVERY)
    x_a, y_a = x + (1 - c) * (1 - 2 * x), y + c * (1 - 2 * y)
    x_b, y_b = x + c * (1 - 2 * x), y + (1 - c) * (1 - 2 * y)
    return (x, l, y, c), (x, l, y, 1 - c), (x_a, l, y_a, c), (x_b, l, y_b, c)


def slot_of(device):
    return device[0] * 4 + device[2] * 2 + device[3]


def over_rows(length, rows, step):
    @pl.loop(0, length // rows)
    def _(i):
        step(pl.ds(pl.multiple_of(i * rows, rows), rows))


def block_maker(lhs, rhs, length, transposed):
    def make(slot, target):
        rows = lhs[pl.ds(pl.multiple_of(slot * length, length), length)]
        wide = target.shape[1] // 4
        for part in range(4):
            at = slice(part * wide, (part + 1) * wide)
            if transposed:
                block = lax.dot_general(
                    rows, rhs[at], (((1,), (1,)), ((), ())), preferred_element_type=F32
                )
            else:
                block = jnp.dot(rows, rhs[:, at], preferred_element_type=F32)
            target[:, at] = block.astype(BF)

    return make


class PlaneSum:
    def __init__(self, wires, make, away, own, got, hop_a, hop_b, cuts):
        self.make, self.away = make, away
        self.own, self.got, self.hop_a, self.hop_b = own, got, hop_a, hop_b
        self.cuts, self.part = cuts, own.shape[1] // cuts
        me, core, side_a, side_b = sides()
        diag = (1 - me[0], me[1], 1 - me[2], me[3])
        self.chips = [me, side_a, side_b, diag]
        self.theirs = {0: 0, 1: 2, 2: 1, 3: 3}
        self.order = [3, 1, 2, 0]
        self.swaps = {}
        self.far_a, self.near_a, self.far_b = {}, {}, {}
        for piece in range(cuts):
            rows = pl.ds(piece * self.part, self.part)
            for rel in self.order:
                self.swaps[rel, piece] = wires.far(
                    away.at[rel, rows], got.at[self.theirs[rel], rows], core
                )
            self.far_a[piece] = wires.far(own.at[3, rows], hop_a.at[0, rows], side_a)
            self.near_a[piece] = wires.far(own.at[1, rows], hop_a.at[1, rows], side_a)
            self.far_b[piece] = wires.far(own.at[2, rows], hop_b.at[rows], side_b)

    def make_away(self, rel):
        chip = self.chips[rel]
        self.make(slot_of((chip[0], chip[1], chip[2], 1 - chip[3])), self.away.at[rel])
        for piece in range(self.cuts):
            self.swaps[rel, piece].start()

    def make_home(self, rel):
        self.make(slot_of(self.chips[rel]), self.own.at[rel])

    def landed(self, rel, piece):
        self.swaps[self.theirs[rel], piece].wait_recv()

    def join(self, rel, piece, hopped):
        @pl.loop(0, self.part // 16)
        def _(i):
            rows = pl.ds(pl.multiple_of(piece * self.part + i * 16, 16), 16)
            total = self.own[rel, rows].astype(F32) + self.got[rel, rows].astype(F32)
            if hopped:
                total = total + self.hop_a[0, rows].astype(F32)
            self.own[rel, rows] = total.astype(BF)

    def pass_side(self, rel, copies):
        for piece in range(self.cuts):
            self.landed(rel, piece)
            self.join(rel, piece, False)
            copies[piece].start()

    def first_side(self):
        self.make_away(3)
        self.make_home(3)
        self.make_away(2)
        self.pass_side(3, self.far_a)
        self.make_home(1)
        self.make_away(1)
        self.pass_side(1, self.near_a)
        self.make_home(2)
        self.make_away(0)
        self.make_home(0)

    def second_side(self):
        for piece in range(self.cuts):
            self.landed(2, piece)
            self.far_a[piece].wait_recv()
            self.join(2, piece, True)
            self.far_b[piece].start()

    def finish(self, piece, use):
        self.landed(0, piece)
        self.near_a[piece].wait_recv()
        self.far_b[piece].wait_recv()

        @pl.loop(0, self.part // 16)
        def _(i):
            rows = pl.ds(pl.multiple_of(piece * self.part + i * 16, 16), 16)
            total = self.own[0, rows].astype(F32) + self.got[0, rows].astype(F32)
            total = total + self.hop_a[1, rows].astype(F32) + self.hop_b[rows].astype(F32)
            use(rows, total)

    def drain(self):
        for piece in range(self.cuts):
            for rel in self.order:
                self.swaps[rel, piece].wait_send()
            for copy in (self.far_a[piece], self.near_a[piece], self.far_b[piece]):
                copy.wait_send()


class LineSum:
    def __init__(self, wires, lines, own, from_left, from_right, root):
        x, l, y, c = (lax.axis_index(name) for name in EVERY)
        self.own, self.from_left, self.from_right = own, from_left, from_right
        self.l, self.root, self.lines = l, root, lines
        self.to_right = wires.far(own, from_left, (x, l + 1, y, c))
        self.to_left = wires.far(own, from_right, (x, l - 1, y, c))

    def add(self, other):
        @pl.loop(0, self.own.shape[0] // 16)
        def _(i):
            at = pl.ds(pl.multiple_of(i * 16, 16), 16)
            self.own[at] = (self.own[at].astype(F32) + other[at].astype(F32)).astype(BF)

    def begin(self):
        @pl.when(jnp.logical_and(self.l == 0, self.l < self.root))
        def _():
            self.to_right.start()

        @pl.when(jnp.logical_and(self.l == self.lines - 1, self.l > self.root))
        def _():
            self.to_left.start()

    def through(self):
        @pl.when(jnp.logical_and(self.l > 0, self.l < self.root))
        def _():
            self.to_right.wait_recv()
            self.add(self.from_left)
            self.to_right.start()

        @pl.when(jnp.logical_and(self.l < self.lines - 1, self.l > self.root))
        def _():
            self.to_left.wait_recv()
            self.add(self.from_right)
            self.to_left.start()

    def end(self):
        @pl.when(self.l == self.root)
        def _():
            @pl.when(self.l > 0)
            def _():
                self.to_right.wait_recv()
                self.add(self.from_left)

            @pl.when(self.l < self.lines - 1)
            def _():
                self.to_left.wait_recv()
                self.add(self.from_right)

    def drain(self):
        @pl.when(self.l < self.root)
        def _():
            self.to_right.wait_send()

        @pl.when(self.l > self.root)
        def _():
            self.to_left.wait_send()


def back_rows(base_ref, up_ref, gain_ref, out_ref, gain_out, mine):
    def use(rows, total):
        base = base_ref[rows].astype(F32)
        scale = lax.rsqrt(jnp.mean(base * base, axis=-1, keepdims=True) + EPSILON)
        lean = total * gain_ref[...]
        along = jnp.mean(lean * base, axis=-1, keepdims=True)
        grad = up_ref[rows].astype(F32) + scale * lean
        grad = grad - base * (scale * scale * scale * along)
        out_ref[rows] = grad
        if mine is not None:
            mine[rows] = grad.astype(BF)
        share = total * base * scale
        gain_out[...] += share[:8] + share[8:]

    return use


def forward_rows(base_ref, gain_ref, out_ref, mine):
    def use(rows, total):
        base = base_ref[rows].astype(F32) + total
        out_ref[rows] = base
        scale = lax.rsqrt(jnp.mean(base * base, axis=-1, keepdims=True) + EPSILON)
        mine[rows] = (base * scale * gain_ref[...]).astype(BF)

    return use


class PlaneGather:
    def __init__(self, wires, mine, everything, cuts):
        me, core, side_a, side_b = sides()
        diag = (1 - me[0], me[1], 1 - me[2], me[3])
        here, from_a, from_b, from_diag = [slot_of(at) for at in (me, side_a, side_b, diag)]
        self.cuts, self.copies = cuts, {}
        part = mine.shape[0] // cuts
        for piece in range(cuts):
            rows = pl.ds(piece * part, part)
            for name, src, slot, target in (
                ("a", mine.at[rows], here, side_a),
                ("b", mine.at[rows], here, side_b),
                ("c", mine.at[rows], here, core),
                ("ab", everything.at[from_a, rows], from_a, side_b),
                ("ac", everything.at[from_a, rows], from_a, core),
                ("bc", everything.at[from_b, rows], from_b, core),
                ("dc", everything.at[from_diag, rows], from_diag, core),
            ):
                self.copies[name, piece] = wires.far(src, everything.at[slot, rows], target)
            self.copies["own", piece] = wires.near(mine.at[rows], everything.at[here, rows])

    def start(self, piece):
        for name in ("a", "b", "c", "own"):
            self.copies[name, piece].start()

    def forward(self, came, goes):
        for piece in range(self.cuts):
            self.copies[came, piece].wait_recv()
            for name in goes:
                self.copies[name, piece].start()

    def finish(self):
        for piece in range(self.cuts):
            for name in ("c", "ac", "bc", "dc"):
                self.copies[name, piece].wait_recv()
            self.copies["own", piece].wait()
            for name in ("a", "b", "c", "ab", "ac", "bc", "dc"):
                self.copies[name, piece].wait_send()


def plane_kernel(mode, cuts, *refs):
    refs = list(refs)
    lhs_far, rhs_far, base_far = refs.pop(0), refs.pop(0), refs.pop(0)
    up_far = refs.pop(0) if mode == "back" else None
    gain_ref, out_far = refs.pop(0), refs.pop(0)
    gain_out = refs.pop(0) if mode == "back" else None
    all_ref, lhs, rhs, away, own, got, hop_a, hop_b, base_ref, out_ref = refs[:10]
    up_ref = refs[10] if mode == "back" else None
    mine, send_sems, recv_sems = refs[-3:]
    _, core, side_a, side_b = sides()
    wires = Wires(send_sems, recv_sems)
    operands = [wires.near(lhs_far, lhs), wires.near(rhs_far, rhs)]
    for copy in operands:
        copy.start()
    greet([core, side_a, side_b])
    make = block_maker(lhs, rhs, out_ref.shape[0], mode == "back")
    total = PlaneSum(wires, make, away, own, got, hop_a, hop_b, cuts)
    spread = PlaneGather(wires, mine, all_ref, cuts)
    loads = [wires.near(base_far, base_ref)]
    if mode == "back":
        loads.append(wires.near(up_far, up_ref))
    part = out_ref.shape[0] // cuts
    stores = []
    for piece in range(cuts):
        rows = pl.ds(piece * part, part)
        stores.append(wires.near(out_ref.at[rows], out_far.at[rows]))
    for copy in operands:
        copy.wait()
    for copy in loads:
        copy.start()
    total.first_side()
    total.second_side()
    if mode == "back":
        gain_out[...] = jnp.zeros_like(gain_out)
        use = back_rows(base_ref, up_ref, gain_ref, out_ref, gain_out, mine)
    else:
        use = forward_rows(base_ref, gain_ref, out_ref, mine)
    for copy in loads:
        copy.wait()
    for piece in range(cuts):
        total.finish(piece, use)
        spread.start(piece)
    for copy in stores:
        copy.start()
    spread.forward("a", ("ab", "ac"))
    spread.forward("b", ("bc",))
    spread.forward("ab", ("dc",))
    spread.finish()
    for copy in stores:
        copy.wait()
    total.drain()


def sum_scratch(lhs, rhs, length, width):
    return [
        pltpu.VMEM(lhs.shape, BF),
        pltpu.VMEM(rhs.shape, BF),
        pltpu.VMEM((4, length, width), BF),
        pltpu.VMEM((4, length, width), BF),
        pltpu.VMEM((4, length, width), BF),
        pltpu.VMEM((2, length, width), BF),
        pltpu.VMEM((length, width), BF),
    ]


def plane_sum(lhs, rhs, base, up, gain, number):
    mode = "forward" if up is None else "back"
    length, width = base.shape
    cuts = 2
    vmem, left = pl.BlockSpec(memory_space=pltpu.VMEM), pl.BlockSpec(memory_space=pl.ANY)
    args, specs = [lhs, rhs, base], [left, left, left]
    outs, out_specs = [jax.ShapeDtypeStruct((length, width), F32)], [left]
    scratch = [pltpu.VMEM((length, width), base.dtype), pltpu.VMEM((length, width), F32)]
    if mode == "back":
        args.append(up)
        specs.append(left)
        outs.append(jax.ShapeDtypeStruct((8, width), F32))
        out_specs.append(vmem)
        scratch.append(pltpu.VMEM((length, width), up.dtype))
    args.append(gain.reshape(1, width))
    specs.append(vmem)
    outs.append(jax.ShapeDtypeStruct((8, length, width), BF))
    out_specs.append(left)
    sems = cuts * (4 + 3 + 8 + 1) + 4
    got = list(
        pl.pallas_call(
            functools.partial(plane_kernel, mode, cuts),
            out_shape=outs,
            in_specs=specs,
            out_specs=out_specs,
            scratch_shapes=sum_scratch(lhs, rhs, length, width)
            + scratch
            + [
                pltpu.VMEM((length, width), BF),
                pltpu.SemaphoreType.DMA((sems,)),
                pltpu.SemaphoreType.DMA((sems,)),
            ],
            compiler_params=pltpu.CompilerParams(
                collective_id=number, has_side_effects=True, vmem_limit_bytes=56 << 20
            ),
            cost_estimate=pl.CostEstimate(
                flops=2 * lhs.size * width, bytes_accessed=400 * base.size, transcendentals=0
            ),
            name=f"plane_{mode}_{number}",
        )(*args)
    )
    got[-1] = got[-1].reshape(8 * length, width)
    return got


def tail_kernel(lines, cuts, straight, *refs):
    (lhs_far, rhs_far, base_far, up_far, gain_ref, other_gain, in_ref, chan_ref, upz, downz) = refs[:10]
    (out_far, in_all, chan_out, up_all, down_all, gains) = refs[10:16]
    base_ref, up_ref, out_ref = refs[-3:]
    refs = refs[:-3]
    (lhs, rhs, away, own, got, hop_a, hop_b) = refs[16:23]
    (gain_out, in_own, in_left, in_right) = refs[23:27]
    (chan_own, chan_left, chan_right, chan_got, tiny, tiny_line, send_sems, recv_sems) = refs[27:]
    me, core, side_a, side_b = sides()
    x, l, y, c = me
    k = 2 * y + c
    mates = [core, (x, l, 1 - y, c), (x, l, 1 - y, 1 - c)]
    twin = (1 - x, l, y, c)
    twins = [(1 - x, l, at[2], at[3]) for at in mates]
    wires = Wires(send_sems, recv_sems)
    others = [(x, lax.rem(l + d, lines), y, c) for d in range(1, lines)]
    greet(mates + [twin] + twins + others)

    make = block_maker(lhs, rhs, out_ref.shape[0], True)
    total = PlaneSum(wires, make, away, own, got, hop_a, hop_b, cuts)
    operands = [wires.near(lhs_far, lhs), wires.near(rhs_far, rhs)]
    per = chan_ref.shape[0]
    load_in = wires.near(in_ref, in_own)
    load_chan = wires.near(chan_ref, chan_own)
    in_sums = [
        LineSum(wires, lines, in_own.at[q], in_left.at[q], in_right.at[q], q)
        for q in range(lines)
    ]
    chan_roots = [owner_of(x, k, i, per, straight) // 4 for i in range(per)]
    chan_sums = [
        LineSum(wires, lines, chan_own.at[i], chan_left.at[i], chan_right.at[i], chan_roots[i])
        for i in range(per)
    ]

    def deliver(block, target):
        copies = [wires.near(block(k), target.at[x, k])]
        for at in [twin] + mates + twins:
            copies.append(wires.far(block(2 * at[2] + at[3]), target.at[x, k], at))
        return copies

    loads = [wires.near(base_far, base_ref), wires.near(up_far, up_ref)]
    part = out_ref.shape[0] // cuts
    stores = []
    for piece in range(cuts):
        at = pl.ds(piece * part, part)
        stores.append(wires.near(out_ref.at[at], out_far.at[at]))
    load_in.start()
    for copy in operands:
        copy.start()
    load_chan.start()
    for copy in loads:
        copy.start()
    up_copies = deliver(lambda to: upz.at[to], up_all)
    down_copies = [wires.near(downz, down_all.at[x]), wires.far(downz, down_all.at[x], twin)]
    load_in.wait()
    load_chan.wait()
    for copy in operands:
        copy.wait()

    def pass_right(q):
        one = in_sums[q]

        @pl.when(jnp.logical_and(l > 0, l < q))
        def _():
            one.to_right.wait_recv()
            one.add(one.from_left)
            one.to_right.start()

    def pass_left(q):
        one = in_sums[q]

        @pl.when(jnp.logical_and(l < lines - 1, l > q))
        def _():
            one.to_left.wait_recv()
            one.add(one.from_right)
            one.to_left.start()

    def send_ends(q):
        @pl.when(jnp.logical_and(l == 0, q > 0))
        def _():
            in_sums[q].to_right.start()

        @pl.when(jnp.logical_and(l == lines - 1, q > 0))
        def _():
            in_sums[lines - 1 - q].to_left.start()

    send_ends(lines - 1)
    total.first_side()
    if lines > 2:
        send_ends(lines - 2)
    pass_right(lines - 1)
    pass_left(0)
    total.second_side()
    for q in reversed(range(1, lines - 2)):
        send_ends(q)
    for copy in down_copies + up_copies:
        copy.start()
    for q in reversed(range(1, lines - 1)):
        pass_right(q)
        pass_left(lines - 1 - q)
    for one in chan_sums:
        one.begin()
    gain_out[...] = jnp.zeros_like(gain_out)
    use = back_rows(base_ref, up_ref, gain_ref, out_ref, gain_out, None)
    for copy in loads:
        copy.wait()
    for piece in range(cuts):
        total.finish(piece, use)
        stores[piece].start()
    for one in chan_sums:
        one.through()
    for q in range(lines):
        in_sums[q].end()
    rows = in_all.shape[2]
    in_copies = deliver(
        lambda to: in_own.at[l, pl.ds(pl.multiple_of(to * rows, rows), rows)], in_all
    )
    for copy in in_copies:
        copy.start()
    lane = lax.broadcasted_iota(jnp.int32, tiny.shape[1:], 0)
    first = jnp.sum(gain_out[...], axis=0, keepdims=True)
    second = jnp.sum(other_gain[...], axis=0, keepdims=True)
    tiny[0] = jnp.where(lane == 0, first, jnp.where(lane == 1, second, 0.0))
    for step, at in enumerate((core, twin, (x, l, 1 - y, c))):
        copy = wires.far(tiny.at[2 * step], tiny.at[2 * step + 1], at)
        copy.start()
        copy.wait()
        tiny[2 * step + 2] = tiny[2 * step] + tiny[2 * step + 1]
    line_copies = []
    for d, device in enumerate(others):
        line_copies.append(wires.far(tiny.at[6], tiny_line.at[l], device))
        line_copies[-1].start()
    tiny_line[l] = tiny[6]
    for one in chan_sums:
        one.end()
    goal = 4 * l + k
    for_x, holder, piece = holder_of(goal, per, straight)
    holds = for_x == x
    chan_far, chan_near = [], []
    for i in range(per):
        s = owner_of(x, k, i, per, straight)
        mate = (x, l, lax.rem(s, 4) // 2, lax.rem(s, 2))
        far = wires.far(chan_own.at[i], chan_got, mate)
        near = wires.near(chan_own.at[i], chan_got)
        at_root = chan_roots[i] == l
        away = jnp.logical_and(at_root, lax.rem(s, 4) != k)
        stay = jnp.logical_and(at_root, lax.rem(s, 4) == k)
        chan_far.append((far, away))
        chan_near.append((near, stay))

        @pl.when(away)
        def _():
            far.start()

        @pl.when(stay)
        def _():
            near.start()
            near.wait()

    for i in range(per):
        mine_here = jnp.logical_and(holds, piece == i)

        @pl.when(jnp.logical_and(mine_here, holder != k))
        def _():
            chan_far[i][0].wait_recv()

    to_twin = wires.far(chan_got, chan_out, twin)
    keep = wires.near(chan_got, chan_out)

    @pl.when(holds)
    def _():
        to_twin.start()
        keep.start()
        keep.wait()

    @pl.when(jnp.logical_not(holds))
    def _():
        to_twin.wait_recv()

    for copy in line_copies:
        copy.wait()
    gains[...] = tiny_line[0]
    for q in range(1, lines):
        gains[...] += tiny_line[q]
    for copies in (in_copies, up_copies, down_copies, stores):
        for copy in copies:
            copy.wait()

    @pl.when(holds)
    def _():
        to_twin.wait_send()

    for far, away in chan_far:

        @pl.when(away)
        def _():
            far.wait_send()

    for one in in_sums + chan_sums:
        one.drain()
    total.drain()


def tail(lhs, rhs, base, up, gain, other_gain, in_grad, chan, upz, downz, lines, straight):
    length, width = base.shape
    cuts = 2
    vmem, left = pl.BlockSpec(memory_space=pltpu.VMEM), pl.BlockSpec(memory_space=pl.ANY)
    rows = in_grad.shape[0] // (4 * lines)
    pieces = in_grad.reshape(lines, 4 * rows, in_grad.shape[1])
    per = chan.shape[0]
    sems = cuts * 8 + 6 + 2 * (lines + per) + 16 + 2 + 8 + 3 + lines + 2 * per + 4
    return pl.pallas_call(
        functools.partial(tail_kernel, lines, cuts, straight),
        out_shape=[
            jax.ShapeDtypeStruct((length, width), F32),
            jax.ShapeDtypeStruct((2, 4, rows, in_grad.shape[1]), BF),
            jax.ShapeDtypeStruct(chan.shape[1:], BF),
            jax.ShapeDtypeStruct((2,) + upz.shape, BF),
            jax.ShapeDtypeStruct((2,) + downz.shape, BF),
            jax.ShapeDtypeStruct((8, width), F32),
        ],
        in_specs=[left, left, left, left, vmem, vmem, left, left, left, left],
        out_specs=[left, left, left, left, left, vmem],
        scratch_shapes=sum_scratch(lhs, rhs, length, width)
        + [pltpu.VMEM((8, width), F32)]
        + [pltpu.VMEM(pieces.shape, BF)] * 3
        + [pltpu.VMEM(chan.shape, BF)] * 3
        + [
            pltpu.VMEM(chan.shape[1:], BF),
            pltpu.VMEM((7, 8, width), F32),
            pltpu.VMEM((lines, 8, width), F32),
            pltpu.SemaphoreType.DMA((sems,)),
            pltpu.SemaphoreType.DMA((sems,)),
            pltpu.VMEM((length, width), base.dtype),
            pltpu.VMEM((length, width), F32),
            pltpu.VMEM((length, width), F32),
        ],
        compiler_params=pltpu.CompilerParams(
            collective_id=3, has_side_effects=True, vmem_limit_bytes=56 << 20
        ),
        cost_estimate=pl.CostEstimate(
            flops=20 * base.size, bytes_accessed=400 * base.size, transcendentals=0
        ),
        name="tail",
    )(lhs, rhs, base, up, gain.reshape(1, width), other_gain, pieces, chan, upz, downz)


def owner_of(x, k, i, per, straight):
    return 4 * (x * per + i) + k if straight else (4 * x + k) * per + i


def holder_of(s, per, straight):
    if straight:
        return s // 4 // per, lax.rem(s, 4), lax.rem(s // 4, per)
    return s // (4 * per), lax.rem(s // per, 4), lax.rem(s, per)


class LineGather:
    def __init__(self, wires, lines, blocks):
        x, l, y, c = (lax.axis_index(name) for name in EVERY)
        self.l, self.lines = l, lines
        self.right, self.left = [], []
        for d in range(lines - 1):
            block = blocks.at[jnp.maximum(l - d, 0)]
            self.right.append(wires.far(block, block, (x, l + 1, y, c)))
            block = blocks.at[jnp.minimum(l + d, lines - 1)]
            self.left.append(wires.far(block, block, (x, l - 1, y, c)))

    def step(self, d):
        l, last = self.l, self.lines - 1

        @pl.when(l >= d)
        def _():
            if d > 0:
                self.right[d - 1].wait_recv()
            if d < last:

                @pl.when(l < last)
                def _():
                    self.right[d].start()

        @pl.when(l + d <= last)
        def _():
            if d > 0:
                self.left[d - 1].wait_recv()
            if d < last:

                @pl.when(l > 0)
                def _():
                    self.left[d].start()

    def drain(self):
        l, last = self.l, self.lines - 1
        for d in range(last):

            @pl.when(jnp.logical_and(l >= d, l < last))
            def _():
                self.right[d].wait_send()

            @pl.when(jnp.logical_and(l + d <= last, l > 0))
            def _():
                self.left[d].wait_send()


class FromRoot:
    def __init__(self, wires, lines, source, target, i, per, straight):
        x, l, y, c = (lax.axis_index(name) for name in EVERY)
        k = 2 * y + c
        self.l, self.lines = l, lines
        wanted = owner_of(x, k, i, per, straight)
        self.root = wanted // 4
        for_x, goal, piece = holder_of(4 * l + k, per, straight)
        mine = jnp.logical_and(for_x == x, piece == i)
        self.leaves = jnp.logical_and(mine, goal != k)
        self.stays = jnp.logical_and(mine, goal == k)
        self.comes = jnp.logical_and(self.root == l, lax.rem(wanted, 4) != k)
        self.far = wires.far(source, target.at[i], (x, l, goal // 2, lax.rem(goal, 2)))
        self.near = wires.near(source, target.at[i])
        self.right = wires.far(target.at[i], target.at[i], (x, l + 1, y, c))
        self.left = wires.far(target.at[i], target.at[i], (x, l - 1, y, c))

    def start(self):
        @pl.when(self.leaves)
        def _():
            self.far.start()

        @pl.when(self.stays)
        def _():
            self.near.start()

    def onward(self):
        l, root, last = self.l, self.root, self.lines - 1

        @pl.when(jnp.logical_and(l >= root, l < last))
        def _():
            self.right.start()

        @pl.when(jnp.logical_and(l <= root, l > 0))
        def _():
            self.left.start()

    def from_owner(self):
        @pl.when(self.stays)
        def _():
            self.near.wait()

        @pl.when(self.comes)
        def _():
            self.far.wait_recv()

        @pl.when(self.l == self.root)
        def _():
            self.onward()

    def from_line(self):
        @pl.when(self.l > self.root)
        def _():
            self.right.wait_recv()
            self.onward()

        @pl.when(self.l < self.root)
        def _():
            self.left.wait_recv()
            self.onward()

    def drain(self):
        l, root, last = self.l, self.root, self.lines - 1

        @pl.when(self.leaves)
        def _():
            self.far.wait_send()

        @pl.when(jnp.logical_and(l >= root, l < last))
        def _():
            self.right.wait_send()

        @pl.when(jnp.logical_and(l <= root, l > 0))
        def _():
            self.left.wait_send()


def start_kernel(lines, cuts, straight, *refs):
    (tok, mix, up, small, tiny) = refs[:5]
    (tok_all, halo, mix_all, up_all, small_all, tiny_all) = refs[5:11]
    send_sems, recv_sems = refs[11:]
    me, core, side_a, side_b = sides()
    x, l, y, c = me
    k = 2 * y + c
    other_y, cross, twin = (x, l, 1 - y, c), (x, l, 1 - y, 1 - c), (1 - x, l, y, c)
    mates = [core, other_y, cross]
    others = [(x, lax.rem(l + d, lines), y, c) for d in range(1, lines)]
    per = small_all.shape[0]
    wires = Wires(send_sems, recv_sems)
    greet(mates + [twin] + others)

    def exchange(source, target):
        copies = [wires.near(source.at[k], target.at[k])]
        for at in mates:
            copies.append(wires.far(source.at[2 * at[2] + at[3]], target.at[k], at))
        return copies

    mix_swap = exchange(mix, mix_all.at[l])
    up_swap = exchange(up, up_all)
    spread = PlaneGather(wires, tok, tok_all, cuts)
    walk = LineGather(wires, lines, mix_all)
    roots = [FromRoot(wires, lines, small, small_all, i, per, straight) for i in range(per)]
    tiny_own = wires.near(tiny, tiny_all.at[x, c, y, l])
    tiny_line = [wires.far(tiny, tiny_all.at[x, c, y, l], at) for at in others]
    tiny_steps = [
        wires.far(tiny_all.at[x, c, y], tiny_all.at[x, c, y], other_y),
        wires.far(tiny_all.at[x, c], tiny_all.at[x, c], core),
        wires.far(tiny_all.at[x], tiny_all.at[x], twin),
    ]
    length = tok.shape[0]
    edge = pl.ds(length - 8, 8)
    halo_far = [
        wires.far(tok_all.at[4 * run + 3, edge], halo.at[run], (x, l + 1, y, c))
        for run in range(2)
    ]
    halo_near = [wires.near(tok.at[edge], halo.at[run]) for run in range(2)]

    for copy in mix_swap + [tiny_own] + tiny_line:
        copy.start()
    for one in roots:
        one.start()
    for piece in range(cuts):
        spread.copies["a", piece].start()
    for piece in range(cuts):
        spread.copies["b", piece].start()
    for copy in mix_swap:
        copy.wait()
    walk.step(0)
    for one in roots:
        one.from_owner()
    for piece in range(cuts):
        spread.copies["c", piece].start()
        spread.copies["own", piece].start()
    for copy in [tiny_own] + tiny_line:
        copy.wait()
    for copy in tiny_steps:
        copy.start()
        copy.wait()
    walk.step(1)
    spread.forward("a", ("ab", "ac"))
    for one in roots:
        one.from_line()
    spread.forward("b", ("bc",))
    for copy in up_swap:
        copy.start()
    for d in range(2, lines):
        walk.step(d)
    spread.forward("ab", ("dc",))
    spread.finish()

    @pl.when(l < lines - 1)
    def _():
        for copy in halo_far:
            copy.start()

    @pl.when(l == 0)
    def _():
        for copy in halo_near:
            copy.start()
            copy.wait()

    for copy in up_swap:
        copy.wait()

    @pl.when(l > 0)
    def _():
        for copy in halo_far:
            copy.wait_recv()

    @pl.when(l < lines - 1)
    def _():
        for copy in halo_far:
            copy.wait_send()

    walk.drain()
    for one in roots:
        one.drain()


def spread_inputs(tok, mix, up, small, tiny, lines, per, straight):
    length, width = tok.shape
    cuts = 2
    vmem, left = pl.BlockSpec(memory_space=pltpu.VMEM), pl.BlockSpec(memory_space=pl.ANY)
    sems = 12 + cuts * 8 + 2 * lines + per * 4 + lines + 1 + 3 + 4
    return pl.pallas_call(
        functools.partial(start_kernel, lines, cuts, straight),
        out_shape=[
            jax.ShapeDtypeStruct((8, length, width), BF),
            jax.ShapeDtypeStruct((2, 8, width), BF),
            jax.ShapeDtypeStruct((lines,) + mix.shape, BF),
            jax.ShapeDtypeStruct(up.shape, BF),
            jax.ShapeDtypeStruct((per,) + small.shape, BF),
            jax.ShapeDtypeStruct((2, 2, 2, lines) + tiny.shape, F32),
        ],
        in_specs=[left] * 4 + [vmem],
        out_specs=[left] * 5 + [vmem],
        scratch_shapes=[
            pltpu.SemaphoreType.DMA((sems,)),
            pltpu.SemaphoreType.DMA((sems,)),
        ],
        compiler_params=pltpu.CompilerParams(
            collective_id=4, has_side_effects=True, vmem_limit_bytes=56 << 20
        ),
        cost_estimate=pl.CostEstimate(
            flops=20 * tok.size, bytes_accessed=400 * tok.size, transcendentals=0
        ),
        name="spread",
    )(tok, mix, up, small, tiny)


def pick_kernel(lines, straight, mlp, mix, up, mix_out):
    x = lax.axis_index("x")
    share = up.shape[-1] // (2 * lines)
    own = mix_out.shape[-1] // 2
    for k in range(4):
        parts = []
        for g in range(2 * lines):
            at = (4 * g + k) * 2 * share
            first, second = mlp[:, at : at + share], mlp[:, at + share : at + 2 * share]
            parts.append(jnp.where(x == 0, first, second))
        up[k] = jnp.concatenate(parts, axis=1)
    for k in range(4):
        parts = []
        for side in range(2):
            halves = []
            for half in range(2):
                base = side * 8 * own + half * 4 * own
                if straight:
                    owned = own * 8 // (4 * lines)
                    per = own // owned
                    starts = [(base + (4 * i + k) * owned, owned) for i in range(per)]
                else:
                    starts = [(base + k * own, own)]
                halves.append(
                    jnp.concatenate([mix[:, at : at + wide] for at, wide in starts], axis=1)
                )
            parts.append(jnp.where(x == 0, halves[0], halves[1]))
        mix_out[k] = jnp.concatenate(parts, axis=1)


def pick(mlp_in, mix_in, lines, straight):
    rows, wide = mlp_in.shape
    narrow = mix_in.shape[1]
    steps = 4 if rows % 64 == 0 else 1
    r = rows // steps
    shapes = [wide // 8, narrow // 8]
    return pl.pallas_call(
        functools.partial(pick_kernel, lines, straight),
        grid=(steps,),
        in_specs=[
            pl.BlockSpec((r, wide), lambda i: (i, 0)),
            pl.BlockSpec((r, narrow), lambda i: (i, 0)),
        ],
        out_specs=[pl.BlockSpec((4, r, w), lambda i: (0, i, 0)) for w in shapes],
        out_shape=[jax.ShapeDtypeStruct((4, rows, w), BF) for w in shapes],
        compiler_params=pltpu.CompilerParams(vmem_limit_bytes=40 << 20),
        name="pick",
    )(mlp_in, mix_in)


def gelu_parts(value):
    slope = 0.7978845608028654
    bend = jnp.tanh(slope * (value + 0.044715 * value * value * value))
    gelu = 0.5 * value * (1.0 + bend)
    inner = slope * (1.0 + 0.134145 * value * value)
    return gelu, 0.5 * (1.0 + bend) + 0.5 * value * (1.0 - bend * bend) * inner


def recur_parts(conv_out, chan, gate_ref, keep):
    pre = jnp.dot(conv_out, gate_ref[...], preferred_element_type=F32) + chan[5:6]
    recur = jax.nn.sigmoid(pre)
    log_decay = chan[7:8] * recur
    decayed = jnp.exp(log_decay)
    twice = -2.0 * log_decay
    return recur, decayed, decayed * keep, twice


def below_one(decayed, twice):
    series = 1.0 / 5040.0
    for term in (-1.0 / 720.0, 1.0 / 120.0, -1.0 / 24.0, 1.0 / 6.0, -0.5, 1.0):
        series = series * twice + term
    return jnp.where(twice < 0.5, twice * series, 1.0 - decayed * decayed)


def scan_tiles(rows, backward, first, second, out_first, out_second, carry):
    channels = first.shape[-1]
    where = lax.broadcasted_iota(jnp.int32, (8, channels), 0)
    tiles = rows // 8

    def step(i, state):
        before_a, before_b = state
        tile = tiles - 1 - i if backward else i
        at = pl.ds(pl.multiple_of(tile * 8, 8), 8)
        a, b = first[at], second[at]
        for gap in (1, 2, 4):
            turn = 8 - gap if backward else gap
            inside = where < 8 - gap if backward else where >= gap
            near_a = jnp.where(inside, pltpu.roll(a, turn, 0), 1.0)
            near_b = jnp.where(inside, pltpu.roll(b, turn, 0), 0.0)
            b = b + a * near_b
            a = a * near_a
        b = b + a * before_b
        a = a * before_a
        out_first[at] = a
        out_second[at] = b
        last = 0 if backward else 7
        return (
            jnp.broadcast_to(a[last : last + 1], a.shape),
            jnp.broadcast_to(b[last : last + 1], b.shape),
        )

    end = lax.fori_loop(0, tiles, step, (carry[0], carry[1]), unroll=4)
    carry[0] = end[0]
    carry[1] = end[1]


def mix_forward_kernel(*refs):
    (tok, halo, weight, gain, chan_ref, gate_r, gate_i, fac, cot) = refs[:9]
    (normed, branch, conv_in, conv_out, pa, pb, ends, cot_all) = refs[9:17]
    (rows_in, coef, drive, carry, send_sems, recv_sems) = refs[17:]
    length, own = branch.shape
    chunk = pl.program_id(1)
    chan = chan_ref[...]
    turn = pl.program_id(0) * pl.num_programs(1) + chunk
    last = 2 * pl.num_programs(1) - 1
    _, core, side_a, side_b = sides()
    spread = PlaneGather(Wires(send_sems, recv_sems), cot, cot_all, 2)

    @pl.when(turn == 0)
    def _():
        greet([core, side_a, side_b])
        for piece in range(2):
            spread.start(piece)

    @pl.when(turn == last - 2)
    def _():
        spread.forward("a", ("ab", "ac"))
        spread.forward("b", ("bc",))

    def norm_of(values):
        values = values.astype(F32)
        scale = lax.rsqrt(jnp.mean(values * values, axis=-1, keepdims=True) + EPSILON)
        return (values * scale * gain[...]).astype(BF)

    @pl.when(chunk == 0)
    def _():
        carry[0] = jnp.ones_like(carry[0])
        carry[1] = jnp.zeros_like(carry[1])
        edge = jnp.dot(norm_of(halo[0]), weight[...], preferred_element_type=F32)
        rows_in[8:16] = pltpu.roll(edge, own, 1)[:, :own].astype(BF).astype(F32)
        rows_in[0:8] = jnp.zeros((8, own), F32)
        conv_in[0, 0:16] = rows_in[0:16].astype(BF)

    @pl.when(chunk > 0)
    def _():
        rows_in[0:16] = rows_in[length : length + 16]

    @pl.loop(0, length // 16)
    def _(i):
        at = pl.ds(pl.multiple_of(i * 16, 16), 16)
        normed[0, at] = norm_of(tok[0, at])

    projected = jnp.dot(normed[0], weight[...], preferred_element_type=F32)
    branch[...] = projected[:, :own]
    rounded = pltpu.roll(projected, own, 1)[:, :own].astype(BF)
    conv_in[0, pl.ds(pl.multiple_of(16 + chunk * length, 16), length)] = rounded
    rows_in[16 : 16 + length] = rounded.astype(F32)
    window = rows_in[8 : 16 + length]
    total = chan[4:5] + chan[0:1] * window[8:]
    for gap in range(1, 4):
        total = total + chan[gap : gap + 1] * pltpu.roll(window, gap, 0)[8:] * fac[:, gap - 1 : gap]
    low = total.astype(BF)
    conv_out[...] = low
    keep = fac[:, 0:1]
    _, decayed, coefficient, twice = recur_parts(low, chan, gate_r, keep)
    coef[...] = coefficient
    input_gate = jax.nn.sigmoid(
        jnp.dot(low, gate_i[...], preferred_element_type=F32) + chan[6:7]
    )
    scaling = jnp.where(keep == 0.0, 1.0, jnp.sqrt(below_one(decayed, twice)))
    drive[...] = scaling * input_gate * low.astype(F32)
    scan_tiles(length, False, coef, drive, pa, pb, carry)
    ends[0, 0:8] = carry[0]
    ends[0, 8:16] = carry[1]

    @pl.when(turn == last)
    def _():
        spread.forward("ab", ("dc",))
        spread.finish()


def mix_state_kernel(*refs):
    (res, weight, branch, pa, pb, state_in, conv_out, chan_ref, gate_r, fac) = refs[:10]
    (branch_grad, ta, tb, ends) = refs[10:14]
    (coef, grad, carry, first_coef) = refs[14:]
    length, own = branch.shape
    chan = chan_ref[...]
    turn = pl.program_id(1)

    @pl.when(turn == 0)
    def _():
        carry[0] = jnp.ones_like(carry[0])
        carry[1] = jnp.zeros_like(carry[1])
        first_coef[...] = jnp.ones_like(first_coef)

    mixed_grad = lax.dot_general(
        res[...], weight[...], (((1,), (1,)), ((), ())), preferred_element_type=F32
    )
    state = pb[...] + pa[...] * state_in[0, 0:1]
    gelu, slope = gelu_parts(branch[...])
    branch_grad[...] = (mixed_grad * state * slope).astype(BF)
    grad[...] = mixed_grad * gelu
    _, _, coefficient, _ = recur_parts(conv_out[...], chan, gate_r, fac[:, 0:1])
    row = lax.broadcasted_iota(jnp.int32, (length, own), 0)
    shifted = pltpu.roll(coefficient, length - 1, 0)
    coef[...] = jnp.where(row == length - 1, first_coef[0:1], shifted)
    first = jnp.broadcast_to(coefficient[0:1], first_coef.shape)
    first_coef[...] = first
    scan_tiles(length, True, coef, grad, ta, tb, carry)
    ends[0, 0:8] = first * carry[0]
    ends[0, 8:16] = first * carry[1]


def mix_gates_kernel(*refs):
    (ta, tb, from_right, pa, pb, pa_before, pb_before, state_in) = refs[:8]
    (conv_in, conv_out, branch_grad, chan_ref, gate_r, gate_i, fac) = refs[8:15]
    (proj_grad, last_rows, edges, sums, gate_grad) = refs[15:20]
    (after,) = refs[20:]
    length, own = ta.shape
    turn, turns = pl.program_id(1), pl.num_programs(1)
    chunk = turns - 1 - turn
    chan = chan_ref[...]

    @pl.when(jnp.logical_and(turn == 0, pl.program_id(0) == 0))
    def _():
        sums[...] = jnp.zeros_like(sums)
        gate_grad[...] = jnp.zeros_like(gate_grad)

    @pl.when(turn == 0)
    def _():
        after[...] = jnp.zeros_like(after)

    start = state_in[0, 0:1]
    total = tb[...] + ta[...] * from_right[0, 0:1]
    state = pb[...] + pa[...] * start
    row = lax.broadcasted_iota(jnp.int32, (length, own), 0)
    before = pb_before[7:8] + pa_before[7:8] * start
    before = jnp.where(chunk == 0, start, before)
    prev_state = jnp.where(row == 0, before, pltpu.roll(state, 1, 0))
    keep = fac[:, 0:1]
    low = conv_out[...]
    conv = low.astype(F32)
    recur, decayed, coefficient, twice = recur_parts(low, chan, gate_r, keep)
    input_gate = jax.nn.sigmoid(
        jnp.dot(low, gate_i[...], preferred_element_type=F32) + chan[6:7]
    )
    rest = below_one(decayed, twice)
    fresh = keep == 0.0
    scaling = jnp.where(fresh, 1.0, jnp.sqrt(rest))
    gated = total * input_gate
    by_scaling = jnp.where(fresh, 0.0, gated * conv * decayed * decayed * lax.rsqrt(rest))
    decay_grad = total * prev_state * coefficient - by_scaling
    recur_grad = (chan[7:8] * decay_grad * recur * (1.0 - recur)).astype(BF)
    input_grad = (total * scaling * conv * input_gate * (1.0 - input_gate)).astype(BF)

    def fold(values):
        return jnp.sum(values.reshape(length // 8, 8, own), axis=0)

    sums[5] += fold(recur_grad.astype(F32))
    sums[6] += fold(input_grad.astype(F32))
    sums[7] += fold(decay_grad * recur)
    contract = (((0,), (0,)), ((), ()))
    gate_grad[0] += lax.dot_general(low, recur_grad, contract, preferred_element_type=F32)
    gate_grad[1] += lax.dot_general(low, input_grad, contract, preferred_element_type=F32)
    across = (((1,), (1,)), ((), ()))
    conv_grad = gated * scaling
    conv_grad = conv_grad + lax.dot_general(
        recur_grad, gate_r[...], across, preferred_element_type=F32
    )
    conv_grad = conv_grad + lax.dot_general(
        input_grad, gate_i[...], across, preferred_element_type=F32
    )
    window = conv_in[0, pl.ds(pl.multiple_of(chunk * length, 16), length + 16)].astype(F32)[8:]
    sums[4] += fold(conv_grad)
    sums[0] += fold(conv_grad * window[8:])
    conv_in_grad = chan[0:1] * conv_grad
    edge_row = lax.broadcasted_iota(jnp.int32, (8, own), 0)
    edge = jnp.zeros((8, own), F32)
    for gap in range(1, 4):
        masked = conv_grad * fac[:, gap - 1 : gap]
        sums[gap] += fold(masked * pltpu.roll(window, gap, 0)[8:])
        moved = pltpu.roll(jnp.concatenate([masked, after[gap - 1]], axis=0), length + 8 - gap, 0)
        conv_in_grad = conv_in_grad + chan[gap : gap + 1] * moved[:length]
        head = masked[0:8]
        after[gap - 1] = head
        given = pltpu.roll(head, 3 - gap, 0)
        given = jnp.where((edge_row >= 3 - gap) & (edge_row < 3), given, 0.0)
        edge = edge + chan[gap : gap + 1] * given
    edges[0] = edge

    @pl.when(turn == 0)
    def _():
        last_rows[0] = conv_in_grad[length - 8 :]

    proj_grad[:, :own] = branch_grad[...]
    proj_grad[:, own:] = conv_in_grad.astype(BF)


def line_kernel(lines, backward, ends, start, got, send_sems, recv_sems):
    x, l, y, c = (lax.axis_index(name) for name in EVERY)
    wires = Wires(send_sems, recv_sems)
    others = [(x, lax.rem(l + d, lines), y, c) for d in range(1, lines)]
    greet(others)
    copies = [wires.far(ends, got.at[l], at) for at in others]
    for copy in copies:
        copy.start()
    for copy in copies:
        copy.wait()
    for run in range(2):
        value = jnp.zeros(start.shape[1:], F32)
        order = reversed(range(1, lines)) if backward else range(lines - 1)
        for other in order:
            longer = got[other, run, 0:8] * value + got[other, run, 8:16]
            reached = other > l if backward else other < l
            value = jnp.where(reached, longer, value)
        start[run] = value


def line_start(ends, lines, backward, number):
    vmem = pl.BlockSpec(memory_space=pltpu.VMEM)
    own = ends.shape[-1]
    return pl.pallas_call(
        functools.partial(line_kernel, lines, backward),
        out_shape=jax.ShapeDtypeStruct((2, 8, own), F32),
        in_specs=[vmem],
        out_specs=vmem,
        scratch_shapes=[
            pltpu.VMEM((lines,) + ends.shape, F32),
            pltpu.SemaphoreType.DMA((lines,)),
            pltpu.SemaphoreType.DMA((lines,)),
        ],
        compiler_params=pltpu.CompilerParams(
            collective_id=number, has_side_effects=True, vmem_limit_bytes=8 << 20
        ),
        name=f"line_{number}",
    )(ends)


def mix_specs(run, length, own, backward):
    steps = run // length

    def turn(j):
        return steps - 1 - j if backward else j

    def rows(width):
        return pl.BlockSpec((length, width), lambda i, j: (i * steps + turn(j), 0))

    def slots(width):
        return pl.BlockSpec((1, length, width), lambda i, j: (i * steps + turn(j), 0, 0))

    def whole(*shape):
        return pl.BlockSpec(shape, lambda i, j: (0,) * len(shape), pipeline_mode=pl.Buffered(1))

    def held(*shape):
        return pl.BlockSpec((1,) + shape, lambda i, j: (i,) + (0,) * len(shape))

    return steps, rows, slots, whole, held


def mix_forward(tok_all, halo, weight, gain, chan, gate_r, gate_i, fac, cot):
    slots_in, length, width = tok_all.shape
    own, run = chan.shape[1], 4 * length
    steps, rows, slots, whole, held = mix_specs(run, length, own, False)
    flat = jax.ShapeDtypeStruct((2 * run, own), F32)
    return pl.pallas_call(
        mix_forward_kernel,
        grid=(2, steps),
        in_specs=[
            slots(width),
            held(8, width),
            whole(width, 2 * own),
            whole(1, width),
            whole(8, own),
            whole(own, own),
            whole(own, own),
            rows(fac.shape[1]),
            pl.BlockSpec(memory_space=pl.ANY),
        ],
        out_specs=[
            slots(width),
            rows(own),
            held(16 + run, own),
            rows(own),
            rows(own),
            rows(own),
            held(16, own),
            pl.BlockSpec(memory_space=pl.ANY),
        ],
        out_shape=[
            jax.ShapeDtypeStruct(tok_all.shape, BF),
            flat,
            jax.ShapeDtypeStruct((2, 16 + run, own), BF),
            jax.ShapeDtypeStruct((2 * run, own), BF),
            flat,
            flat,
            jax.ShapeDtypeStruct((2, 16, own), F32),
            jax.ShapeDtypeStruct((8,) + cot.shape, BF),
        ],
        scratch_shapes=[
            pltpu.VMEM((16 + length, own), F32),
            pltpu.VMEM((length, own), F32),
            pltpu.VMEM((length, own), F32),
            pltpu.VMEM((2, 8, own), F32),
            pltpu.SemaphoreType.DMA((16,)),
            pltpu.SemaphoreType.DMA((16,)),
        ],
        compiler_params=pltpu.CompilerParams(
            collective_id=7, has_side_effects=True, vmem_limit_bytes=40 << 20
        ),
        cost_estimate=pl.CostEstimate(
            flops=4 * run * width * 2 * own, bytes_accessed=60 << 20, transcendentals=0
        ),
        name="mix_forward",
    )(tok_all, halo, weight, gain.reshape(1, width), chan, gate_r, gate_i, fac, cot)


def mix_state(res, weight, branch, pa, pb, state_in, conv_out, chan, gate_r, fac, length):
    own, width = weight.shape
    run = res.shape[0] // 2
    steps, rows, slots, whole, held = mix_specs(run, length, own, True)
    flat = jax.ShapeDtypeStruct((2 * run, own), F32)
    return pl.pallas_call(
        mix_state_kernel,
        grid=(2, steps),
        in_specs=[
            rows(width),
            whole(own, width),
            rows(own),
            rows(own),
            rows(own),
            held(8, own),
            rows(own),
            whole(8, own),
            whole(own, own),
            rows(fac.shape[1]),
        ],
        out_specs=[rows(own), rows(own), rows(own), held(16, own)],
        out_shape=[
            jax.ShapeDtypeStruct((2 * run, own), BF),
            flat,
            flat,
            jax.ShapeDtypeStruct((2, 16, own), F32),
        ],
        scratch_shapes=[
            pltpu.VMEM((length, own), F32),
            pltpu.VMEM((length, own), F32),
            pltpu.VMEM((2, 8, own), F32),
            pltpu.VMEM((8, own), F32),
        ],
        compiler_params=pltpu.CompilerParams(vmem_limit_bytes=40 << 20),
        cost_estimate=pl.CostEstimate(
            flops=4 * run * width * own, bytes_accessed=40 << 20, transcendentals=0
        ),
        name="mix_state",
    )(res, weight, branch, pa, pb, state_in, conv_out, chan, gate_r, fac)


def mix_gates(
    ta, tb, from_right, pa, pb, state_in, conv_in, conv_out, branch_grad, chan, gate_r, gate_i, fac, length
):
    own = chan.shape[1]
    run = ta.shape[0] // 2
    steps, rows, slots, whole, held = mix_specs(run, length, own, True)
    eights = length // 8
    earlier = pl.BlockSpec(
        (8, own), lambda i, j: (jnp.maximum((i * steps + steps - 1 - j) * eights - 1, 0), 0)
    )
    return pl.pallas_call(
        mix_gates_kernel,
        grid=(2, steps),
        in_specs=[
            rows(own),
            rows(own),
            held(8, own),
            rows(own),
            rows(own),
            earlier,
            earlier,
            held(8, own),
            held(16 + run, own),
            rows(own),
            rows(own),
            whole(8, own),
            whole(own, own),
            whole(own, own),
            rows(fac.shape[1]),
        ],
        out_specs=[
            rows(2 * own),
            held(8, own),
            held(8, own),
            pl.BlockSpec((8, 8, own), lambda i, j: (0, 0, 0)),
            pl.BlockSpec((2, own, own), lambda i, j: (0, 0, 0)),
        ],
        out_shape=[
            jax.ShapeDtypeStruct((2 * run, 2 * own), BF),
            jax.ShapeDtypeStruct((2, 8, own), F32),
            jax.ShapeDtypeStruct((2, 8, own), F32),
            jax.ShapeDtypeStruct((8, 8, own), F32),
            jax.ShapeDtypeStruct((2, own, own), F32),
        ],
        scratch_shapes=[pltpu.VMEM((3, 8, own), F32)],
        compiler_params=pltpu.CompilerParams(vmem_limit_bytes=40 << 20),
        cost_estimate=pl.CostEstimate(
            flops=16 * run * own * own, bytes_accessed=40 << 20, transcendentals=0
        ),
        name="mix_gates",
    )(ta, tb, from_right, pa, pb, pa, pb, state_in, conv_in, conv_out, branch_grad, chan, gate_r, gate_i, fac)


def settle_kernel(lines, straight, up_all, in_all, down_all, chan, up_out, in_out, down_out, out_out):
    share = up_all.shape[-1] // (2 * lines)
    own = in_all.shape[-1] // 2
    ups = [[up_all[x, k].astype(F32) for k in range(4)] for x in range(2)]
    for part in range(2 * lines):
        at = slice(part * share, (part + 1) * share)
        row = [ups[x][k][:, at] for k in range(4) for x in range(2)]
        up_out[:, part * 8 * share : (part + 1) * 8 * share] = jnp.concatenate(row, axis=1)
    for part in range(2):
        if straight:
            owned = own * 8 // (4 * lines)
            row = [
                in_all[x, k].astype(F32)[:, part * own + i * owned : part * own + (i + 1) * owned]
                for x in range(2)
                for i in range(own // owned)
                for k in range(4)
            ]
        else:
            at = slice(part * own, (part + 1) * own)
            row = [in_all[x, k].astype(F32)[:, at] for x in range(2) for k in range(4)]
        in_out[:, part * 8 * own : (part + 1) * 8 * own] = jnp.concatenate(row, axis=1)
    down_out[...] = down_all[...].astype(F32)
    out_out[...] = chan[:, : out_out.shape[1]].astype(F32)


def settle(up_all, in_all, down_all, chan, owned, width, lines, straight):
    rows, share2 = up_all.shape[2], down_all.shape[0]
    steps = 4 if not (rows % 64 or share2 % 64 or owned % 32) else 1
    r, d, o = rows // steps, share2 // steps, owned // steps
    wide, narrow = up_all.shape[-1], in_all.shape[-1]
    shapes = [(rows, 8 * wide), (rows, 8 * narrow), (share2, width), (owned, width)]
    return pl.pallas_call(
        functools.partial(settle_kernel, lines, straight),
        grid=(steps,),
        in_specs=[
            pl.BlockSpec((2, 4, r, wide), lambda i: (0, 0, i, 0)),
            pl.BlockSpec((2, 4, r, narrow), lambda i: (0, 0, i, 0)),
            pl.BlockSpec((d, width), lambda i: (i, 0)),
            pl.BlockSpec((o, chan.shape[1]), lambda i: (i, 0)),
        ],
        out_specs=[
            pl.BlockSpec((n // steps, w), lambda i: (i, 0)) for n, w in shapes
        ],
        out_shape=[jax.ShapeDtypeStruct(one, F32) for one in shapes],
        compiler_params=pltpu.CompilerParams(vmem_limit_bytes=40 << 20),
        cost_estimate=pl.CostEstimate(
            flops=0, bytes_accessed=6 * sum(a * b for a, b in shapes), transcendentals=0
        ),
        name="settle",
    )(up_all, in_all, down_all, chan[:owned])


def act_back_kernel(cot, down, hidden, out):
    part = down.shape[0]
    grad = lax.dot_general(
        cot[...], down[...], (((1,), (1,)), ((), ())), preferred_element_type=F32
    )
    gelu, slope = gelu_parts(hidden[:, :part])
    out[:, :part] = (grad * hidden[:, part:] * slope).astype(BF)
    out[:, part:] = (grad * gelu).astype(BF)


def act_back(cot, down, hidden):
    tokens, width = cot.shape
    part = down.shape[0]
    rows = 256
    return pl.pallas_call(
        act_back_kernel,
        grid=(tokens // rows,),
        in_specs=[
            pl.BlockSpec((rows, width), lambda i: (i, 0)),
            pl.BlockSpec((part, width), lambda i: (0, 0), pipeline_mode=pl.Buffered(1)),
            pl.BlockSpec((rows, 2 * part), lambda i: (i, 0)),
        ],
        out_specs=pl.BlockSpec((rows, 2 * part), lambda i: (i, 0)),
        out_shape=jax.ShapeDtypeStruct((tokens, 2 * part), BF),
        compiler_params=pltpu.CompilerParams(vmem_limit_bytes=40 << 20),
        cost_estimate=pl.CostEstimate(
            flops=2 * tokens * width * part, bytes_accessed=30 << 20, transcendentals=0
        ),
        name="act_back",
    )(cot, down, hidden)


def act_kernel(two, up, hidden, out):
    part = out.shape[1]
    value = jnp.dot(two[...], up[...], preferred_element_type=F32)
    hidden[...] = value
    gelu, _ = gelu_parts(value[:, :part])
    out[...] = (gelu * value[:, part:]).astype(BF)


def act(two, up):
    tokens, width = two.shape
    wide = up.shape[1]
    rows = 256
    return pl.pallas_call(
        act_kernel,
        grid=(tokens // rows,),
        in_specs=[
            pl.BlockSpec((rows, width), lambda i: (i, 0)),
            pl.BlockSpec((width, wide), lambda i: (0, 0), pipeline_mode=pl.Buffered(1)),
        ],
        out_specs=[
            pl.BlockSpec((rows, wide), lambda i: (i, 0)),
            pl.BlockSpec((rows, wide // 2), lambda i: (i, 0)),
        ],
        out_shape=[
            jax.ShapeDtypeStruct((tokens, wide), F32),
            jax.ShapeDtypeStruct((tokens, wide // 2), BF),
        ],
        compiler_params=pltpu.CompilerParams(vmem_limit_bytes=40 << 20),
        cost_estimate=pl.CostEstimate(
            flops=2 * tokens * width * wide, bytes_accessed=30 << 20, transcendentals=0
        ),
        name="act",
    )(two, up)


def on_device(
    tokens,
    seg_ids,
    mix_gain,
    mix_in,
    conv_par,
    gate_w,
    gate_bias,
    decay,
    out_proj,
    mlp_gain,
    mlp_in,
    mlp_out,
    cotangent,
):
    lines = lax.axis_size("l")
    owners = 4 * lines
    half, line = lax.axis_index("x"), lax.axis_index("l")
    quarter = 2 * lax.axis_index("y") + lax.axis_index("c")
    mine = 4 * half + quarter
    me = 4 * line + quarter
    length, width = tokens.shape
    channels = owners * decay.shape[0]
    block_size = channels // NBLK
    own = channels // 8
    blocks = NBLK // 8
    ff = owners * mlp_out.shape[0]
    run = 4 * length
    plane = 8 * length
    share = mlp_out.shape[0] // 2
    rows = mix_in.shape[0]

    per = owners // 8
    owned = channels // owners
    straight = owned == block_size
    up_sent, mix_sent = pick(mlp_in, mix_in, lines, straight)
    small = jnp.concatenate([conv_par.T, gate_bias.T, decay[:, None], gate_w], axis=1)
    used = small.shape[1]
    small = jnp.pad(small, ((0, 0), (0, -used % 128)))
    tiny = jnp.concatenate([mix_gain.astype(F32), mlp_gain.astype(F32), seg_ids.astype(F32)])
    tiny = jnp.pad(tiny, (0, -tiny.shape[0] % 1024)).reshape(-1, 128)
    tok_all, halo, in_matrix, up_rows, packed, tiny = spread_inputs(
        tokens, mix_sent, up_sent, small, tiny, lines, per, straight
    )
    up_matrix = lax.all_gather(up_rows.reshape(4 * rows, -1), "l", axis=0, tiled=True)
    if straight:
        out_matrix = lax.all_gather(out_proj, "l", axis=0, tiled=True)
        out_matrix = lax.dynamic_slice_in_dim(out_matrix, half * own, own, 0)
    else:
        out_matrix = lax.all_gather(out_proj, SHARD, axis=0, tiled=True)
        out_matrix = lax.dynamic_slice_in_dim(out_matrix, mine * own, own, 0)
    in_matrix = in_matrix.reshape(-1, 2 * own)
    packed = packed.reshape(own, -1)
    tiny = tiny.transpose(0, 3, 2, 1, 4, 5).reshape(2, owners, -1)
    gain_one = tiny[0, :, :rows].reshape(-1)
    gain_two = tiny[0, :, rows : 2 * rows].reshape(-1)
    ids_all = tiny[:, :, 2 * rows : 2 * rows + length].reshape(2, lines, run).astype(jnp.int32)
    decay_own = packed[:, 7].astype(F32)
    chan = packed[:, :8].T.astype(F32)
    chan = chan.at[7].set(-DECAY_RATE * jax.nn.softplus(-decay_own))
    place = lax.broadcasted_iota(jnp.int32, (own, own), 0) // block_size
    place = place == lax.broadcasted_iota(jnp.int32, (own, own), 1) // block_size
    gate_r, gate_i = (
        jnp.where(place, jnp.concatenate([packed[:, at : at + block_size]] * blocks, axis=1), 0)
        for at in (8, 8 + block_size)
    )

    ids = lax.dynamic_index_in_dim(ids_all, line, 1, keepdims=False)
    ids_before = lax.dynamic_index_in_dim(
        ids_all, jnp.maximum(line - 1, 0), 1, keepdims=False
    )[:, -3:]
    extended = jnp.concatenate([ids_before, ids], axis=1)
    places = (line * run + lax.broadcasted_iota(jnp.int32, (2, run), 1)) % SEQ_LEN
    fresh = (extended[:, 3:] != extended[:, 2:-1]) | (places == 0)
    keep = 1.0 - fresh.astype(F32)
    same = jnp.concatenate(
        [(extended[:, 1:3] == extended[:, 0:2]).astype(F32), keep], axis=1
    )
    fac = [keep]
    for offset in range(2, 4):
        fac.append(fac[-1] * same[:, 3 - offset : 3 - offset + run])
    fac = jnp.stack(fac + [keep], axis=-1).reshape(plane, 4)
    all_one, branch, conv_in, conv_out, pa, pb, ends, all_cot = mix_forward(
        tok_all, halo, in_matrix, gain_one, chan, gate_r, gate_i, fac, cotangent
    )
    all_one = all_one.reshape(plane, width)
    all_cot = all_cot.reshape(plane, width)
    ends, out_matrix = lax.optimization_barrier((ends, out_matrix))
    state_in = line_start(ends, lines, False, 5)
    down_rows, state_in = lax.optimization_barrier((mlp_out, state_in))
    down_matrix = lax.all_gather(
        lax.dynamic_slice_in_dim(down_rows, half * share, share, 0), "l", axis=0, tiled=True
    )
    state = pb.reshape(2, run, own) + pa.reshape(2, run, own) * state_in[:, :1]
    mixed = (state * jax.nn.gelu(branch.reshape(2, run, own))).astype(BF).reshape(plane, own)
    residual, all_two = plane_sum(mixed, out_matrix, tokens, None, gain_two, 1)
    hidden, activated = act(all_two, up_matrix)
    down_grad = contract_rows(activated, all_cot).astype(BF)
    down_grad, cot = lax.optimization_barrier((down_grad, all_cot))
    down_line = lax.psum_scatter(down_grad, "l", scatter_dimension=0, tiled=True)
    hidden_grad = act_back(cot, down_matrix, hidden)
    up_grad = contract_rows(all_two, hidden_grad).astype(BF)
    up_grad, hidden_grad = lax.optimization_barrier((up_grad, hidden_grad))
    up_line = lax.psum_scatter(up_grad, "l", scatter_dimension=0, tiled=True)
    residual_grad, gain_two_grad, all_res = plane_sum(
        hidden_grad, up_matrix, residual, cotangent, gain_two, 2
    )
    activated, all_res = lax.optimization_barrier((activated, all_res))
    out_partial = jnp.dot(activated, down_matrix, preferred_element_type=F32).astype(BF)
    out_partial, all_res = lax.optimization_barrier((out_partial, all_res))
    output = (residual + plane_scatter(out_partial).astype(F32)).astype(BF)
    out_grad = contract_rows(mixed, all_res)
    branch_grad, ta, tb, ends = mix_state(
        all_res, out_matrix, branch, pa, pb, state_in, conv_out, chan, gate_r, fac, length
    )
    from_right = line_start(ends, lines, True, 6)
    proj_grad, last_rows, edges, sums, gate_grad = mix_gates(
        ta, tb, from_right, pa, pb, state_in, conv_in, conv_out, branch_grad, chan, gate_r, gate_i, fac, length
    )
    edges = lax.ppermute(edges, "l", [(i + 1, i) for i in range(lines - 1)])
    last_rows = last_rows + jnp.pad(edges[:, :3], ((0, 0), (5, 0), (0, 0)))
    for one in range(2):
        proj_grad = lax.dynamic_update_slice(
            proj_grad, last_rows[one].astype(BF), ((one + 1) * run - 8, own)
        )
    sums = jnp.sum(sums, axis=1)
    sums = sums.at[7].multiply(DECAY_RATE * jax.nn.sigmoid(-decay_own))
    gate_grad = jnp.stack(
        [
            gate_grad[:, b * block_size : (b + 1) * block_size, b * block_size : (b + 1) * block_size]
            for b in range(blocks)
        ]
    )
    gate_grad = gate_grad.transpose(0, 2, 1, 3).reshape(own, 2 * block_size)
    in_grad = contract_rows(all_one, proj_grad).astype(BF)
    chan = jnp.concatenate(
        [out_grad, sums.T, gate_grad], axis=1
    ).astype(BF)
    used = chan.shape[1]
    chan = jnp.pad(
        chan.reshape(own // owned, owned, used), ((0, 0), (0, -owned % 16), (0, -used % 128))
    )
    input_grad, in_all, chan, up_all, down_all, gain_grads = tail(
        proj_grad,
        in_matrix,
        tokens,
        residual_grad,
        gain_one,
        gain_two_grad,
        in_grad,
        chan,
        up_line.reshape(4, rows, -1),
        down_line,
        lines,
        straight,
    )
    up_grad, in_grad, down_grad, out_grad = settle(
        up_all, in_all, down_all.reshape(2 * share, width), chan, owned, width, lines, straight
    )
    small = chan[:owned, width:used].astype(F32)
    gain_grads = lax.dynamic_slice_in_dim(gain_grads[:2], me * rows, rows, 1)
    return (
        output,
        input_grad,
        gain_grads[0],
        in_grad,
        small[:, :5].T,
        small[:, 8:],
        small[:, 5:7].T,
        small[:, 7],
        out_grad,
        gain_grads[1],
        up_grad,
        down_grad,
    )


def solution(mesh):
    count = mesh.shape["shard"]
    fine = Mesh(mesh.devices.reshape(2, count // 4, 2, 2), EVERY)
    rows, cols = P(EVERY, None), P(SHARD, None)
    placed = (
        rows,
        P(EVERY),
        P(SHARD),
        cols,
        P(None, SHARD),
        cols,
        P(None, SHARD),
        P(SHARD),
        cols,
        P(SHARD),
        cols,
        cols,
        rows,
    )
    return jax.shard_map(
        on_device,
        mesh=fine,
        in_specs=placed,
        out_specs=(
            rows,
            rows,
            P(SHARD),
            cols,
            P(None, SHARD),
            cols,
            P(None, SHARD),
            P(SHARD),
            cols,
            P(SHARD),
            cols,
            cols,
        ),
        check_vma=False,
    )
```

```python
import functools

import jax
import jax.numpy as jnp
from jax import lax
from jax.experimental import pallas as pl
from jax.experimental.pallas import tpu as pltpu
from jax.sharding import Mesh, PartitionSpec as P

NBLK = 16
SEQ_LEN = 4096

EPSILON = 1e-06
DECAY_RATE = 8.0
PLANE = ("x", "y", "c")
SHARD = ("l", "y", "c")
EVERY = ("x", "l", "y", "c")
BF = jnp.bfloat16
F32 = jnp.float32


def norm_rows(values, factor):
    return values * lax.rsqrt(jnp.mean(values * values, axis=-1, keepdims=True) + EPSILON) * factor


def contract_rows(left_in, right_in):
    return lax.dot_general(
        left_in, right_in, (((0,), (0,)), ((), ())), preferred_element_type=F32
    )


def times_transposed(left_in, matrix):
    return lax.dot_general(
        left_in, matrix, (((1,), (1,)), ((), ())), preferred_element_type=F32
    )


def gated_product(first_in, second_in):
    return jax.nn.gelu(first_in) * second_in


def plane_gather(block):
    return lax.all_gather(block, PLANE, axis=0, tiled=True)


def plane_scatter(partial):
    return lax.psum_scatter(partial.astype(BF), PLANE, scatter_dimension=0, tiled=True)


MESH = pl.DeviceIdType.MESH


class Wires:
    def __init__(self, send_sems, recv_sems):
        self.send_sems, self.recv_sems, self.used = send_sems, recv_sems, 0

    def far(self, src, dst, device):
        at = self.used
        self.used += 1
        return pltpu.make_async_remote_copy(
            src_ref=src,
            dst_ref=dst,
            send_sem=self.send_sems.at[at],
            recv_sem=self.recv_sems.at[at],
            device_id=device,
            device_id_type=MESH,
        )

    def near(self, src, dst):
        at = self.used
        self.used += 1
        return pltpu.make_async_copy(src, dst, self.send_sems.at[at])


def greet(devices):
    barrier = pltpu.get_barrier_semaphore()
    for device in devices:
        pl.semaphore_signal(barrier, inc=1, device_id=device, device_id_type=MESH)
    pl.semaphore_wait(barrier, len(devices))


def sides():
    x, l, y, c = tuple(lax.axis_index(name) for name in EVERY)
    x_a, y_a = x + (1 - c) * (1 - 2 * x), y + c * (1 - 2 * y)
    x_b, y_b = x + c * (1 - 2 * x), y + (1 - c) * (1 - 2 * y)
    return (x, l, y, c), (x, l, y, 1 - c), (x_a, l, y_a, c), (x_b, l, y_b, c)


def slot_of(device):
    return device[0] * 4 + device[2] * 2 + device[3]


def over_rows(length, rows, step):
    @pl.loop(0, length // rows)
    def _(i):
        step(pl.ds(pl.multiple_of(i * rows, rows), rows))


def block_maker(lhs, rhs, length, transposed):
    def make(slot, target):
        rows = lhs[pl.ds(pl.multiple_of(slot * length, length), length)]
        wide = target.shape[1] // 4
        for part in range(4):
            at = slice(part * wide, (part + 1) * wide)
            if transposed:
                block = lax.dot_general(
                    rows, rhs[at], (((1,), (1,)), ((), ())), preferred_element_type=F32
                )
            else:
                block = jnp.dot(rows, rhs[:, at], preferred_element_type=F32)
            target[:, at] = block.astype(BF)

    return make


class PlaneSum:
    def __init__(self, wires, make, away, own, got, hop_a, hop_b, cuts):
        self.make, self.away = make, away
        self.own, self.got, self.hop_a, self.hop_b = own, got, hop_a, hop_b
        self.cuts, self.part = cuts, own.shape[1] // cuts
        me, core, side_a, side_b = sides()
        diag = (1 - me[0], me[1], 1 - me[2], me[3])
        self.chips = [me, side_a, side_b, diag]
        self.theirs = {0: 0, 1: 2, 2: 1, 3: 3}
        self.order = [3, 1, 2, 0]
        self.swaps = {}
        self.far_a, self.near_a, self.far_b = {}, {}, {}
        for piece in range(cuts):
            rows = pl.ds(piece * self.part, self.part)
            for rel in self.order:
                self.swaps[rel, piece] = wires.far(
                    away.at[rel, rows], got.at[self.theirs[rel], rows], core
                )
            self.far_a[piece] = wires.far(own.at[3, rows], hop_a.at[0, rows], side_a)
            self.near_a[piece] = wires.far(own.at[1, rows], hop_a.at[1, rows], side_a)
            self.far_b[piece] = wires.far(own.at[2, rows], hop_b.at[rows], side_b)

    def make_away(self, rel):
        chip = self.chips[rel]
        self.make(slot_of((chip[0], chip[1], chip[2], 1 - chip[3])), self.away.at[rel])
        for piece in range(self.cuts):
            self.swaps[rel, piece].start()

    def make_home(self, rel):
        self.make(slot_of(self.chips[rel]), self.own.at[rel])

    def landed(self, rel, piece):
        self.swaps[self.theirs[rel], piece].wait_recv()

    def join(self, rel, piece, hopped):
        @pl.loop(0, self.part // 16)
        def _(i):
            rows = pl.ds(pl.multiple_of(piece * self.part + i * 16, 16), 16)
            total = self.own[rel, rows].astype(F32) + self.got[rel, rows].astype(F32)
            if hopped:
                total = total + self.hop_a[0, rows].astype(F32)
            self.own[rel, rows] = total.astype(BF)

    def pass_side(self, rel, copies):
        for piece in range(self.cuts):
            self.landed(rel, piece)
            self.join(rel, piece, False)
            copies[piece].start()

    def first_side(self):
        self.make_away(3)
        self.make_home(3)
        self.make_away(2)
        self.pass_side(3, self.far_a)
        self.make_home(1)
        self.make_away(1)
        self.pass_side(1, self.near_a)
        self.make_home(2)
        self.make_away(0)
        self.make_home(0)

    def second_side(self):
        for piece in range(self.cuts):
            self.landed(2, piece)
            self.far_a[piece].wait_recv()
            self.join(2, piece, True)
            self.far_b[piece].start()

    def finish(self, piece, use):
        self.landed(0, piece)
        self.near_a[piece].wait_recv()
        self.far_b[piece].wait_recv()

        @pl.loop(0, self.part // 16)
        def _(i):
            rows = pl.ds(pl.multiple_of(piece * self.part + i * 16, 16), 16)
            total = self.own[0, rows].astype(F32) + self.got[0, rows].astype(F32)
            total = total + self.hop_a[1, rows].astype(F32) + self.hop_b[rows].astype(F32)
            use(rows, total)

    def drain(self):
        for piece in range(self.cuts):
            for rel in self.order:
                self.swaps[rel, piece].wait_send()
            for copy in (self.far_a[piece], self.near_a[piece], self.far_b[piece]):
                copy.wait_send()


class LineSum:
    def __init__(self, wires, lines, own, from_left, from_right, root):
        x, l, y, c = (lax.axis_index(name) for name in EVERY)
        self.own, self.from_left, self.from_right = own, from_left, from_right
        self.l, self.root, self.lines = l, root, lines
        self.to_right = wires.far(own, from_left, (x, l + 1, y, c))
        self.to_left = wires.far(own, from_right, (x, l - 1, y, c))

    def add(self, other):
        @pl.loop(0, self.own.shape[0] // 16)
        def _(i):
            at = pl.ds(pl.multiple_of(i * 16, 16), 16)
            self.own[at] = (self.own[at].astype(F32) + other[at].astype(F32)).astype(BF)

    def begin(self):
        @pl.when(jnp.logical_and(self.l == 0, self.l < self.root))
        def _():
            self.to_right.start()

        @pl.when(jnp.logical_and(self.l == self.lines - 1, self.l > self.root))
        def _():
            self.to_left.start()

    def through(self):
        @pl.when(jnp.logical_and(self.l > 0, self.l < self.root))
        def _():
            self.to_right.wait_recv()
            self.add(self.from_left)
            self.to_right.start()

        @pl.when(jnp.logical_and(self.l < self.lines - 1, self.l > self.root))
        def _():
            self.to_left.wait_recv()
            self.add(self.from_right)
            self.to_left.start()

    def end(self):
        @pl.when(self.l == self.root)
        def _():
            @pl.when(self.l > 0)
            def _():
                self.to_right.wait_recv()
                self.add(self.from_left)

            @pl.when(self.l < self.lines - 1)
            def _():
                self.to_left.wait_recv()
                self.add(self.from_right)

    def drain(self):
        @pl.when(self.l < self.root)
        def _():
            self.to_right.wait_send()

        @pl.when(self.l > self.root)
        def _():
            self.to_left.wait_send()


def back_rows(base_ref, up_ref, gain_ref, out_ref, gain_out, mine):
    def use(rows, total):
        base = base_ref[rows].astype(F32)
        scale = lax.rsqrt(jnp.mean(base * base, axis=-1, keepdims=True) + EPSILON)
        lean = total * gain_ref[...]
        along = jnp.mean(lean * base, axis=-1, keepdims=True)
        grad = up_ref[rows].astype(F32) + scale * lean
        grad = grad - base * (scale * scale * scale * along)
        out_ref[rows] = grad
        if mine is not None:
            mine[rows] = grad.astype(BF)
        share = total * base * scale
        gain_out[...] += share[:8] + share[8:]

    return use


def forward_rows(base_ref, gain_ref, out_ref, mine):
    def use(rows, total):
        base = base_ref[rows].astype(F32) + total
        out_ref[rows] = base
        scale = lax.rsqrt(jnp.mean(base * base, axis=-1, keepdims=True) + EPSILON)
        mine[rows] = (base * scale * gain_ref[...]).astype(BF)

    return use


class PlaneGather:
    def __init__(self, wires, mine, everything, cuts):
        me, core, side_a, side_b = sides()
        diag = (1 - me[0], me[1], 1 - me[2], me[3])
        here, from_a, from_b, from_diag = [slot_of(at) for at in (me, side_a, side_b, diag)]
        self.cuts, self.copies = cuts, {}
        part = mine.shape[0] // cuts
        for piece in range(cuts):
            rows = pl.ds(piece * part, part)
            for name, src, slot, target in (
                ("a", mine.at[rows], here, side_a),
                ("b", mine.at[rows], here, side_b),
                ("c", mine.at[rows], here, core),
                ("ab", everything.at[from_a, rows], from_a, side_b),
                ("ac", everything.at[from_a, rows], from_a, core),
                ("bc", everything.at[from_b, rows], from_b, core),
                ("dc", everything.at[from_diag, rows], from_diag, core),
            ):
                self.copies[name, piece] = wires.far(src, everything.at[slot, rows], target)
            self.copies["own", piece] = wires.near(mine.at[rows], everything.at[here, rows])

    def start(self, piece):
        for name in ("a", "b", "c", "own"):
            self.copies[name, piece].start()

    def forward(self, came, goes):
        for piece in range(self.cuts):
            self.copies[came, piece].wait_recv()
            for name in goes:
                self.copies[name, piece].start()

    def finish(self):
        for piece in range(self.cuts):
            for name in ("c", "ac", "bc", "dc"):
                self.copies[name, piece].wait_recv()
            self.copies["own", piece].wait()
            for name in ("a", "b", "c", "ab", "ac", "bc", "dc"):
                self.copies[name, piece].wait_send()


def plane_kernel(mode, cuts, *refs):
    refs = list(refs)
    lhs_far, rhs_far, base_far = refs.pop(0), refs.pop(0), refs.pop(0)
    up_far = refs.pop(0) if mode == "back" else None
    side_far = [refs.pop(0), refs.pop(0)] if mode == "back" else []
    gain_ref, out_far = refs.pop(0), refs.pop(0)
    gain_out = refs.pop(0) if mode == "back" else None
    side_out = refs.pop(0) if mode == "back" else None
    all_ref, lhs, rhs, away, own, got, hop_a, hop_b, base_ref, out_ref = refs[:10]
    up_ref, side_lhs, side_rhs, stage = refs[10:14] if mode == "back" else (None,) * 4
    mine, send_sems, recv_sems = refs[-3:]
    _, core, side_a, side_b = sides()
    wires = Wires(send_sems, recv_sems)
    operands = [wires.near(lhs_far, lhs), wires.near(rhs_far, rhs)]
    for copy in operands:
        copy.start()
    greet([core, side_a, side_b])
    make = block_maker(lhs, rhs, out_ref.shape[0], mode == "back")
    total = PlaneSum(wires, make, away, own, got, hop_a, hop_b, cuts)
    spread = PlaneGather(wires, mine, all_ref, cuts)
    loads = [wires.near(base_far, base_ref)]
    if mode == "back":
        loads.append(wires.near(up_far, up_ref))
    length = out_ref.shape[0]
    part = length // cuts
    beside = []
    if mode == "back":
        loads += [wires.near(side_far[0], side_lhs), wires.near(side_far[1], side_rhs)]
        make_side = block_maker(side_lhs, side_rhs, length, False)
        for block in range(8):
            rows = pl.ds(block * length, length)
            beside.append(wires.near(stage.at[block % 2], side_out.at[rows]))

    def work(blocks):
        for block in blocks if mode == "back" else ():
            if block > 1:
                beside[block - 2].wait()
            make_side(block, stage.at[block % 2])
            beside[block].start()

    stores = []
    for piece in range(cuts):
        rows = pl.ds(piece * part, part)
        stores.append(wires.near(out_ref.at[rows], out_far.at[rows]))
    for copy in operands:
        copy.wait()
    for copy in loads:
        copy.start()
    total.first_side()
    for copy in loads:
        copy.wait()
    work(range(3))
    total.second_side()
    work(range(3, 5))
    if mode == "back":
        gain_out[...] = jnp.zeros_like(gain_out)
        use = back_rows(base_ref, up_ref, gain_ref, out_ref, gain_out, mine)
    else:
        use = forward_rows(base_ref, gain_ref, out_ref, mine)
    for piece in range(cuts):
        total.finish(piece, use)
        spread.start(piece)
    for copy in stores:
        copy.start()
    work(range(5, 8))
    spread.forward("a", ("ab", "ac"))
    spread.forward("b", ("bc",))
    spread.forward("ab", ("dc",))
    spread.finish()
    for copy in stores + beside[6:]:
        copy.wait()
    total.drain()


def sum_scratch(lhs, rhs, length, width):
    return [
        pltpu.VMEM(lhs.shape, BF),
        pltpu.VMEM(rhs.shape, BF),
        pltpu.VMEM((4, length, width), BF),
        pltpu.VMEM((4, length, width), BF),
        pltpu.VMEM((4, length, width), BF),
        pltpu.VMEM((2, length, width), BF),
        pltpu.VMEM((length, width), BF),
    ]


def plane_sum(lhs, rhs, base, up, gain, number, side=()):
    mode = "forward" if up is None else "back"
    length, width = base.shape
    cuts = 2
    vmem, left = pl.BlockSpec(memory_space=pltpu.VMEM), pl.BlockSpec(memory_space=pl.ANY)
    args, specs = [lhs, rhs, base], [left, left, left]
    outs, out_specs = [jax.ShapeDtypeStruct((length, width), F32)], [left]
    scratch = [pltpu.VMEM((length, width), base.dtype), pltpu.VMEM((length, width), F32)]
    if mode == "back":
        args += [up, *side]
        specs += [left, left, left]
        outs.append(jax.ShapeDtypeStruct((8, width), F32))
        outs.append(jax.ShapeDtypeStruct((8 * length, width), BF))
        out_specs += [vmem, left]
        scratch.append(pltpu.VMEM((length, width), up.dtype))
        scratch += [pltpu.VMEM(one.shape, BF) for one in side]
        scratch.append(pltpu.VMEM((2, length, width), BF))
    args.append(gain.reshape(1, width))
    specs.append(vmem)
    outs.append(jax.ShapeDtypeStruct((8, length, width), BF))
    out_specs.append(left)
    sems = cuts * (4 + 3 + 8 + 1) + 14
    got = list(
        pl.pallas_call(
            functools.partial(plane_kernel, mode, cuts),
            out_shape=outs,
            in_specs=specs,
            out_specs=out_specs,
            scratch_shapes=sum_scratch(lhs, rhs, length, width)
            + scratch
            + [
                pltpu.VMEM((length, width), BF),
                pltpu.SemaphoreType.DMA((sems,)),
                pltpu.SemaphoreType.DMA((sems,)),
            ],
            compiler_params=pltpu.CompilerParams(
                collective_id=number, has_side_effects=True, vmem_limit_bytes=56 << 20
            ),
            cost_estimate=pl.CostEstimate(
                flops=2 * lhs.size * width, bytes_accessed=400 * base.size, transcendentals=0
            ),
            name=f"plane_{mode}_{number}",
        )(*args)
    )
    got[-1] = got[-1].reshape(8 * length, width)
    return got


def tail_kernel(lines, cuts, straight, *refs):
    (lhs_far, rhs_far, base_far, up_far, gain_ref, other_gain, in_ref, chan_ref, upz) = refs[:9]
    (out_far, in_all, chan_out, up_all, gains) = refs[9:14]
    base_ref, up_ref, out_ref = refs[-3:]
    refs = refs[:-3]
    (lhs, rhs, away, own, got, hop_a, hop_b) = refs[14:21]
    (gain_out, in_own, in_left, in_right) = refs[21:25]
    (chan_own, chan_left, chan_right, chan_got, tiny, tiny_line, send_sems, recv_sems) = refs[25:]
    me, core, side_a, side_b = sides()
    x, l, y, c = me
    k = 2 * y + c
    mates = [core, (x, l, 1 - y, c), (x, l, 1 - y, 1 - c)]
    twin = (1 - x, l, y, c)
    twins = [(1 - x, l, at[2], at[3]) for at in mates]
    wires = Wires(send_sems, recv_sems)
    others = [(x, lax.rem(l + d, lines), y, c) for d in range(1, lines)]
    greet(mates + [twin] + twins + others)

    make = block_maker(lhs, rhs, out_ref.shape[0], True)
    total = PlaneSum(wires, make, away, own, got, hop_a, hop_b, cuts)
    operands = [wires.near(lhs_far, lhs), wires.near(rhs_far, rhs)]
    per = chan_ref.shape[0]
    load_in = wires.near(in_ref, in_own)
    load_chan = wires.near(chan_ref, chan_own)
    in_sums = [
        LineSum(wires, lines, in_own.at[q], in_left.at[q], in_right.at[q], q)
        for q in range(lines)
    ]
    chan_roots = [owner_of(x, k, i, per, straight) // 4 for i in range(per)]
    chan_sums = [
        LineSum(wires, lines, chan_own.at[i], chan_left.at[i], chan_right.at[i], chan_roots[i])
        for i in range(per)
    ]

    def deliver(block, target):
        copies = [wires.near(block(k), target.at[x, k])]
        for at in [twin] + mates + twins:
            copies.append(wires.far(block(2 * at[2] + at[3]), target.at[x, k], at))
        return copies

    loads = [wires.near(base_far, base_ref), wires.near(up_far, up_ref)]
    part = out_ref.shape[0] // cuts
    stores = []
    for piece in range(cuts):
        at = pl.ds(piece * part, part)
        stores.append(wires.near(out_ref.at[at], out_far.at[at]))
    load_in.start()
    for copy in operands:
        copy.start()
    load_chan.start()
    for copy in loads:
        copy.start()
    up_copies = deliver(lambda to: upz.at[to], up_all)
    for copy in up_copies[:5]:
        copy.start()
    load_in.wait()
    load_chan.wait()
    for copy in operands:
        copy.wait()

    def pass_right(q):
        one = in_sums[q]

        @pl.when(jnp.logical_and(l > 0, l < q))
        def _():
            one.to_right.wait_recv()
            one.add(one.from_left)
            one.to_right.start()

    def pass_left(q):
        one = in_sums[q]

        @pl.when(jnp.logical_and(l < lines - 1, l > q))
        def _():
            one.to_left.wait_recv()
            one.add(one.from_right)
            one.to_left.start()

    def send_ends(q):
        @pl.when(jnp.logical_and(l == 0, q > 0))
        def _():
            in_sums[q].to_right.start()

        @pl.when(jnp.logical_and(l == lines - 1, q > 0))
        def _():
            in_sums[lines - 1 - q].to_left.start()

    send_ends(lines - 1)
    total.first_side()
    if lines > 2:
        send_ends(lines - 2)
    pass_right(lines - 1)
    pass_left(0)
    total.second_side()
    for q in reversed(range(1, lines - 2)):
        send_ends(q)
    for copy in up_copies[5:]:
        copy.start()
    for q in reversed(range(1, lines - 1)):
        pass_right(q)
        pass_left(lines - 1 - q)
    for one in chan_sums:
        one.begin()
    gain_out[...] = jnp.zeros_like(gain_out)
    use = back_rows(base_ref, up_ref, gain_ref, out_ref, gain_out, None)
    for copy in loads:
        copy.wait()
    for piece in range(cuts):
        total.finish(piece, use)
        stores[piece].start()
    for one in chan_sums:
        one.through()
    for q in range(lines):
        in_sums[q].end()
    rows = in_all.shape[2]
    in_copies = deliver(
        lambda to: in_own.at[l, pl.ds(pl.multiple_of(to * rows, rows), rows)], in_all
    )
    for copy in in_copies:
        copy.start()
    lane = lax.broadcasted_iota(jnp.int32, tiny.shape[1:], 0)
    first = jnp.sum(gain_out[...], axis=0, keepdims=True)
    second = jnp.sum(other_gain[...], axis=0, keepdims=True)
    tiny[0] = jnp.where(lane == 0, first, jnp.where(lane == 1, second, 0.0))
    for step, at in enumerate((core, twin, (x, l, 1 - y, c))):
        copy = wires.far(tiny.at[2 * step], tiny.at[2 * step + 1], at)
        copy.start()
        copy.wait()
        tiny[2 * step + 2] = tiny[2 * step] + tiny[2 * step + 1]
    line_copies = []
    for d, device in enumerate(others):
        line_copies.append(wires.far(tiny.at[6], tiny_line.at[l], device))
        line_copies[-1].start()
    tiny_line[l] = tiny[6]
    for one in chan_sums:
        one.end()
    goal = 4 * l + k
    for_x, holder, piece = holder_of(goal, per, straight)
    holds = for_x == x
    chan_far, chan_near = [], []
    for i in range(per):
        s = owner_of(x, k, i, per, straight)
        mate = (x, l, lax.rem(s, 4) // 2, lax.rem(s, 2))
        far = wires.far(chan_own.at[i], chan_got, mate)
        near = wires.near(chan_own.at[i], chan_got)
        at_root = chan_roots[i] == l
        away = jnp.logical_and(at_root, lax.rem(s, 4) != k)
        stay = jnp.logical_and(at_root, lax.rem(s, 4) == k)
        chan_far.append((far, away))
        chan_near.append((near, stay))

        @pl.when(away)
        def _():
            far.start()

        @pl.when(stay)
        def _():
            near.start()
            near.wait()

    for i in range(per):
        mine_here = jnp.logical_and(holds, piece == i)

        @pl.when(jnp.logical_and(mine_here, holder != k))
        def _():
            chan_far[i][0].wait_recv()

    to_twin = wires.far(chan_got, chan_out, twin)
    keep = wires.near(chan_got, chan_out)

    @pl.when(holds)
    def _():
        to_twin.start()
        keep.start()
        keep.wait()

    @pl.when(jnp.logical_not(holds))
    def _():
        to_twin.wait_recv()

    for copy in line_copies:
        copy.wait()
    gains[...] = tiny_line[0]
    for q in range(1, lines):
        gains[...] += tiny_line[q]
    for copies in (in_copies, up_copies, stores):
        for copy in copies:
            copy.wait()

    @pl.when(holds)
    def _():
        to_twin.wait_send()

    for far, away in chan_far:

        @pl.when(away)
        def _():
            far.wait_send()

    for one in in_sums + chan_sums:
        one.drain()
    total.drain()


def tail(lhs, rhs, base, up, gain, other_gain, in_grad, chan, upz, lines, straight):
    length, width = base.shape
    cuts = 2
    vmem, left = pl.BlockSpec(memory_space=pltpu.VMEM), pl.BlockSpec(memory_space=pl.ANY)
    rows = in_grad.shape[0] // (4 * lines)
    pieces = in_grad.reshape(lines, 4 * rows, in_grad.shape[1])
    per = chan.shape[0]
    sems = cuts * 8 + 6 + 2 * (lines + per) + 16 + 2 + 8 + 3 + lines + 2 * per + 4
    return pl.pallas_call(
        functools.partial(tail_kernel, lines, cuts, straight),
        out_shape=[
            jax.ShapeDtypeStruct((length, width), F32),
            jax.ShapeDtypeStruct((2, 4, rows, in_grad.shape[1]), BF),
            jax.ShapeDtypeStruct(chan.shape[1:], BF),
            jax.ShapeDtypeStruct((2,) + upz.shape, BF),
            jax.ShapeDtypeStruct((8, width), F32),
        ],
        in_specs=[left, left, left, left, vmem, vmem, left, left, left],
        out_specs=[left, left, left, left, vmem],
        scratch_shapes=sum_scratch(lhs, rhs, length, width)
        + [pltpu.VMEM((8, width), F32)]
        + [pltpu.VMEM(pieces.shape, BF)] * 3
        + [pltpu.VMEM(chan.shape, BF)] * 3
        + [
            pltpu.VMEM(chan.shape[1:], BF),
            pltpu.VMEM((7, 8, width), F32),
            pltpu.VMEM((lines, 8, width), F32),
            pltpu.SemaphoreType.DMA((sems,)),
            pltpu.SemaphoreType.DMA((sems,)),
            pltpu.VMEM((length, width), base.dtype),
            pltpu.VMEM((length, width), F32),
            pltpu.VMEM((length, width), F32),
        ],
        compiler_params=pltpu.CompilerParams(
            collective_id=3, has_side_effects=True, vmem_limit_bytes=56 << 20
        ),
        cost_estimate=pl.CostEstimate(
            flops=20 * base.size, bytes_accessed=400 * base.size, transcendentals=0
        ),
        name="tail",
    )(lhs, rhs, base, up, gain.reshape(1, width), other_gain, pieces, chan, upz)


def owner_of(x, k, i, per, straight):
    return 4 * (x * per + i) + k if straight else (4 * x + k) * per + i


def holder_of(s, per, straight):
    if straight:
        return s // 4 // per, lax.rem(s, 4), lax.rem(s // 4, per)
    return s // (4 * per), lax.rem(s // per, 4), lax.rem(s, per)


class LineGather:
    def __init__(self, wires, lines, blocks):
        x, l, y, c = (lax.axis_index(name) for name in EVERY)
        self.l, self.lines = l, lines
        self.right, self.left = [], []
        for d in range(lines - 1):
            block = blocks.at[jnp.maximum(l - d, 0)]
            self.right.append(wires.far(block, block, (x, l + 1, y, c)))
            block = blocks.at[jnp.minimum(l + d, lines - 1)]
            self.left.append(wires.far(block, block, (x, l - 1, y, c)))

    def step(self, d):
        l, last = self.l, self.lines - 1

        @pl.when(l >= d)
        def _():
            if d > 0:
                self.right[d - 1].wait_recv()
            if d < last:

                @pl.when(l < last)
                def _():
                    self.right[d].start()

        @pl.when(l + d <= last)
        def _():
            if d > 0:
                self.left[d - 1].wait_recv()
            if d < last:

                @pl.when(l > 0)
                def _():
                    self.left[d].start()

    def drain(self):
        l, last = self.l, self.lines - 1
        for d in range(last):

            @pl.when(jnp.logical_and(l >= d, l < last))
            def _():
                self.right[d].wait_send()

            @pl.when(jnp.logical_and(l + d <= last, l > 0))
            def _():
                self.left[d].wait_send()


class FromRoot:
    def __init__(self, wires, lines, source, target, i, per, straight):
        x, l, y, c = (lax.axis_index(name) for name in EVERY)
        k = 2 * y + c
        self.l, self.lines = l, lines
        wanted = owner_of(x, k, i, per, straight)
        self.root = wanted // 4
        for_x, goal, piece = holder_of(4 * l + k, per, straight)
        mine = jnp.logical_and(for_x == x, piece == i)
        self.leaves = jnp.logical_and(mine, goal != k)
        self.stays = jnp.logical_and(mine, goal == k)
        self.comes = jnp.logical_and(self.root == l, lax.rem(wanted, 4) != k)
        self.far = wires.far(source, target.at[i], (x, l, goal // 2, lax.rem(goal, 2)))
        self.near = wires.near(source, target.at[i])
        self.right = wires.far(target.at[i], target.at[i], (x, l + 1, y, c))
        self.left = wires.far(target.at[i], target.at[i], (x, l - 1, y, c))

    def start(self):
        @pl.when(self.leaves)
        def _():
            self.far.start()

        @pl.when(self.stays)
        def _():
            self.near.start()

    def onward(self):
        l, root, last = self.l, self.root, self.lines - 1

        @pl.when(jnp.logical_and(l >= root, l < last))
        def _():
            self.right.start()

        @pl.when(jnp.logical_and(l <= root, l > 0))
        def _():
            self.left.start()

    def from_owner(self):
        @pl.when(self.stays)
        def _():
            self.near.wait()

        @pl.when(self.comes)
        def _():
            self.far.wait_recv()

        @pl.when(self.l == self.root)
        def _():
            self.onward()

    def from_line(self):
        @pl.when(self.l > self.root)
        def _():
            self.right.wait_recv()
            self.onward()

        @pl.when(self.l < self.root)
        def _():
            self.left.wait_recv()
            self.onward()

    def drain(self):
        l, root, last = self.l, self.root, self.lines - 1

        @pl.when(self.leaves)
        def _():
            self.far.wait_send()

        @pl.when(jnp.logical_and(l >= root, l < last))
        def _():
            self.right.wait_send()

        @pl.when(jnp.logical_and(l <= root, l > 0))
        def _():
            self.left.wait_send()


def start_kernel(lines, cuts, straight, *refs):
    (tok, mix, up, small, tiny) = refs[:5]
    (tok_all, halo, mix_all, up_all, small_all, tiny_all) = refs[5:11]
    send_sems, recv_sems = refs[11:]
    me, core, side_a, side_b = sides()
    x, l, y, c = me
    k = 2 * y + c
    other_y, cross, twin = (x, l, 1 - y, c), (x, l, 1 - y, 1 - c), (1 - x, l, y, c)
    mates = [core, other_y, cross]
    others = [(x, lax.rem(l + d, lines), y, c) for d in range(1, lines)]
    per = small_all.shape[0]
    wires = Wires(send_sems, recv_sems)
    greet(mates + [twin] + others)

    def exchange(source, target):
        copies = [wires.near(source.at[k], target.at[k])]
        for at in mates:
            copies.append(wires.far(source.at[2 * at[2] + at[3]], target.at[k], at))
        return copies

    mix_swap = exchange(mix, mix_all.at[l])
    up_swap = exchange(up, up_all)
    spread = PlaneGather(wires, tok, tok_all, cuts)
    walk = LineGather(wires, lines, mix_all)
    roots = [FromRoot(wires, lines, small, small_all, i, per, straight) for i in range(per)]
    tiny_own = wires.near(tiny, tiny_all.at[x, c, y, l])
    tiny_line = [wires.far(tiny, tiny_all.at[x, c, y, l], at) for at in others]
    tiny_steps = [
        wires.far(tiny_all.at[x, c, y], tiny_all.at[x, c, y], other_y),
        wires.far(tiny_all.at[x, c], tiny_all.at[x, c], core),
        wires.far(tiny_all.at[x], tiny_all.at[x], twin),
    ]
    length = tok.shape[0]
    edge = pl.ds(length - 8, 8)
    halo_far = [
        wires.far(tok_all.at[4 * run + 3, edge], halo.at[run], (x, l + 1, y, c))
        for run in range(2)
    ]
    halo_near = [wires.near(tok.at[edge], halo.at[run]) for run in range(2)]

    for copy in mix_swap + [tiny_own] + tiny_line:
        copy.start()
    for one in roots:
        one.start()
    for piece in range(cuts):
        spread.copies["a", piece].start()
    for piece in range(cuts):
        spread.copies["b", piece].start()
    for copy in mix_swap:
        copy.wait()
    walk.step(0)
    for one in roots:
        one.from_owner()
    for piece in range(cuts):
        spread.copies["c", piece].start()
        spread.copies["own", piece].start()
    for copy in [tiny_own] + tiny_line:
        copy.wait()
    for copy in tiny_steps:
        copy.start()
        copy.wait()
    walk.step(1)
    spread.forward("a", ("ab", "ac"))
    for one in roots:
        one.from_line()
    spread.forward("b", ("bc",))
    for copy in up_swap:
        copy.start()
    for d in range(2, lines):
        walk.step(d)
    spread.forward("ab", ("dc",))
    spread.finish()

    @pl.when(l < lines - 1)
    def _():
        for copy in halo_far:
            copy.start()

    @pl.when(l == 0)
    def _():
        for copy in halo_near:
            copy.start()
            copy.wait()

    for copy in up_swap:
        copy.wait()

    @pl.when(l > 0)
    def _():
        for copy in halo_far:
            copy.wait_recv()

    @pl.when(l < lines - 1)
    def _():
        for copy in halo_far:
            copy.wait_send()

    walk.drain()
    for one in roots:
        one.drain()


def spread_inputs(tok, mix, up, small, tiny, lines, per, straight):
    length, width = tok.shape
    cuts = 2
    vmem, left = pl.BlockSpec(memory_space=pltpu.VMEM), pl.BlockSpec(memory_space=pl.ANY)
    sems = 12 + cuts * 8 + 2 * lines + per * 4 + lines + 1 + 3 + 4
    return pl.pallas_call(
        functools.partial(start_kernel, lines, cuts, straight),
        out_shape=[
            jax.ShapeDtypeStruct((8, length, width), BF),
            jax.ShapeDtypeStruct((2, 8, width), BF),
            jax.ShapeDtypeStruct((lines,) + mix.shape, BF),
            jax.ShapeDtypeStruct(up.shape, BF),
            jax.ShapeDtypeStruct((per,) + small.shape, BF),
            jax.ShapeDtypeStruct((2, 2, 2, lines) + tiny.shape, F32),
        ],
        in_specs=[left] * 4 + [vmem],
        out_specs=[left] * 5 + [vmem],
        scratch_shapes=[
            pltpu.SemaphoreType.DMA((sems,)),
            pltpu.SemaphoreType.DMA((sems,)),
        ],
        compiler_params=pltpu.CompilerParams(
            collective_id=4, has_side_effects=True, vmem_limit_bytes=56 << 20
        ),
        cost_estimate=pl.CostEstimate(
            flops=20 * tok.size, bytes_accessed=400 * tok.size, transcendentals=0
        ),
        name="spread",
    )(tok, mix, up, small, tiny)


def pick_kernel(lines, straight, mlp, mix, up, mix_out):
    x = lax.axis_index("x")
    share = up.shape[-1] // (2 * lines)
    own = mix_out.shape[-1] // 2
    for k in range(4):
        parts = []
        for g in range(2 * lines):
            at = (4 * g + k) * 2 * share
            first, second = mlp[:, at : at + share], mlp[:, at + share : at + 2 * share]
            parts.append(jnp.where(x == 0, first, second))
        up[k] = jnp.concatenate(parts, axis=1)
    for k in range(4):
        parts = []
        for side in range(2):
            halves = []
            for half in range(2):
                base = side * 8 * own + half * 4 * own
                if straight:
                    owned = own * 8 // (4 * lines)
                    per = own // owned
                    starts = [(base + (4 * i + k) * owned, owned) for i in range(per)]
                else:
                    starts = [(base + k * own, own)]
                halves.append(
                    jnp.concatenate([mix[:, at : at + wide] for at, wide in starts], axis=1)
                )
            parts.append(jnp.where(x == 0, halves[0], halves[1]))
        mix_out[k] = jnp.concatenate(parts, axis=1)


def pick(mlp_in, mix_in, lines, straight):
    rows, wide = mlp_in.shape
    narrow = mix_in.shape[1]
    steps = 4 if rows % 64 == 0 else 1
    r = rows // steps
    shapes = [wide // 8, narrow // 8]
    return pl.pallas_call(
        functools.partial(pick_kernel, lines, straight),
        grid=(steps,),
        in_specs=[
            pl.BlockSpec((r, wide), lambda i: (i, 0)),
            pl.BlockSpec((r, narrow), lambda i: (i, 0)),
        ],
        out_specs=[pl.BlockSpec((4, r, w), lambda i: (0, i, 0)) for w in shapes],
        out_shape=[jax.ShapeDtypeStruct((4, rows, w), BF) for w in shapes],
        compiler_params=pltpu.CompilerParams(vmem_limit_bytes=40 << 20),
        name="pick",
    )(mlp_in, mix_in)


def gelu_parts(value):
    slope = 0.7978845608028654
    bend = jnp.tanh(slope * (value + 0.044715 * value * value * value))
    gelu = 0.5 * value * (1.0 + bend)
    inner = slope * (1.0 + 0.134145 * value * value)
    return gelu, 0.5 * (1.0 + bend) + 0.5 * value * (1.0 - bend * bend) * inner


def recur_parts(conv_out, chan, gate_ref, keep):
    pre = jnp.dot(conv_out, gate_ref[...], preferred_element_type=F32) + chan[5:6]
    recur = jax.nn.sigmoid(pre)
    log_decay = chan[7:8] * recur
    decayed = jnp.exp(log_decay)
    twice = -2.0 * log_decay
    return recur, decayed, decayed * keep, twice


def below_one(decayed, twice):
    series = 1.0 / 5040.0
    for term in (-1.0 / 720.0, 1.0 / 120.0, -1.0 / 24.0, 1.0 / 6.0, -0.5, 1.0):
        series = series * twice + term
    return jnp.where(twice < 0.5, twice * series, 1.0 - decayed * decayed)


def scan_tiles(rows, backward, first, second, out_first, out_second, carry):
    channels = first.shape[-1]
    where = lax.broadcasted_iota(jnp.int32, (8, channels), 0)
    tiles = rows // 8

    def step(i, state):
        before_a, before_b = state
        tile = tiles - 1 - i if backward else i
        at = pl.ds(pl.multiple_of(tile * 8, 8), 8)
        a, b = first[at], second[at]
        for gap in (1, 2, 4):
            turn = 8 - gap if backward else gap
            inside = where < 8 - gap if backward else where >= gap
            near_a = jnp.where(inside, pltpu.roll(a, turn, 0), 1.0)
            near_b = jnp.where(inside, pltpu.roll(b, turn, 0), 0.0)
            b = b + a * near_b
            a = a * near_a
        b = b + a * before_b
        a = a * before_a
        out_first[at] = a
        out_second[at] = b
        last = 0 if backward else 7
        return (
            jnp.broadcast_to(a[last : last + 1], a.shape),
            jnp.broadcast_to(b[last : last + 1], b.shape),
        )

    end = lax.fori_loop(0, tiles, step, (carry[0], carry[1]), unroll=4)
    carry[0] = end[0]
    carry[1] = end[1]


def mix_forward_kernel(*refs):
    (tok, halo, weight, gain, chan_ref, gate_r, gate_i, fac, cot) = refs[:9]
    (normed, branch, conv_in, conv_out, pa, pb, ends, cot_all) = refs[9:17]
    (rows_in, coef, drive, carry, send_sems, recv_sems) = refs[17:]
    length, own = branch.shape
    chunk = pl.program_id(1)
    chan = chan_ref[...]
    turn = pl.program_id(0) * pl.num_programs(1) + chunk
    last = 2 * pl.num_programs(1) - 1
    _, core, side_a, side_b = sides()
    spread = PlaneGather(Wires(send_sems, recv_sems), cot, cot_all, 2)

    @pl.when(turn == 0)
    def _():
        greet([core, side_a, side_b])
        for piece in range(2):
            spread.start(piece)

    @pl.when(turn == last - 2)
    def _():
        spread.forward("a", ("ab", "ac"))
        spread.forward("b", ("bc",))

    def norm_of(values):
        values = values.astype(F32)
        scale = lax.rsqrt(jnp.mean(values * values, axis=-1, keepdims=True) + EPSILON)
        return (values * scale * gain[...]).astype(BF)

    @pl.when(chunk == 0)
    def _():
        carry[0] = jnp.ones_like(carry[0])
        carry[1] = jnp.zeros_like(carry[1])
        edge = jnp.dot(norm_of(halo[0]), weight[...], preferred_element_type=F32)
        rows_in[8:16] = pltpu.roll(edge, own, 1)[:, :own].astype(BF).astype(F32)
        rows_in[0:8] = jnp.zeros((8, own), F32)
        conv_in[0, 0:16] = rows_in[0:16].astype(BF)

    @pl.when(chunk > 0)
    def _():
        rows_in[0:16] = rows_in[length : length + 16]

    @pl.loop(0, length // 16)
    def _(i):
        at = pl.ds(pl.multiple_of(i * 16, 16), 16)
        normed[0, at] = norm_of(tok[0, at])

    projected = jnp.dot(normed[0], weight[...], preferred_element_type=F32)
    branch[...] = projected[:, :own]
    rounded = pltpu.roll(projected, own, 1)[:, :own].astype(BF)
    conv_in[0, pl.ds(pl.multiple_of(16 + chunk * length, 16), length)] = rounded
    rows_in[16 : 16 + length] = rounded.astype(F32)
    window = rows_in[8 : 16 + length]
    total = chan[4:5] + chan[0:1] * window[8:]
    for gap in range(1, 4):
        total = total + chan[gap : gap + 1] * pltpu.roll(window, gap, 0)[8:] * fac[:, gap - 1 : gap]
    low = total.astype(BF)
    conv_out[...] = low
    keep = fac[:, 0:1]
    _, decayed, coefficient, twice = recur_parts(low, chan, gate_r, keep)
    coef[...] = coefficient
    input_gate = jax.nn.sigmoid(
        jnp.dot(low, gate_i[...], preferred_element_type=F32) + chan[6:7]
    )
    scaling = jnp.where(keep == 0.0, 1.0, jnp.sqrt(below_one(decayed, twice)))
    drive[...] = scaling * input_gate * low.astype(F32)
    scan_tiles(length, False, coef, drive, pa, pb, carry)
    ends[0, 0:8] = carry[0]
    ends[0, 8:16] = carry[1]

    @pl.when(turn == last)
    def _():
        spread.forward("ab", ("dc",))
        spread.finish()


def mix_state_kernel(*refs):
    (res, weight, branch, pa, pb, state_in, conv_out, chan_ref, gate_r, fac, down) = refs[:11]
    (branch_grad, ta, tb, ends, down_all) = refs[11:16]
    (coef, grad, carry, first_coef, send_sems, recv_sems) = refs[16:]
    length, own = branch.shape
    chan = chan_ref[...]
    turn = pl.program_id(1)
    x, l, y, c = (lax.axis_index(name) for name in EVERY)
    twin = (1 - x, l, y, c)
    wires = Wires(send_sems, recv_sems)
    copies = [wires.near(down, down_all.at[x]), wires.far(down, down_all.at[x], twin)]
    step = pl.program_id(0) * pl.num_programs(1) + turn

    @pl.when(step == 0)
    def _():
        greet([twin])
        for copy in copies:
            copy.start()

    @pl.when(turn == 0)
    def _():
        carry[0] = jnp.ones_like(carry[0])
        carry[1] = jnp.zeros_like(carry[1])
        first_coef[...] = jnp.ones_like(first_coef)

    mixed_grad = lax.dot_general(
        res[...], weight[...], (((1,), (1,)), ((), ())), preferred_element_type=F32
    )
    state = pb[...] + pa[...] * state_in[0, 0:1]
    gelu, slope = gelu_parts(branch[...])
    branch_grad[...] = (mixed_grad * state * slope).astype(BF)
    grad[...] = mixed_grad * gelu
    _, _, coefficient, _ = recur_parts(conv_out[...], chan, gate_r, fac[:, 0:1])
    row = lax.broadcasted_iota(jnp.int32, (length, own), 0)
    shifted = pltpu.roll(coefficient, length - 1, 0)
    coef[...] = jnp.where(row == length - 1, first_coef[0:1], shifted)
    first = jnp.broadcast_to(coefficient[0:1], first_coef.shape)
    first_coef[...] = first
    scan_tiles(length, True, coef, grad, ta, tb, carry)
    ends[0, 0:8] = first * carry[0]
    ends[0, 8:16] = first * carry[1]

    @pl.when(step == 2 * pl.num_programs(1) - 1)
    def _():
        for copy in copies:
            copy.wait()


def mix_gates_kernel(*refs):
    (ta, tb, from_right, pa, pb, pa_before, pb_before, state_in) = refs[:8]
    (conv_in, conv_out, branch_grad, chan_ref, gate_r, gate_i, fac) = refs[8:15]
    (proj_grad, last_rows, edges, sums, gate_grad) = refs[15:20]
    (after,) = refs[20:]
    length, own = ta.shape
    turn, turns = pl.program_id(1), pl.num_programs(1)
    chunk = turns - 1 - turn
    chan = chan_ref[...]

    @pl.when(jnp.logical_and(turn == 0, pl.program_id(0) == 0))
    def _():
        sums[...] = jnp.zeros_like(sums)
        gate_grad[...] = jnp.zeros_like(gate_grad)

    @pl.when(turn == 0)
    def _():
        after[...] = jnp.zeros_like(after)

    start = state_in[0, 0:1]
    total = tb[...] + ta[...] * from_right[0, 0:1]
    state = pb[...] + pa[...] * start
    row = lax.broadcasted_iota(jnp.int32, (length, own), 0)
    before = pb_before[7:8] + pa_before[7:8] * start
    before = jnp.where(chunk == 0, start, before)
    prev_state = jnp.where(row == 0, before, pltpu.roll(state, 1, 0))
    keep = fac[:, 0:1]
    low = conv_out[...]
    conv = low.astype(F32)
    recur, decayed, coefficient, twice = recur_parts(low, chan, gate_r, keep)
    input_gate = jax.nn.sigmoid(
        jnp.dot(low, gate_i[...], preferred_element_type=F32) + chan[6:7]
    )
    rest = below_one(decayed, twice)
    fresh = keep == 0.0
    scaling = jnp.where(fresh, 1.0, jnp.sqrt(rest))
    gated = total * input_gate
    by_scaling = jnp.where(fresh, 0.0, gated * conv * decayed * decayed * lax.rsqrt(rest))
    decay_grad = total * prev_state * coefficient - by_scaling
    recur_grad = (chan[7:8] * decay_grad * recur * (1.0 - recur)).astype(BF)
    input_grad = (total * scaling * conv * input_gate * (1.0 - input_gate)).astype(BF)

    def fold(values):
        return jnp.sum(values.reshape(length // 8, 8, own), axis=0)

    sums[5] += fold(recur_grad.astype(F32))
    sums[6] += fold(input_grad.astype(F32))
    sums[7] += fold(decay_grad * recur)
    contract = (((0,), (0,)), ((), ()))
    gate_grad[0] += lax.dot_general(low, recur_grad, contract, preferred_element_type=F32)
    gate_grad[1] += lax.dot_general(low, input_grad, contract, preferred_element_type=F32)
    across = (((1,), (1,)), ((), ()))
    conv_grad = gated * scaling
    conv_grad = conv_grad + lax.dot_general(
        recur_grad, gate_r[...], across, preferred_element_type=F32
    )
    conv_grad = conv_grad + lax.dot_general(
        input_grad, gate_i[...], across, preferred_element_type=F32
    )
    window = conv_in[0, pl.ds(pl.multiple_of(chunk * length, 16), length + 16)].astype(F32)[8:]
    sums[4] += fold(conv_grad)
    sums[0] += fold(conv_grad * window[8:])
    conv_in_grad = chan[0:1] * conv_grad
    edge_row = lax.broadcasted_iota(jnp.int32, (8, own), 0)
    edge = jnp.zeros((8, own), F32)
    for gap in range(1, 4):
        masked = conv_grad * fac[:, gap - 1 : gap]
        sums[gap] += fold(masked * pltpu.roll(window, gap, 0)[8:])
        moved = pltpu.roll(jnp.concatenate([masked, after[gap - 1]], axis=0), length + 8 - gap, 0)
        conv_in_grad = conv_in_grad + chan[gap : gap + 1] * moved[:length]
        head = masked[0:8]
        after[gap - 1] = head
        given = pltpu.roll(head, 3 - gap, 0)
        given = jnp.where((edge_row >= 3 - gap) & (edge_row < 3), given, 0.0)
        edge = edge + chan[gap : gap + 1] * given
    edges[0] = edge

    @pl.when(turn == 0)
    def _():
        last_rows[0] = conv_in_grad[length - 8 :]

    proj_grad[:, :own] = branch_grad[...]
    proj_grad[:, own:] = conv_in_grad.astype(BF)


def line_kernel(lines, backward, ends, start, got, send_sems, recv_sems):
    x, l, y, c = (lax.axis_index(name) for name in EVERY)
    wires = Wires(send_sems, recv_sems)
    others = [(x, lax.rem(l + d, lines), y, c) for d in range(1, lines)]
    greet(others)
    copies = [wires.far(ends, got.at[l], at) for at in others]
    for copy in copies:
        copy.start()
    for copy in copies:
        copy.wait()
    for run in range(2):
        value = jnp.zeros(start.shape[1:], F32)
        order = reversed(range(1, lines)) if backward else range(lines - 1)
        for other in order:
            longer = got[other, run, 0:8] * value + got[other, run, 8:16]
            reached = other > l if backward else other < l
            value = jnp.where(reached, longer, value)
        start[run] = value


def line_start(ends, lines, backward, number):
    vmem = pl.BlockSpec(memory_space=pltpu.VMEM)
    own = ends.shape[-1]
    return pl.pallas_call(
        functools.partial(line_kernel, lines, backward),
        out_shape=jax.ShapeDtypeStruct((2, 8, own), F32),
        in_specs=[vmem],
        out_specs=vmem,
        scratch_shapes=[
            pltpu.VMEM((lines,) + ends.shape, F32),
            pltpu.SemaphoreType.DMA((lines,)),
            pltpu.SemaphoreType.DMA((lines,)),
        ],
        compiler_params=pltpu.CompilerParams(
            collective_id=number, has_side_effects=True, vmem_limit_bytes=8 << 20
        ),
        name=f"line_{number}",
    )(ends)


def mix_specs(run, length, own, backward):
    steps = run // length

    def turn(j):
        return steps - 1 - j if backward else j

    def rows(width):
        return pl.BlockSpec((length, width), lambda i, j: (i * steps + turn(j), 0))

    def slots(width):
        return pl.BlockSpec((1, length, width), lambda i, j: (i * steps + turn(j), 0, 0))

    def whole(*shape):
        return pl.BlockSpec(shape, lambda i, j: (0,) * len(shape), pipeline_mode=pl.Buffered(1))

    def held(*shape):
        return pl.BlockSpec((1,) + shape, lambda i, j: (i,) + (0,) * len(shape))

    return steps, rows, slots, whole, held


def mix_forward(tok_all, halo, weight, gain, chan, gate_r, gate_i, fac, cot):
    slots_in, length, width = tok_all.shape
    own, run = chan.shape[1], 4 * length
    steps, rows, slots, whole, held = mix_specs(run, length, own, False)
    flat = jax.ShapeDtypeStruct((2 * run, own), F32)
    return pl.pallas_call(
        mix_forward_kernel,
        grid=(2, steps),
        in_specs=[
            slots(width),
            held(8, width),
            whole(width, 2 * own),
            whole(1, width),
            whole(8, own),
            whole(own, own),
            whole(own, own),
            rows(fac.shape[1]),
            pl.BlockSpec(memory_space=pl.ANY),
        ],
        out_specs=[
            slots(width),
            rows(own),
            held(16 + run, own),
            rows(own),
            rows(own),
            rows(own),
            held(16, own),
            pl.BlockSpec(memory_space=pl.ANY),
        ],
        out_shape=[
            jax.ShapeDtypeStruct(tok_all.shape, BF),
            flat,
            jax.ShapeDtypeStruct((2, 16 + run, own), BF),
            jax.ShapeDtypeStruct((2 * run, own), BF),
            flat,
            flat,
            jax.ShapeDtypeStruct((2, 16, own), F32),
            jax.ShapeDtypeStruct((8,) + cot.shape, BF),
        ],
        scratch_shapes=[
            pltpu.VMEM((16 + length, own), F32),
            pltpu.VMEM((length, own), F32),
            pltpu.VMEM((length, own), F32),
            pltpu.VMEM((2, 8, own), F32),
            pltpu.SemaphoreType.DMA((16,)),
            pltpu.SemaphoreType.DMA((16,)),
        ],
        compiler_params=pltpu.CompilerParams(
            collective_id=7, has_side_effects=True, vmem_limit_bytes=40 << 20
        ),
        cost_estimate=pl.CostEstimate(
            flops=4 * run * width * 2 * own, bytes_accessed=60 << 20, transcendentals=0
        ),
        name="mix_forward",
    )(tok_all, halo, weight, gain.reshape(1, width), chan, gate_r, gate_i, fac, cot)


def mix_state(res, weight, branch, pa, pb, state_in, conv_out, chan, gate_r, fac, down, length):
    own, width = weight.shape
    run = res.shape[0] // 2
    steps, rows, slots, whole, held = mix_specs(run, length, own, True)
    flat = jax.ShapeDtypeStruct((2 * run, own), F32)
    return pl.pallas_call(
        mix_state_kernel,
        grid=(2, steps),
        in_specs=[
            rows(width),
            whole(own, width),
            rows(own),
            rows(own),
            rows(own),
            held(8, own),
            rows(own),
            whole(8, own),
            whole(own, own),
            rows(fac.shape[1]),
            pl.BlockSpec(memory_space=pl.ANY),
        ],
        out_specs=[
            rows(own),
            rows(own),
            rows(own),
            held(16, own),
            pl.BlockSpec(memory_space=pl.ANY),
        ],
        out_shape=[
            jax.ShapeDtypeStruct((2 * run, own), BF),
            flat,
            flat,
            jax.ShapeDtypeStruct((2, 16, own), F32),
            jax.ShapeDtypeStruct((2,) + down.shape, BF),
        ],
        scratch_shapes=[
            pltpu.VMEM((length, own), F32),
            pltpu.VMEM((length, own), F32),
            pltpu.VMEM((2, 8, own), F32),
            pltpu.VMEM((8, own), F32),
            pltpu.SemaphoreType.DMA((2,)),
            pltpu.SemaphoreType.DMA((2,)),
        ],
        compiler_params=pltpu.CompilerParams(
            collective_id=8, has_side_effects=True, vmem_limit_bytes=40 << 20
        ),
        cost_estimate=pl.CostEstimate(
            flops=4 * run * width * own, bytes_accessed=40 << 20, transcendentals=0
        ),
        name="mix_state",
    )(res, weight, branch, pa, pb, state_in, conv_out, chan, gate_r, fac, down)


def mix_gates(
    ta, tb, from_right, pa, pb, state_in, conv_in, conv_out, branch_grad, chan, gate_r, gate_i, fac, length
):
    own = chan.shape[1]
    run = ta.shape[0] // 2
    steps, rows, slots, whole, held = mix_specs(run, length, own, True)
    eights = length // 8
    earlier = pl.BlockSpec(
        (8, own), lambda i, j: (jnp.maximum((i * steps + steps - 1 - j) * eights - 1, 0), 0)
    )
    return pl.pallas_call(
        mix_gates_kernel,
        grid=(2, steps),
        in_specs=[
            rows(own),
            rows(own),
            held(8, own),
            rows(own),
            rows(own),
            earlier,
            earlier,
            held(8, own),
            held(16 + run, own),
            rows(own),
            rows(own),
            whole(8, own),
            whole(own, own),
            whole(own, own),
            rows(fac.shape[1]),
        ],
        out_specs=[
            rows(2 * own),
            held(8, own),
            held(8, own),
            pl.BlockSpec((8, 8, own), lambda i, j: (0, 0, 0)),
            pl.BlockSpec((2, own, own), lambda i, j: (0, 0, 0)),
        ],
        out_shape=[
            jax.ShapeDtypeStruct((2 * run, 2 * own), BF),
            jax.ShapeDtypeStruct((2, 8, own), F32),
            jax.ShapeDtypeStruct((2, 8, own), F32),
            jax.ShapeDtypeStruct((8, 8, own), F32),
            jax.ShapeDtypeStruct((2, own, own), F32),
        ],
        scratch_shapes=[pltpu.VMEM((3, 8, own), F32)],
        compiler_params=pltpu.CompilerParams(vmem_limit_bytes=40 << 20),
        cost_estimate=pl.CostEstimate(
            flops=16 * run * own * own, bytes_accessed=40 << 20, transcendentals=0
        ),
        name="mix_gates",
    )(ta, tb, from_right, pa, pb, pa, pb, state_in, conv_in, conv_out, branch_grad, chan, gate_r, gate_i, fac)


def settle_kernel(lines, straight, up_all, in_all, down_all, chan, up_out, in_out, down_out, out_out):
    share = up_all.shape[-1] // (2 * lines)
    own = in_all.shape[-1] // 2
    ups = [[up_all[x, k].astype(F32) for k in range(4)] for x in range(2)]
    for part in range(2 * lines):
        at = slice(part * share, (part + 1) * share)
        row = [ups[x][k][:, at] for k in range(4) for x in range(2)]
        up_out[:, part * 8 * share : (part + 1) * 8 * share] = jnp.concatenate(row, axis=1)
    for part in range(2):
        if straight:
            owned = own * 8 // (4 * lines)
            row = [
                in_all[x, k].astype(F32)[:, part * own + i * owned : part * own + (i + 1) * owned]
                for x in range(2)
                for i in range(own // owned)
                for k in range(4)
            ]
        else:
            at = slice(part * own, (part + 1) * own)
            row = [in_all[x, k].astype(F32)[:, at] for x in range(2) for k in range(4)]
        in_out[:, part * 8 * own : (part + 1) * 8 * own] = jnp.concatenate(row, axis=1)
    down_out[...] = down_all[...].astype(F32)
    out_out[...] = chan[:, : out_out.shape[1]].astype(F32)


def settle(up_all, in_all, down_all, chan, owned, width, lines, straight):
    rows, share2 = up_all.shape[2], down_all.shape[0]
    steps = 4 if not (rows % 64 or share2 % 64 or owned % 32) else 1
    r, d, o = rows // steps, share2 // steps, owned // steps
    wide, narrow = up_all.shape[-1], in_all.shape[-1]
    shapes = [(rows, 8 * wide), (rows, 8 * narrow), (share2, width), (owned, width)]
    return pl.pallas_call(
        functools.partial(settle_kernel, lines, straight),
        grid=(steps,),
        in_specs=[
            pl.BlockSpec((2, 4, r, wide), lambda i: (0, 0, i, 0)),
            pl.BlockSpec((2, 4, r, narrow), lambda i: (0, 0, i, 0)),
            pl.BlockSpec((d, width), lambda i: (i, 0)),
            pl.BlockSpec((o, chan.shape[1]), lambda i: (i, 0)),
        ],
        out_specs=[
            pl.BlockSpec((n // steps, w), lambda i: (i, 0)) for n, w in shapes
        ],
        out_shape=[jax.ShapeDtypeStruct(one, F32) for one in shapes],
        compiler_params=pltpu.CompilerParams(vmem_limit_bytes=40 << 20),
        cost_estimate=pl.CostEstimate(
            flops=0, bytes_accessed=6 * sum(a * b for a, b in shapes), transcendentals=0
        ),
        name="settle",
    )(up_all, in_all, down_all, chan[:owned])


def act_back_kernel(cot, down, hidden, out):
    part = down.shape[0]
    grad = lax.dot_general(
        cot[...], down[...], (((1,), (1,)), ((), ())), preferred_element_type=F32
    )
    gelu, slope = gelu_parts(hidden[:, :part])
    out[:, :part] = (grad * hidden[:, part:] * slope).astype(BF)
    out[:, part:] = (grad * gelu).astype(BF)


def act_back(cot, down, hidden):
    tokens, width = cot.shape
    part = down.shape[0]
    rows = 256
    return pl.pallas_call(
        act_back_kernel,
        grid=(tokens // rows,),
        in_specs=[
            pl.BlockSpec((rows, width), lambda i: (i, 0)),
            pl.BlockSpec((part, width), lambda i: (0, 0), pipeline_mode=pl.Buffered(1)),
            pl.BlockSpec((rows, 2 * part), lambda i: (i, 0)),
        ],
        out_specs=pl.BlockSpec((rows, 2 * part), lambda i: (i, 0)),
        out_shape=jax.ShapeDtypeStruct((tokens, 2 * part), BF),
        compiler_params=pltpu.CompilerParams(vmem_limit_bytes=40 << 20),
        cost_estimate=pl.CostEstimate(
            flops=2 * tokens * width * part, bytes_accessed=30 << 20, transcendentals=0
        ),
        name="act_back",
    )(cot, down, hidden)


def act_kernel(two, up, hidden, out):
    part = out.shape[1]
    value = jnp.dot(two[...], up[...], preferred_element_type=F32)
    hidden[...] = value
    gelu, _ = gelu_parts(value[:, :part])
    out[...] = (gelu * value[:, part:]).astype(BF)


def act(two, up):
    tokens, width = two.shape
    wide = up.shape[1]
    rows = 256
    return pl.pallas_call(
        act_kernel,
        grid=(tokens // rows,),
        in_specs=[
            pl.BlockSpec((rows, width), lambda i: (i, 0)),
            pl.BlockSpec((width, wide), lambda i: (0, 0), pipeline_mode=pl.Buffered(1)),
        ],
        out_specs=[
            pl.BlockSpec((rows, wide), lambda i: (i, 0)),
            pl.BlockSpec((rows, wide // 2), lambda i: (i, 0)),
        ],
        out_shape=[
            jax.ShapeDtypeStruct((tokens, wide), F32),
            jax.ShapeDtypeStruct((tokens, wide // 2), BF),
        ],
        compiler_params=pltpu.CompilerParams(vmem_limit_bytes=40 << 20),
        cost_estimate=pl.CostEstimate(
            flops=2 * tokens * width * wide, bytes_accessed=30 << 20, transcendentals=0
        ),
        name="act",
    )(two, up)


def on_device(
    tokens,
    seg_ids,
    mix_gain,
    mix_in,
    conv_par,
    gate_w,
    gate_bias,
    decay,
    out_proj,
    mlp_gain,
    mlp_in,
    mlp_out,
    cotangent,
):
    lines = lax.axis_size("l")
    owners = 4 * lines
    half, line = lax.axis_index("x"), lax.axis_index("l")
    quarter = 2 * lax.axis_index("y") + lax.axis_index("c")
    mine = 4 * half + quarter
    me = 4 * line + quarter
    length, width = tokens.shape
    channels = owners * decay.shape[0]
    block_size = channels // NBLK
    own = channels // 8
    blocks = NBLK // 8
    ff = owners * mlp_out.shape[0]
    run = 4 * length
    plane = 8 * length
    share = mlp_out.shape[0] // 2
    rows = mix_in.shape[0]

    per = owners // 8
    owned = channels // owners
    straight = owned == block_size
    up_sent, mix_sent = pick(mlp_in, mix_in, lines, straight)
    small = jnp.concatenate([conv_par.T, gate_bias.T, decay[:, None], gate_w], axis=1)
    used = small.shape[1]
    small = jnp.pad(small, ((0, 0), (0, -used % 128)))
    tiny = jnp.concatenate([mix_gain.astype(F32), mlp_gain.astype(F32), seg_ids.astype(F32)])
    tiny = jnp.pad(tiny, (0, -tiny.shape[0] % 1024)).reshape(-1, 128)
    tok_all, halo, in_matrix, up_rows, packed, tiny = spread_inputs(
        tokens, mix_sent, up_sent, small, tiny, lines, per, straight
    )
    up_matrix = lax.all_gather(up_rows.reshape(4 * rows, -1), "l", axis=0, tiled=True)
    if straight:
        out_matrix = lax.all_gather(out_proj, "l", axis=0, tiled=True)
        out_matrix = lax.dynamic_slice_in_dim(out_matrix, half * own, own, 0)
    else:
        out_matrix = lax.all_gather(out_proj, SHARD, axis=0, tiled=True)
        out_matrix = lax.dynamic_slice_in_dim(out_matrix, mine * own, own, 0)
    in_matrix = in_matrix.reshape(-1, 2 * own)
    packed = packed.reshape(own, -1)
    tiny = tiny.transpose(0, 3, 2, 1, 4, 5).reshape(2, owners, -1)
    gain_one = tiny[0, :, :rows].reshape(-1)
    gain_two = tiny[0, :, rows : 2 * rows].reshape(-1)
    ids_all = tiny[:, :, 2 * rows : 2 * rows + length].reshape(2, lines, run).astype(jnp.int32)
    decay_own = packed[:, 7].astype(F32)
    chan = packed[:, :8].T.astype(F32)
    chan = chan.at[7].set(-DECAY_RATE * jax.nn.softplus(-decay_own))
    place = lax.broadcasted_iota(jnp.int32, (own, own), 0) // block_size
    place = place == lax.broadcasted_iota(jnp.int32, (own, own), 1) // block_size
    gate_r, gate_i = (
        jnp.where(place, jnp.concatenate([packed[:, at : at + block_size]] * blocks, axis=1), 0)
        for at in (8, 8 + block_size)
    )

    ids = lax.dynamic_index_in_dim(ids_all, line, 1, keepdims=False)
    ids_before = lax.dynamic_index_in_dim(
        ids_all, jnp.maximum(line - 1, 0), 1, keepdims=False
    )[:, -3:]
    extended = jnp.concatenate([ids_before, ids], axis=1)
    places = (line * run + lax.broadcasted_iota(jnp.int32, (2, run), 1)) % SEQ_LEN
    fresh = (extended[:, 3:] != extended[:, 2:-1]) | (places == 0)
    keep = 1.0 - fresh.astype(F32)
    same = jnp.concatenate(
        [(extended[:, 1:3] == extended[:, 0:2]).astype(F32), keep], axis=1
    )
    fac = [keep]
    for offset in range(2, 4):
        fac.append(fac[-1] * same[:, 3 - offset : 3 - offset + run])
    fac = jnp.stack(fac + [keep], axis=-1).reshape(plane, 4)
    all_one, branch, conv_in, conv_out, pa, pb, ends, all_cot = mix_forward(
        tok_all, halo, in_matrix, gain_one, chan, gate_r, gate_i, fac, cotangent
    )
    all_one = all_one.reshape(plane, width)
    all_cot = all_cot.reshape(plane, width)
    ends, out_matrix = lax.optimization_barrier((ends, out_matrix))
    state_in = line_start(ends, lines, False, 5)
    down_rows, state_in = lax.optimization_barrier((mlp_out, state_in))
    down_matrix = lax.all_gather(
        lax.dynamic_slice_in_dim(down_rows, half * share, share, 0), "l", axis=0, tiled=True
    )
    state = pb.reshape(2, run, own) + pa.reshape(2, run, own) * state_in[:, :1]
    mixed = (state * jax.nn.gelu(branch.reshape(2, run, own))).astype(BF).reshape(plane, own)
    residual, all_two = plane_sum(mixed, out_matrix, tokens, None, gain_two, 1)
    hidden, activated = act(all_two, up_matrix)
    down_grad = contract_rows(activated, all_cot).astype(BF)
    down_grad, cot = lax.optimization_barrier((down_grad, all_cot))
    down_line = lax.psum_scatter(down_grad, "l", scatter_dimension=0, tiled=True)
    hidden_grad = act_back(cot, down_matrix, hidden)
    up_grad = contract_rows(all_two, hidden_grad).astype(BF)
    up_grad, hidden_grad = lax.optimization_barrier((up_grad, hidden_grad))
    up_line = lax.psum_scatter(up_grad, "l", scatter_dimension=0, tiled=True)
    residual_grad, gain_two_grad, out_partial, all_res = plane_sum(
        hidden_grad, up_matrix, residual, cotangent, gain_two, 2, (activated, down_matrix)
    )
    output = (residual + plane_scatter(out_partial).astype(F32)).astype(BF)
    out_grad = contract_rows(mixed, all_res)
    branch_grad, ta, tb, ends, down_all = mix_state(
        all_res, out_matrix, branch, pa, pb, state_in, conv_out, chan, gate_r, fac, down_line, length
    )
    from_right = line_start(ends, lines, True, 6)
    proj_grad, last_rows, edges, sums, gate_grad = mix_gates(
        ta, tb, from_right, pa, pb, state_in, conv_in, conv_out, branch_grad, chan, gate_r, gate_i, fac, length
    )
    edges = lax.ppermute(edges, "l", [(i + 1, i) for i in range(lines - 1)])
    last_rows = last_rows + jnp.pad(edges[:, :3], ((0, 0), (5, 0), (0, 0)))
    for one in range(2):
        proj_grad = lax.dynamic_update_slice(
            proj_grad, last_rows[one].astype(BF), ((one + 1) * run - 8, own)
        )
    sums = jnp.sum(sums, axis=1)
    sums = sums.at[7].multiply(DECAY_RATE * jax.nn.sigmoid(-decay_own))
    gate_grad = jnp.stack(
        [
            gate_grad[:, b * block_size : (b + 1) * block_size, b * block_size : (b + 1) * block_size]
            for b in range(blocks)
        ]
    )
    gate_grad = gate_grad.transpose(0, 2, 1, 3).reshape(own, 2 * block_size)
    in_grad = contract_rows(all_one, proj_grad).astype(BF)
    chan = jnp.concatenate(
        [out_grad, sums.T, gate_grad], axis=1
    ).astype(BF)
    used = chan.shape[1]
    chan = jnp.pad(
        chan.reshape(own // owned, owned, used), ((0, 0), (0, -owned % 16), (0, -used % 128))
    )
    input_grad, in_all, chan, up_all, gain_grads = tail(
        proj_grad,
        in_matrix,
        tokens,
        residual_grad,
        gain_one,
        gain_two_grad,
        in_grad,
        chan,
        up_line.reshape(4, rows, -1),
        lines,
        straight,
    )
    up_grad, in_grad, down_grad, out_grad = settle(
        up_all, in_all, down_all.reshape(2 * share, width), chan, owned, width, lines, straight
    )
    small = chan[:owned, width:used].astype(F32)
    gain_grads = lax.dynamic_slice_in_dim(gain_grads[:2], me * rows, rows, 1)
    return (
        output,
        input_grad,
        gain_grads[0],
        in_grad,
        small[:, :5].T,
        small[:, 8:],
        small[:, 5:7].T,
        small[:, 7],
        out_grad,
        gain_grads[1],
        up_grad,
        down_grad,
    )


def solution(mesh):
    count = mesh.shape["shard"]
    fine = Mesh(mesh.devices.reshape(2, count // 4, 2, 2), EVERY)
    rows, cols = P(EVERY, None), P(SHARD, None)
    placed = (
        rows,
        P(EVERY),
        P(SHARD),
        cols,
        P(None, SHARD),
        cols,
        P(None, SHARD),
        P(SHARD),
        cols,
        P(SHARD),
        cols,
        cols,
        rows,
    )
    return jax.shard_map(
        on_device,
        mesh=fine,
        in_specs=placed,
        out_specs=(
            rows,
            rows,
            P(SHARD),
            cols,
            P(None, SHARD),
            cols,
            P(None, SHARD),
            P(SHARD),
            cols,
            P(SHARD),
            cols,
            cols,
        ),
        check_vma=False,
    )
```
